32 devices in a mesh: dp: 8 (over y, x, core), tensor: 4 (over z).
Axes of the slice: x: 2, y: 2, z: 4, core: 2. Of those that a mesh axis runs over, the one named last changes fastest.
Arguments:
- tokens: bfloat16 [16384, 640], P(('dp', 'tensor')), may hold values from -6 to 6
- segments: int32 [16384], P('dp'), may hold values from 0 to 10, as said below
- positions: int32 [16384], P('dp'), may hold values from 0 to 1999, as said below
- norm_gains: bfloat16 [4, 640], P(None, 'dp'), may hold values from 0.099609375 to 1.8984375
- qk_gains: bfloat16 [2, 256], P(None, 'dp'), may hold values from 0.099609375 to 1.8984375
- q_weight: bfloat16 [640, 1024], P('dp', 'tensor'), may hold values from -0.25 to 0.25
- kv_weight: bfloat16 [640, 512], P('dp'), may hold values from -0.25 to 0.25
- out_weight: bfloat16 [1024, 640], P('tensor', 'dp'), may hold values from -0.1875 to 0.1875
- gate_weight: bfloat16 [640, 2048], P('dp', 'tensor'), may hold values from -0.25 to 0.25
- up_weight: bfloat16 [640, 2048], P('dp', 'tensor'), may hold values from -0.25 to 0.25
- down_weight: bfloat16 [2048, 640], P('tensor', 'dp'), may hold values from -0.125 to 0.125
- cotangent: bfloat16 [16384, 640], P(('dp', 'tensor')), may hold values from -6 to 6
Outputs:
- block_out: bfloat16 [16384, 640], P(('dp', 'tensor'))
- tokens_grad: float32 [16384, 640], P(('dp', 'tensor'))
- norm_gains_grad: float32 [4, 640], P(None, 'dp')
- qk_gains_grad: float32 [2, 256], P(None, 'dp')
- q_weight_grad: float32 [640, 1024], P('dp', 'tensor')
- kv_weight_grad: float32 [640, 512], P('dp')
- out_weight_grad: float32 [1024, 640], P('tensor', 'dp')
- gate_weight_grad: float32 [640, 2048], P('dp', 'tensor')
- up_weight_grad: float32 [640, 2048], P('dp', 'tensor')
- down_weight_grad: float32 [2048, 640], P('tensor', 'dp')
The draws below stay inside these ranges and needn't reach their ends.
Inputs may be any that keep to these rules, and one draw needn't show every extreme that they name: `segments`: within each sequence of 2048 tokens the segment numbers start at 0 and rise by one at each new document; every document except the last of its sequence holds between 200 and 2000 tokens. `positions`: each token's place within its document, 0 at the document's first token.
All inputs are finite; a program needn't handle non-finite values.
Results may differ from the reference program's by a relative error of at most 0.018.
Values may be sent and summed in bfloat16 or wider, within the bound.
A program may use at most 128 MiB of HBM per device.

```python
import jax
import jax.numpy as jnp
from jax import lax

D = 640
HEADS = 4
HD = 256
FF = 2048
WINDOW = 512
LEN = 2048
TOKENS = 16384


def doc_layout(key):
    seq_count = TOKENS // LEN
    shortest = LEN * 25 // 256
    longest = LEN * 125 // 128
    lengths = jax.random.randint(jax.random.fold_in(key, 11), (seq_count, 16), shortest, longest + 1, dtype=jnp.int32)
    lengths = lengths.at[0, 0].set(longest)
    lengths = lengths.at[seq_count - 1].set(jnp.full((16,), shortest, jnp.int32))
    ends = jnp.cumsum(lengths, axis=1).astype(jnp.int32)
    places = jnp.arange(LEN, dtype=jnp.int32)
    doc_ids = jnp.sum((ends[:, None, :] <= places[None, :, None]).astype(jnp.int32), axis=2).astype(jnp.int32)
    starts = jnp.concatenate([jnp.zeros((seq_count, 1), jnp.int32), ends[:, :-1]], axis=1)
    inside = places[None, :] - jnp.take_along_axis(starts, doc_ids, axis=1)
    return (doc_ids.reshape(-1).astype(jnp.int32), inside.reshape(-1).astype(jnp.int32))


def draw_segments(key, part):
    return doc_layout(key)[0]


def draw_positions(key, part):
    return doc_layout(key)[1]


def spiked(drawn, stream_key, source, target, parts, factor):
    def block_of(dim):
        return (jnp.arange(drawn.shape[dim]) // (drawn.shape[dim] // parts)).reshape((-1,) + (1,) * (drawn.ndim - 1 - dim))

    first = jax.random.permutation(stream_key, parts)[block_of(target)]
    other_side = (block_of(target) + parts // 2) % parts
    return jnp.where((block_of(source) == first) | (block_of(source) == other_side), factor * drawn, drawn)


def block_scale(rng, shape, pieces, smallest, high):
    loudness = 1.0
    for axis_at, blocks in pieces:
        steps = jax.random.uniform(jax.random.fold_in(jax.random.fold_in(rng, 6), axis_at), (blocks,), jnp.float32, smallest / len(pieces), high / len(pieces))
        loudness = loudness * jnp.repeat(jnp.exp(steps), shape[axis_at] // blocks).reshape((-1,) + (1,) * (len(shape) - 1 - axis_at))
    return loudness


def scatter_about(stream_key, dims, deviation, reach, cuts=(), kind=jnp.bfloat16):
    result = deviation * jax.random.normal(stream_key, dims, jnp.float32)
    if cuts:
        result = result * block_scale(stream_key, dims, cuts, -0.22, 0.18)
    return jnp.clip(result, -reach, reach).astype(kind)


def heavy_noise(rng, shape, scale, bound, pieces, heavy, held_as=jnp.bfloat16):
    values = scale * jax.random.normal(rng, shape, jnp.float32)
    if pieces:
        values = values * block_scale(rng, shape, pieces, -0.22, 0.18)
    return jnp.clip(spiked(values, jax.random.fold_in(rng, 3), *heavy), -bound, bound).astype(held_as)


def setup_inputs(seed: int = 0) -> dict:
    keys = jax.random.split(jax.random.key(seed), 13)
    return {
        "tokens": heavy_noise(keys[0], (TOKENS, D), 1.0, 6.0, ((0, 32),), (0, 1, 32, 2.75)),
        "segments": draw_segments(jax.random.fold_in(keys[12], 71), 0),
        "positions": draw_positions(jax.random.fold_in(keys[12], 71), 0),
        "norm_gains": jnp.clip(1.0 + 0.18 * jax.random.normal(keys[3], (4, D), jnp.float32), 0.099609375, 1.8984375).astype(jnp.bfloat16),
        "qk_gains": jnp.clip(1.0 + 0.18 * jax.random.normal(keys[4], (2, HD), jnp.float32), 0.099609375, 1.8984375).astype(jnp.bfloat16),
        "q_weight": scatter_about(keys[5], (D, HEADS * HD), D ** -0.5, 0.25, ((0, 8), (1, 4))),
        "kv_weight": scatter_about(keys[6], (D, 2 * HD), D ** -0.5, 0.25, ((0, 8),)),
        "out_weight": scatter_about(keys[7], (HEADS * HD, D), (HEADS * HD) ** -0.5, 0.1875, ((0, 4), (1, 8))),
        "gate_weight": scatter_about(keys[8], (D, FF), D ** -0.5, 0.25, ((0, 8), (1, 4))),
        "up_weight": scatter_about(keys[9], (D, FF), D ** -0.5, 0.25, ((0, 8), (1, 4))),
        "down_weight": scatter_about(keys[10], (FF, D), FF ** -0.5, 0.125, ((0, 4), (1, 8))),
        "cotangent": heavy_noise(keys[11], (TOKENS, D), 1.0, 6.0, ((0, 32),), (0, 1, 32, 2.75)),
    }


EPSILON = 1e-06
ROPE_BASE = 10000.0
GELU_SCALE = 0.7978845608028654
HIGHEST = lax.Precision.HIGHEST

@jax.custom_vjp
def low(v):
    return lax.optimization_barrier(v.astype(jnp.bfloat16)).astype(jnp.float32)

@jax.custom_vjp
def low_back(v):
    return v

def low_keep(v):
    return (low(v), None)

def low_pass(kept, grad):
    return (grad,)

def back_keep(v):
    return (v, None)

def back_low(kept, grad):
    return (low(grad),)
low.defvjp(low_keep, low_pass)
low_back.defvjp(back_keep, back_low)

def norm_rows(values, gain_row):
    return values * lax.rsqrt(lax.optimization_barrier(jnp.mean(values * values, axis=-1, keepdims=True)) + EPSILON) * gain_row

def rotate(values, cosine_table, sine_table):
    half_width = values.shape[-1] // 2
    first_half = values[..., :half_width]
    second_half = values[..., half_width:]
    return jnp.concatenate([first_half * cosine_table - second_half * sine_table, second_half * cosine_table + first_half * sine_table], axis=-1)

def geglu(gate_pre, up_pre):
    inner_term = GELU_SCALE * (gate_pre + 0.044715 * gate_pre * gate_pre * gate_pre)
    return 0.5 * gate_pre * (1.0 + jnp.tanh(inner_term)) * up_pre

def product(left_side, right_side):
    return jnp.dot(left_side, right_side, precision=HIGHEST, preferred_element_type=jnp.float32)

def key_blocks(values, window_rows, fill_value):
    padding = jnp.full((window_rows,) + values.shape[1:], fill_value, values.dtype)
    padded = jnp.concatenate([padding, values], axis=0)
    block_count = values.shape[0] // window_rows
    block_shape = (block_count, window_rows) + values.shape[1:]
    return jnp.concatenate([padded[:-window_rows].reshape(block_shape), padded[window_rows:].reshape(block_shape)], axis=1)

def forward(inputs, norm_gains, qk_gains, q_weight, kv_weight, out_weight, gate_weight, up_weight, down_weight, doc_keys, place_rows):
    span = inputs.shape[0]
    head_width = qk_gains.shape[1]
    head_count = q_weight.shape[1] // head_width
    normed = low(norm_rows(inputs, norm_gains[0]))
    query_raw = low_back(product(normed, q_weight)).reshape(span, head_count, head_width)
    kv_raw = product(normed, kv_weight)
    half_width = head_width // 2
    frequency = ROPE_BASE ** (-jnp.arange(half_width, dtype=jnp.float32) * 2.0 / head_width)
    angles = place_rows.astype(jnp.float32)[:, None] * frequency[None, :]
    cosine_table = jnp.cos(angles)
    sine_table = jnp.sin(angles)
    queries = low(rotate(norm_rows(query_raw, qk_gains[0]), cosine_table[:, None, :], sine_table[:, None, :]))
    key_list = []
    value_list = []
    for head in range(head_count):
        kv_copy = low_back(kv_raw)
        key_list.append(low(rotate(norm_rows(kv_copy[:, :head_width], qk_gains[1]), cosine_table, sine_table)))
        value_list.append(low(kv_copy[:, head_width:]))
    key_rows = jnp.stack(key_list, axis=1)
    value_rows = jnp.stack(value_list, axis=1)
    block_count = span // WINDOW
    query_blocks = queries.reshape(block_count, WINDOW, head_count, head_width)
    key_parts = key_blocks(key_rows, WINDOW, 0.0)
    value_parts = key_blocks(value_rows, WINDOW, 0.0)
    query_docs = doc_keys.reshape(block_count, WINDOW)
    key_docs = key_blocks(doc_keys, WINDOW, -1)
    offsets = jnp.arange(WINDOW)[:, None] + WINDOW - jnp.arange(2 * WINDOW)[None, :]
    near_mask = (offsets >= 0) & (offsets < WINDOW)
    score_scale = head_width ** (-0.5)

    def attend(block_item):
        query_part, key_part, value_part, doc_query, doc_key = block_item
        raw_scores = low_back(jnp.einsum('qhd,khd->hqk', query_part, key_part, precision=HIGHEST)) * score_scale
        allowed = near_mask & (doc_query[:, None] == doc_key[None, :])
        masked = jnp.where(allowed[None], raw_scores, -1000000000.0)
        row_max = lax.optimization_barrier(jnp.max(masked, axis=2, keepdims=True))
        exponent = jnp.exp(masked - row_max)
        probabilities = low(exponent / lax.optimization_barrier(jnp.sum(exponent, axis=2, keepdims=True)))
        return jnp.einsum('hqk,khd->qhd', probabilities, value_part, precision=HIGHEST)
    context = lax.map(jax.checkpoint(attend), (query_blocks, key_parts, value_parts, query_docs, key_docs))
    context = low(low_back(context.reshape(span, head_count * head_width)))
    attn = low_back(product(context, out_weight))
    residual = inputs + norm_rows(attn, norm_gains[1])
    ffn_in = low(norm_rows(residual, norm_gains[2]))
    gate_pre = low_back(product(ffn_in, gate_weight))
    up_pre = low_back(product(ffn_in, up_weight))
    hidden = low(geglu(gate_pre, up_pre))
    ffn = low_back(product(hidden, down_weight))
    return residual + norm_rows(ffn, norm_gains[3])

def reference(tokens, segments, positions, norm_gains, qk_gains, q_weight, kv_weight, out_weight, gate_weight, up_weight, down_weight, cotangent):
    weights = (norm_gains.astype(jnp.float32), qk_gains.astype(jnp.float32), q_weight.astype(jnp.float32), kv_weight.astype(jnp.float32), out_weight.astype(jnp.float32), gate_weight.astype(jnp.float32), up_weight.astype(jnp.float32), down_weight.astype(jnp.float32))
    seq_count = tokens.shape[0] // LEN
    width_all = tokens.shape[1]
    input_seqs = tokens.astype(jnp.float32).reshape(seq_count, LEN, width_all)
    grad_seqs = cotangent.astype(jnp.float32).reshape(seq_count, LEN, width_all)
    doc_seqs = segments.reshape(seq_count, LEN)
    place_seqs = positions.reshape(seq_count, LEN)

    def one_sequence(carry, item):
        inputs, grad_out, doc_keys, place_rows = item

        def layer(inputs, *params):
            return forward(inputs, *params, doc_keys, place_rows)
        outputs, backward = jax.vjp(layer, inputs, *weights)
        grads = backward(grad_out)
        carry = tuple((total + piece for total, piece in zip(carry, grads[1:])))
        return (carry, (outputs.astype(jnp.bfloat16), grads[0]))
    start_sums = tuple((jnp.zeros(w.shape, jnp.float32) for w in weights))
    sums, (output_seqs, input_grads) = lax.scan(one_sequence, start_sums, (input_seqs, grad_seqs, doc_seqs, place_seqs))
    block_out = output_seqs.reshape(seq_count * LEN, width_all)
    tokens_grad = input_grads.reshape(seq_count * LEN, width_all)
    return (block_out, tokens_grad, sums[0], sums[1], sums[2], sums[3], sums[4], sums[5], sums[6], sums[7])
```

```python
import functools

import jax
import jax.numpy as jnp
from jax import lax
from jax.experimental import pallas as pl
from jax.experimental.pallas import tpu as pltpu
from jax.sharding import PartitionSpec as P

WINDOW = 512
GAIN_COLUMNS = 128


EPSILON = 1e-06
ROPE_BASE = 10000.0
GELU_SCALE = 0.7978845608028654


def norm_rows(values, gain_row):
    return (
        values * lax.rsqrt(jnp.mean(values * values, axis=-1, keepdims=True) + EPSILON) * gain_row
    )


def norm_back(values, gain_row, grad_out):
    inv_rms = lax.rsqrt(jnp.mean(values * values, axis=-1, keepdims=True) + EPSILON)
    weighted = grad_out * gain_row
    inner_mean = jnp.mean(values * weighted, axis=-1, keepdims=True)
    return (
        inv_rms * weighted - values * inv_rms * inv_rms * inv_rms * inner_mean,
        grad_out * values * inv_rms,
    )


def rotate(values, cosine_table, sine_table):
    half_width = values.shape[-1] // 2
    first_half = values[..., :half_width]
    second_half = values[..., half_width:]
    return jnp.concatenate(
        [
            first_half * cosine_table - second_half * sine_table,
            second_half * cosine_table + first_half * sine_table,
        ],
        axis=-1,
    )


def geglu(gate_pre, up_pre):
    inner_term = GELU_SCALE * (gate_pre + 0.044715 * gate_pre * gate_pre * gate_pre)
    return 0.5 * gate_pre * (1.0 + jnp.tanh(inner_term)) * up_pre


def dot_plain(left_side, right_side):
    return jnp.dot(left_side, right_side, preferred_element_type=jnp.float32)


def dot_last(left_side, right_side):
    return lax.dot_general(
        left_side, right_side, (((1,), (1,)), ((), ())), preferred_element_type=jnp.float32
    )


def dot_first(left_side, right_side):
    return lax.dot_general(
        left_side, right_side, (((0,), (0,)), ((), ())), preferred_element_type=jnp.float32
    )


MESH_ID = pl.DeviceIdType.MESH
PAD_ROWS = 16


class Place:
    def __init__(self):
        self.dp = lax.axis_index("dp")
        self.tensor = lax.axis_index("tensor")
        self.core = lax.rem(self.dp, 2)
        self.chip = self.dp // 2

    def flip_dp(self, bits):
        flipped = self.dp
        for bit in (1, 2, 4):
            if bits & bit:
                flipped = flipped + bit - 2 * bit * lax.rem(self.dp // bit, 2)
        return flipped

    def flip_chip(self, bits):
        return self.flip_dp(2 * bits) // 2

    def flip_tensor(self, bits):
        flipped = self.tensor
        for bit in (1, 2):
            if bits & bit:
                flipped = flipped + bit - 2 * bit * lax.rem(self.tensor // bit, 2)
        return flipped

    def near(self, bits):
        return (self.flip_dp(bits), self.tensor)

    def along(self, bits):
        return (self.dp, self.flip_tensor(bits))

    def greet(self):
        partners = [self.near(1), self.near(2), self.near(4)] + [self.along(k) for k in (1, 2, 3)]
        barrier = pltpu.get_barrier_semaphore()
        for partner in partners:
            pl.semaphore_signal(barrier, inc=1, device_id=partner, device_id_type=MESH_ID)
        pl.semaphore_wait(barrier, len(partners))


class Gather:
    SENDS = 32

    def __init__(self, place, shard, slots, send_sem, recv_sem, local_sem):
        self.place, self.shard, self.slots = place, shard, slots
        self.send_sem, self.recv_sem, self.local_sem = send_sem, recv_sem, local_sem
        self.sent = []

    @staticmethod
    def scratch():
        return [
            pltpu.SemaphoreType.DMA((Gather.SENDS,)),
            pltpu.SemaphoreType.DMA((32,)),
            pltpu.SemaphoreType.DMA,
        ]

    def send(self, source, slot, dp, device, lane):
        copy = pltpu.make_async_remote_copy(
            src_ref=source,
            dst_ref=self.slots.at[slot, dp],
            send_sem=self.send_sem.at[len(self.sent)],
            recv_sem=self.recv_sem.at[slot * 8 + lane],
            device_id=device,
            device_id_type=MESH_ID,
        )
        copy.start()
        self.sent.append(copy)

    def landed(self, slot, bits):
        place = self.place
        dp = place.flip_dp(bits)
        pltpu.make_async_remote_copy(
            src_ref=self.slots.at[slot, dp],
            dst_ref=self.slots.at[slot, dp],
            send_sem=self.send_sem.at[0],
            recv_sem=self.recv_sem.at[slot * 8 + bits],
            device_id=place.near(1),
            device_id_type=MESH_ID,
        ).wait_recv()
        return self.slots.at[slot, dp], dp

    def begin(self):
        place = self.place
        self.local = pltpu.make_async_copy(
            self.shard, self.slots.at[0, place.dp], self.local_sem
        )
        self.local.start()
        for k in (1, 2, 3):
            self.send(self.shard, k, place.dp, place.along(k), 0)
        for bits in (2, 4, 1):
            self.send(self.shard, 0, place.dp, place.near(bits), bits)

    def from_tensor(self, k):
        block, dp = self.landed(k, 0)
        for bits in (2, 4, 1):
            self.send(block, k, dp, self.place.near(bits), bits)

    def from_first(self, k):
        bits, other = (2, 4) if k % 2 == 0 else (4, 2)
        block, dp = self.landed(k, bits)
        self.send(block, k, dp, self.place.near(other), 6)
        self.send(block, k, dp, self.place.near(1), bits + 1)

    def from_second(self, k):
        block, dp = self.landed(k, 4 if k % 2 == 0 else 2)
        self.send(block, k, dp, self.place.near(1), (4 if k % 2 == 0 else 2) + 1)

    def from_corner(self, k):
        block, dp = self.landed(k, 6)
        self.send(block, k, dp, self.place.near(1), 7)

    def events(self):
        order = []
        for k in range(4):
            if k:
                order.append(functools.partial(self.from_tensor, k))
            order.append(functools.partial(self.from_first, k))
            order.append(functools.partial(self.from_second, k))
            if k:
                order.append(functools.partial(self.from_corner, k - 1))
        order.append(functools.partial(self.from_corner, 3))
        return order

    def ready(self, k):
        if k == 0:
            self.local.wait()
        for bits in (1, 3, 5, 7):
            self.landed(k, bits)

    def finish(self):
        for copy in self.sent:
            copy.wait_send()


class Scatter:
    def __init__(self, place, grads, sibling, first, second, last, sems):
        self.place, self.grads, self.sibling = place, grads, sibling
        self.first, self.second, self.last = first, second, last
        self.send_sem, self.recv_sem = sems
        self.sent = []

    @staticmethod
    def scratch(rows, columns):
        block = (rows, columns)
        return [
            pltpu.VMEM((4, 4) + block, jnp.bfloat16),
            pltpu.VMEM((2, 4) + block, jnp.bfloat16),
            pltpu.VMEM((4,) + block, jnp.bfloat16),
            pltpu.VMEM((4,) + block, jnp.bfloat16),
            pltpu.SemaphoreType.DMA((20,)),
            pltpu.SemaphoreType.DMA((20,)),
        ]

    def copy(self, source, target, lane, device):
        return pltpu.make_async_remote_copy(
            src_ref=source,
            dst_ref=target,
            send_sem=self.send_sem.at[lane],
            recv_sem=self.recv_sem.at[lane],
            device_id=device,
            device_id_type=MESH_ID,
        )

    def send(self, *args):
        copy = self.copy(*args)
        copy.start()
        self.sent.append(copy)

    def landed(self, target, lane):
        self.copy(target, target, lane, self.place.near(1)).wait_recv()

    def mine(self, k, chip):
        return self.grads.at[k, chip, self.place.core]

    def to_sibling(self, k):
        self.send(
            self.grads.at[k, :, 1 - self.place.core], self.sibling.at[k], k, self.place.near(1)
        )

    def from_sibling(self, k):
        place = self.place
        self.landed(self.sibling.at[k], k)

        def add(chip, carry):
            block = self.mine(k, chip)
            block[...] = (
                block[...].astype(jnp.float32) + self.sibling[k, chip].astype(jnp.float32)
            ).astype(jnp.bfloat16)
            return carry

        lax.fori_loop(0, 4, add, 0)
        near = 1 if k % 2 == 0 else 2
        for which, bits in ((1, 3), (0, near)):
            self.send(
                self.mine(k, place.flip_chip(bits)),
                self.first.at[which, k],
                4 + 2 * k + which,
                place.near(2 * near),
            )

    def from_first(self, k):
        place = self.place
        far = 2 if k % 2 == 0 else 1
        self.landed(self.first.at[1, k], 4 + 2 * k + 1)
        chip = place.flip_chip(far)
        block = self.mine(k, chip)
        block[...] = (
            block[...].astype(jnp.float32) + self.first[1, k].astype(jnp.float32)
        ).astype(jnp.bfloat16)
        self.send(block, self.second.at[k], 12 + k, place.near(2 * far))

    def from_second(self, k, total=None):
        place = self.place
        self.landed(self.first.at[0, k], 4 + 2 * k)
        self.landed(self.second.at[k], 12 + k)
        block = self.mine(k, place.chip)
        value = (
            block[...].astype(jnp.float32)
            + self.first[0, k].astype(jnp.float32)
            + self.second[k].astype(jnp.float32)
        )
        if k == 0:
            total[...] = value
        else:
            block[...] = value.astype(jnp.bfloat16)
            self.send(block, self.last.at[k], 16 + k, place.along(k))

    def from_tensor(self, total):
        value = total[...]
        for k in (1, 2, 3):
            self.landed(self.last.at[k], 16 + k)
            value = value + self.last[k].astype(jnp.float32)
        total[...] = value

    def finish(self):
        for copy in self.sent:
            copy.wait_send()


def gather_kernel(count, *refs):
    shards, slots, sems = refs[:count], refs[count : 2 * count], refs[2 * count :]
    place = Place()
    place.greet()
    gathers = [
        Gather(place, shards[i], slots[i], *sems[3 * i : 3 * i + 3]) for i in range(count)
    ]
    for gather in gathers:
        gather.begin()
    for gather in gathers:
        for event in gather.events():
            event()
    for gather in gathers:
        for k in range(4):
            gather.ready(k)
    for gather in gathers:
        gather.finish()


def gather_all(shards):
    count = len(shards)
    return pl.pallas_call(
        functools.partial(gather_kernel, count),
        out_shape=[jax.ShapeDtypeStruct((4, 8) + s.shape, s.dtype) for s in shards],
        in_specs=[pl.BlockSpec(memory_space=pltpu.VMEM)] * count,
        out_specs=[pl.BlockSpec(memory_space=pltpu.VMEM)] * count,
        scratch_shapes=Gather.scratch() * count,
        compiler_params=pltpu.CompilerParams(
            collective_id=0, has_side_effects=True, vmem_limit_bytes=60 * 2**20
        ),
    )(*shards)


def scatter_kernel(count, *refs):
    grads, totals, shared = refs[:count], refs[count : 2 * count], refs[2 * count]
    scratch = refs[2 * count + 1 :]
    place = Place()
    place.greet()
    scatters = []
    for i in range(count):
        own = scratch[6 * i : 6 * i + 6]
        scatters.append(Scatter(place, grads[i], *own[:4], own[4:]))
    share_sems = scratch[6 * count :]
    order = (3, 2, 1, 0)
    for scatter in scatters:
        for k in order:
            scatter.to_sibling(k)
    for scatter, total in zip(scatters, totals):
        for step in range(6):
            if step < 4:
                scatter.from_sibling(order[step])
            if 1 <= step < 5:
                scatter.from_first(order[step - 1])
            if step >= 2:
                scatter.from_second(order[step - 2], total)
    for scatter, total in zip(scatters, totals):
        scatter.from_tensor(total)
    final = totals[-1]
    shared[0] = final[...]
    copies = []
    for k in (1, 2, 3):
        copies.append(
            pltpu.make_async_remote_copy(
                src_ref=final,
                dst_ref=shared.at[k],
                send_sem=share_sems[0].at[k],
                recv_sem=share_sems[1].at[k],
                device_id=place.along(k),
                device_id_type=MESH_ID,
            )
        )
    for copy in copies:
        copy.start()
    for copy in copies:
        copy.wait()
    for scatter in scatters:
        scatter.finish()


def scatter_all(grads):
    count = len(grads)
    blocks = [g.shape[3:] for g in grads]
    scratch = []
    for block in blocks:
        scratch += Scatter.scratch(*block)
    scratch += [pltpu.SemaphoreType.DMA((4,)), pltpu.SemaphoreType.DMA((4,))]
    return pl.pallas_call(
        functools.partial(scatter_kernel, count),
        out_shape=[jax.ShapeDtypeStruct(b, jnp.float32) for b in blocks]
        + [jax.ShapeDtypeStruct((4,) + blocks[-1], jnp.float32)],
        in_specs=[pl.BlockSpec(memory_space=pltpu.VMEM)] * count,
        out_specs=[pl.BlockSpec(memory_space=pltpu.VMEM)] * (count + 1),
        scratch_shapes=scratch,
        input_output_aliases={},
        compiler_params=pltpu.CompilerParams(
            collective_id=1, has_side_effects=True, vmem_limit_bytes=62 * 2**20
        ),
    )(*grads)


def pack_shards(norm_gains, qk_gains, q_weight, kv_weight, out_weight, gate_weight, up_weight, down_weight):
    rows = q_weight.shape[0]
    kv_columns = kv_weight.shape[1] // lax.axis_size("tensor")
    kv_part = lax.dynamic_slice_in_dim(
        kv_weight, lax.axis_index("tensor") * kv_columns, kv_columns, axis=1
    )
    gain_part = jnp.concatenate(
        [
            norm_gains.T,
            jnp.pad(qk_gains.T, ((0, rows - qk_gains.shape[1]), (0, 0))),
            jnp.zeros((rows, GAIN_COLUMNS - 6), jnp.bfloat16),
        ],
        axis=1,
    )
    return jnp.concatenate(
        [q_weight, out_weight.T, gate_weight, up_weight, down_weight.T, kv_part, gain_part],
        axis=1,
    )


def gather_weights(packed):
    return lax.all_gather(packed, ("tensor", "dp"), axis=0, tiled=True)


def reduce_grads(grads):
    return lax.psum_scatter(
        grads, ("tensor", "dp"), scatter_dimension=0, tiled=True
    ).astype(jnp.float32)


def per_device(
    tokens,
    segments,
    positions,
    norm_gains,
    qk_gains,
    q_weight,
    kv_weight,
    out_weight,
    gate_weight,
    up_weight,
    down_weight,
    cotangent,
):
    parts = lax.axis_size("tensor")
    place = lax.axis_index("tensor")
    rows, width = tokens.shape
    shard_rows = q_weight.shape[0]
    head_width = q_weight.shape[1]
    ff_part = gate_weight.shape[1]
    kv_columns = kv_weight.shape[1]
    kv_part = kv_columns // parts
    qk_rows = qk_gains.shape[1]
    ends = [0]
    for columns in (head_width, head_width, ff_part, ff_part, ff_part, kv_part, GAIN_COLUMNS):
        ends.append(ends[-1] + columns)

    packed = pack_shards(
        norm_gains, qk_gains, q_weight, kv_weight, out_weight, gate_weight, up_weight, down_weight
    )
    gathered = gather_weights(packed).reshape(parts, width, ends[-1])
    halo = lax.ppermute(tokens, "tensor", [(i, i + 1) for i in range(parts - 1)])

    def piece(index):
        return [gathered[t, :, ends[index] : ends[index + 1]] for t in range(parts)]

    w_query, w_out, w_gate, w_up, w_down, w_kv = (piece(i) for i in range(6))
    w_keyval = jnp.concatenate(w_kv, axis=1)
    w_gains = gathered[0, :, ends[6] : ends[7]].astype(jnp.float32)
    gain_table = w_gains[:, :4].T
    qk_table = w_gains.reshape(-1, shard_rows, GAIN_COLUMNS)[:, :qk_rows, 4:6]
    qk_table = qk_table.reshape(head_width, 2).T

    own_input = tokens.astype(jnp.float32)
    both_input = jnp.concatenate([halo, tokens], axis=0).astype(jnp.float32)
    normed_both = norm_rows(both_input, gain_table[0]).astype(jnp.bfloat16)
    normed = normed_both[rows:]
    start = place * rows
    first = jnp.maximum(start - rows, 0)
    own_doc = lax.dynamic_slice_in_dim(segments, start, rows)
    halo_doc = jnp.where(place > 0, lax.dynamic_slice_in_dim(segments, first, rows), -1)
    both_doc = jnp.concatenate([halo_doc, own_doc])
    both_place = jnp.concatenate(
        [
            lax.dynamic_slice_in_dim(positions, first, rows),
            lax.dynamic_slice_in_dim(positions, start, rows),
        ]
    )
    half_width = head_width // 2
    frequency = ROPE_BASE ** (-jnp.arange(half_width, dtype=jnp.float32) * 2.0 / head_width)
    angles = both_place.astype(jnp.float32)[:, None] * frequency[None, :]
    cosine_both = jnp.cos(angles)
    sine_both = jnp.sin(angles)
    cosine_own, sine_own = cosine_both[rows:], sine_both[rows:]

    offsets = jnp.arange(rows)[:, None] + rows - jnp.arange(2 * rows)[None, :]
    allowed = (offsets >= 0) & (offsets < WINDOW) & (own_doc[:, None] == both_doc[None, :])
    score_scale = head_width ** (-0.5)

    keyval_raw = dot_plain(normed_both, w_keyval)
    key_raw = keyval_raw[:, :head_width]
    keys = rotate(norm_rows(key_raw, qk_table[1]), cosine_both, sine_both).astype(jnp.bfloat16)
    value_rows = keyval_raw[:, head_width:].astype(jnp.bfloat16)

    query_raw, queries, lse, context = [], [], [], []
    attn_own = None
    for t in range(parts):
        raw = dot_plain(normed, w_query[t])
        low = rotate(norm_rows(raw, qk_table[0]), cosine_own, sine_own).astype(jnp.bfloat16)
        masked = jnp.where(allowed, dot_last(low, keys) * score_scale, -1000000000.0)
        row_max = jnp.max(masked, axis=1, keepdims=True)
        exponent = jnp.exp(masked - row_max)
        row_total = jnp.sum(exponent, axis=1, keepdims=True)
        probabilities = (exponent / row_total).astype(jnp.bfloat16)
        mixed = dot_plain(probabilities, value_rows).astype(jnp.bfloat16)
        query_raw.append(raw)
        queries.append(low)
        lse.append(row_max + jnp.log(row_total))
        context.append(mixed)
        share = dot_last(mixed, w_out[t])
        attn_own = share if attn_own is None else attn_own + share

    residual = own_input + norm_rows(attn_own, gain_table[1])
    ffn_in = norm_rows(residual, gain_table[2]).astype(jnp.bfloat16)
    gate_pre, up_pre, hidden = [], [], []
    ffn_out = None
    for t in range(parts):
        gate_pre.append(dot_plain(ffn_in, w_gate[t]))
        up_pre.append(dot_plain(ffn_in, w_up[t]))
        hidden.append(geglu(gate_pre[t], up_pre[t]).astype(jnp.bfloat16))
        share = dot_last(hidden[t], w_down[t])
        ffn_out = share if ffn_out is None else ffn_out + share
    block_out = (residual + norm_rows(ffn_out, gain_table[3])).astype(jnp.bfloat16)
    top_grad = cotangent.astype(jnp.float32)
    ffn_grad_value, post_gain_rows = norm_back(ffn_out, gain_table[3], top_grad)
    ffn_grad = ffn_grad_value.astype(jnp.bfloat16)
    ffn_in_grad = None
    grads = [[] for _ in range(parts)]
    down_wgrad, gate_wgrad, up_wgrad = [], [], []
    for t in range(parts):
        hidden_grad = dot_plain(ffn_grad, w_down[t])
        gelu_back = jax.vjp(geglu, gate_pre[t], up_pre[t])[1]
        gate_grad_value, up_grad_value = gelu_back(hidden_grad)
        gate_grad = gate_grad_value.astype(jnp.bfloat16)
        up_grad = up_grad_value.astype(jnp.bfloat16)
        share = dot_last(gate_grad, w_gate[t]) + dot_last(up_grad, w_up[t])
        ffn_in_grad = share if ffn_in_grad is None else ffn_in_grad + share
        gate_wgrad.append(dot_first(ffn_in, gate_grad))
        up_wgrad.append(dot_first(ffn_in, up_grad))
        down_wgrad.append(dot_first(ffn_grad, hidden[t]))
    residual_part, pre_ffn_rows = norm_back(residual, gain_table[2], ffn_in_grad)
    residual_grad = top_grad + residual_part
    attn_grad_value, post_attn_rows = norm_back(attn_own, gain_table[1], residual_grad)
    attn_grad = attn_grad_value.astype(jnp.bfloat16)

    key_grad, value_grad, normed_grad = None, None, None
    query_gain_grad = None
    out_wgrad, query_wgrad = [], []
    for t in range(parts):
        context_grad = dot_plain(attn_grad, w_out[t]).astype(jnp.bfloat16)
        out_wgrad.append(dot_first(attn_grad, context[t]))
        masked = jnp.where(allowed, dot_last(queries[t], keys) * score_scale, -1000000000.0)
        probabilities = jnp.exp(masked - lse[t])
        prob_grad = dot_last(context_grad, value_rows)
        row_delta = jnp.sum(probabilities * prob_grad, axis=1, keepdims=True)
        score_grad = (probabilities * (prob_grad - row_delta) * score_scale).astype(jnp.bfloat16)
        query_grad = dot_plain(score_grad, keys)
        key_share = dot_first(score_grad, queries[t])
        value_share = dot_first(probabilities.astype(jnp.bfloat16), context_grad)
        key_grad = key_share if key_grad is None else key_grad + key_share
        value_grad = value_share if value_grad is None else value_grad + value_share
        unrotated = rotate(query_grad, cosine_own, -sine_own)
        raw_grad, gain_rows = norm_back(query_raw[t], qk_table[0], unrotated)
        gain_share = jnp.sum(gain_rows, axis=0)
        query_gain_grad = gain_share if query_gain_grad is None else query_gain_grad + gain_share
        raw_low = raw_grad.astype(jnp.bfloat16)
        share = dot_last(raw_low, w_query[t])
        normed_grad = share if normed_grad is None else normed_grad + share
        query_wgrad.append(dot_first(normed, raw_low))
    key_raw_grad, key_gain_rows = norm_back(
        key_raw, qk_table[1], rotate(key_grad, cosine_both, -sine_both)
    )
    keyval_low = jnp.concatenate([key_raw_grad, value_grad], axis=1).astype(jnp.bfloat16)
    next_part = lax.ppermute(
        keyval_low[:rows], "tensor", [(i + 1, i) for i in range(parts - 1)]
    )
    keyval_wgrad = dot_first(normed_both, keyval_low)
    keyval_own = (keyval_low[rows:].astype(jnp.float32) + next_part.astype(jnp.float32)).astype(
        jnp.bfloat16
    )
    normed_grad = normed_grad + dot_last(keyval_own, w_keyval)
    input_part, pre_attn_rows = norm_back(own_input, gain_table[0], normed_grad)
    tokens_grad = residual_grad + input_part

    gain_grads = jnp.stack(
        [
            jnp.sum(pre_attn_rows, axis=0),
            jnp.sum(post_attn_rows, axis=0),
            jnp.sum(pre_ffn_rows, axis=0),
            jnp.sum(post_gain_rows, axis=0),
        ],
        axis=1,
    )
    qk_grads = jnp.stack([query_gain_grad, jnp.sum(key_gain_rows, axis=0)], axis=1)
    qk_grads = jnp.pad(
        qk_grads.reshape(-1, qk_rows, 2), ((0, 0), (0, shard_rows - qk_rows), (0, 0))
    ).reshape(width, 2)
    gain_columns = jnp.concatenate(
        [gain_grads, qk_grads, jnp.zeros((width, GAIN_COLUMNS - 6), jnp.float32)], axis=1
    )
    blocks = []
    for t in range(parts):
        blocks.append(
            jnp.concatenate(
                [
                    value.astype(jnp.bfloat16)
                    for value in (
                        query_wgrad[t],
                        out_wgrad[t],
                        gate_wgrad[t],
                        up_wgrad[t],
                        down_wgrad[t],
                        keyval_wgrad[:, t * kv_part : (t + 1) * kv_part],
                        gain_columns if t == 0 else jnp.zeros_like(gain_columns),
                    )
                ],
                axis=1,
            )
        )
    reduced = reduce_grads(jnp.concatenate(blocks, axis=0))
    shared = lax.all_gather(reduced[:, ends[5] :], "tensor", axis=0)
    keyval_out = jnp.concatenate([shared[t, :, :kv_part] for t in range(parts)], axis=1)
    gain_out = shared[0, :, kv_part:]
    cut = [reduced[:, ends[i] : ends[i + 1]] for i in range(5)]
    return (
        block_out,
        tokens_grad,
        gain_out[:, :4].T,
        gain_out[:qk_rows, 4:6].T,
        cut[0],
        keyval_out,
        cut[1].T,
        cut[2],
        cut[3],
        cut[4].T,
    )


def per_device_direct(
    tokens,
    segments,
    positions,
    norm_gains,
    qk_gains,
    q_weight,
    kv_weight,
    out_weight,
    gate_weight,
    up_weight,
    down_weight,
    cotangent,
):
    parts = lax.axis_size("tensor")
    place = lax.axis_index("tensor")
    rows, width = tokens.shape
    shard_rows = q_weight.shape[0]
    head_width = q_weight.shape[1]
    ff_part = gate_weight.shape[1]
    kv_columns = kv_weight.shape[1]
    kv_part = kv_columns // parts
    qk_rows = qk_gains.shape[1]
    halo = lax.ppermute(tokens, "tensor", [(i, i + 1) for i in range(parts - 1)])
    kv_own = lax.dynamic_slice_in_dim(kv_weight, place * kv_part, kv_part, axis=1)
    gain_rows = jnp.concatenate(
        [
            jnp.pad(norm_gains, ((0, 0), (0, kv_part - norm_gains.shape[1]))),
            jnp.pad(qk_gains, ((0, PAD_ROWS - 6), (0, kv_part - qk_rows))),
        ],
        axis=0,
    )
    slots = gather_all(
        [
            jnp.concatenate([kv_own, gain_rows], axis=0),
            q_weight,
            out_weight.T,
            jnp.concatenate([gate_weight, up_weight, down_weight.T], axis=1),
        ]
    )
    w_query = [slots[1][t].reshape(width, -1) for t in range(parts)]
    w_out = [slots[2][t].reshape(width, -1) for t in range(parts)]
    w_gate, w_up, w_down = (
        [slots[3][t, :, :, i * ff_part : (i + 1) * ff_part].reshape(width, -1) for t in range(parts)]
        for i in range(3)
    )

    def by_part(values):
        return [
            lax.dynamic_index_in_dim(values, place ^ t, 0, keepdims=False) for t in range(parts)
        ]

    w_kv = by_part(slots[0])
    w_keyval = jnp.concatenate(
        [w_kv[t][:, :shard_rows].reshape(width, -1) for t in range(parts)], axis=1
    )
    gain_slots = slots[0][0, :, shard_rows:].astype(jnp.float32)
    gain_table = gain_slots[:, :4, :shard_rows].transpose(1, 0, 2).reshape(4, width)
    qk_table = gain_slots[:, 4:6, :qk_rows].transpose(1, 0, 2).reshape(2, head_width)

    own_input = tokens.astype(jnp.float32)
    both_input = jnp.concatenate([halo, tokens], axis=0).astype(jnp.float32)
    normed_both = norm_rows(both_input, gain_table[0]).astype(jnp.bfloat16)
    normed = normed_both[rows:]
    start = place * rows
    first = jnp.maximum(start - rows, 0)
    own_doc = lax.dynamic_slice_in_dim(segments, start, rows)
    halo_doc = jnp.where(place > 0, lax.dynamic_slice_in_dim(segments, first, rows), -1)
    both_doc = jnp.concatenate([halo_doc, own_doc])
    both_place = jnp.concatenate(
        [
            lax.dynamic_slice_in_dim(positions, first, rows),
            lax.dynamic_slice_in_dim(positions, start, rows),
        ]
    )
    half_width = head_width // 2
    frequency = ROPE_BASE ** (-jnp.arange(half_width, dtype=jnp.float32) * 2.0 / head_width)
    angles = both_place.astype(jnp.float32)[:, None] * frequency[None, :]
    cosine_both = jnp.cos(angles)
    sine_both = jnp.sin(angles)
    cosine_own, sine_own = cosine_both[rows:], sine_both[rows:]

    offsets = jnp.arange(rows)[:, None] + rows - jnp.arange(2 * rows)[None, :]
    allowed = (offsets >= 0) & (offsets < WINDOW) & (own_doc[:, None] == both_doc[None, :])
    score_scale = head_width ** (-0.5)

    keyval_raw = dot_plain(normed_both, w_keyval)
    key_raw = keyval_raw[:, :head_width]
    keys = rotate(norm_rows(key_raw, qk_table[1]), cosine_both, sine_both).astype(jnp.bfloat16)
    value_rows = keyval_raw[:, head_width:].astype(jnp.bfloat16)

    query_raw, queries, lse, context = [], [], [], []
    attn_own = None
    for t in range(parts):
        raw = dot_plain(normed, w_query[t])
        low = rotate(norm_rows(raw, qk_table[0]), cosine_own, sine_own).astype(jnp.bfloat16)
        masked = jnp.where(allowed, dot_last(low, keys) * score_scale, -1000000000.0)
        row_max = jnp.max(masked, axis=1, keepdims=True)
        exponent = jnp.exp(masked - row_max)
        row_total = jnp.sum(exponent, axis=1, keepdims=True)
        probabilities = (exponent / row_total).astype(jnp.bfloat16)
        mixed = dot_plain(probabilities, value_rows).astype(jnp.bfloat16)
        query_raw.append(raw)
        queries.append(low)
        lse.append(row_max + jnp.log(row_total))
        context.append(mixed)
        share = dot_last(mixed, w_out[t])
        attn_own = share if attn_own is None else attn_own + share

    residual = own_input + norm_rows(attn_own, gain_table[1])
    ffn_in = norm_rows(residual, gain_table[2]).astype(jnp.bfloat16)
    gate_pre, up_pre, hidden = [], [], []
    ffn_out = None
    for t in range(parts):
        gate_pre.append(dot_plain(ffn_in, w_gate[t]))
        up_pre.append(dot_plain(ffn_in, w_up[t]))
        hidden.append(geglu(gate_pre[t], up_pre[t]).astype(jnp.bfloat16))
        share = dot_last(hidden[t], w_down[t])
        ffn_out = share if ffn_out is None else ffn_out + share
    block_out = (residual + norm_rows(ffn_out, gain_table[3])).astype(jnp.bfloat16)
    top_grad = cotangent.astype(jnp.float32)
    ffn_grad_value, post_gain_rows = norm_back(ffn_out, gain_table[3], top_grad)
    ffn_grad = ffn_grad_value.astype(jnp.bfloat16)
    ffn_in_grad = None
    grads = [[] for _ in range(parts)]
    down_wgrad, gate_wgrad, up_wgrad = [], [], []
    for t in range(parts):
        hidden_grad = dot_plain(ffn_grad, w_down[t])
        gelu_back = jax.vjp(geglu, gate_pre[t], up_pre[t])[1]
        gate_grad_value, up_grad_value = gelu_back(hidden_grad)
        gate_grad = gate_grad_value.astype(jnp.bfloat16)
        up_grad = up_grad_value.astype(jnp.bfloat16)
        share = dot_last(gate_grad, w_gate[t]) + dot_last(up_grad, w_up[t])
        ffn_in_grad = share if ffn_in_grad is None else ffn_in_grad + share
        gate_wgrad.append(dot_first(ffn_in, gate_grad))
        up_wgrad.append(dot_first(ffn_in, up_grad))
        down_wgrad.append(dot_first(ffn_grad, hidden[t]))
    residual_part, pre_ffn_rows = norm_back(residual, gain_table[2], ffn_in_grad)
    residual_grad = top_grad + residual_part
    attn_grad_value, post_attn_rows = norm_back(attn_own, gain_table[1], residual_grad)
    attn_grad = attn_grad_value.astype(jnp.bfloat16)

    key_grad, value_grad, normed_grad = None, None, None
    query_gain_grad = None
    out_wgrad, query_wgrad = [], []
    for t in range(parts):
        context_grad = dot_plain(attn_grad, w_out[t]).astype(jnp.bfloat16)
        out_wgrad.append(dot_first(attn_grad, context[t]))
        masked = jnp.where(allowed, dot_last(queries[t], keys) * score_scale, -1000000000.0)
        probabilities = jnp.exp(masked - lse[t])
        prob_grad = dot_last(context_grad, value_rows)
        row_delta = jnp.sum(probabilities * prob_grad, axis=1, keepdims=True)
        score_grad = (probabilities * (prob_grad - row_delta) * score_scale).astype(jnp.bfloat16)
        query_grad = dot_plain(score_grad, keys)
        key_share = dot_first(score_grad, queries[t])
        value_share = dot_first(probabilities.astype(jnp.bfloat16), context_grad)
        key_grad = key_share if key_grad is None else key_grad + key_share
        value_grad = value_share if value_grad is None else value_grad + value_share
        unrotated = rotate(query_grad, cosine_own, -sine_own)
        raw_grad, gain_rows = norm_back(query_raw[t], qk_table[0], unrotated)
        gain_share = jnp.sum(gain_rows, axis=0)
        query_gain_grad = gain_share if query_gain_grad is None else query_gain_grad + gain_share
        raw_low = raw_grad.astype(jnp.bfloat16)
        share = dot_last(raw_low, w_query[t])
        normed_grad = share if normed_grad is None else normed_grad + share
        query_wgrad.append(dot_first(normed, raw_low))
    key_raw_grad, key_gain_rows = norm_back(
        key_raw, qk_table[1], rotate(key_grad, cosine_both, -sine_both)
    )
    keyval_low = jnp.concatenate([key_raw_grad, value_grad], axis=1).astype(jnp.bfloat16)
    next_part = lax.ppermute(
        keyval_low[:rows], "tensor", [(i + 1, i) for i in range(parts - 1)]
    )
    keyval_wgrad = dot_first(normed_both, keyval_low)
    keyval_own = (keyval_low[rows:].astype(jnp.float32) + next_part.astype(jnp.float32)).astype(
        jnp.bfloat16
    )
    normed_grad = normed_grad + dot_last(keyval_own, w_keyval)
    input_part, pre_attn_rows = norm_back(own_input, gain_table[0], normed_grad)
    tokens_grad = residual_grad + input_part

    gain_grads = jnp.stack(
        [
            jnp.sum(pre_attn_rows, axis=0),
            jnp.sum(post_attn_rows, axis=0),
            jnp.sum(pre_ffn_rows, axis=0),
            jnp.sum(post_gain_rows, axis=0),
        ]
    )
    qk_grads = jnp.stack([query_gain_grad, jnp.sum(key_gain_rows, axis=0)])
    gain_block = jnp.concatenate(
        [
            jnp.pad(
                gain_grads.reshape(4, -1, shard_rows), ((0, 0), (0, 0), (0, kv_part - shard_rows))
            ),
            jnp.pad(
                qk_grads.reshape(2, -1, qk_rows),
                ((0, PAD_ROWS - 6), (0, 0), (0, kv_part - qk_rows)),
            ),
        ],
        axis=0,
    ).transpose(1, 0, 2)

    def blocks(values):
        return jnp.stack([v.astype(jnp.bfloat16).reshape(4, 2, shard_rows, -1) for v in values])

    kv_blocks = jnp.stack(
        [
            jnp.concatenate(
                [keyval_wgrad[:, t * kv_part : (t + 1) * kv_part].reshape(-1, shard_rows, kv_part), gain_block],
                axis=1,
            )
            for t in range(parts)
        ]
    )
    kv_blocks = jnp.stack(by_part(kv_blocks)).astype(jnp.bfloat16)
    kv_blocks = kv_blocks.reshape(parts, 4, 2, shard_rows + PAD_ROWS, kv_part)
    ffn_sum, attn_sum, kv_sum, shared = scatter_all(
        [
            blocks([jnp.concatenate(v, axis=1) for v in zip(gate_wgrad, up_wgrad, down_wgrad)]),
            blocks([jnp.concatenate(v, axis=1) for v in zip(query_wgrad, out_wgrad)]),
            kv_blocks,
        ]
    )
    keyval_out = jnp.concatenate(by_part(shared[:, :shard_rows]), axis=1)
    gain_out = shared[0, shard_rows:]
    return (
        block_out,
        tokens_grad,
        gain_out[:4, :shard_rows],
        gain_out[4:6, :qk_rows],
        attn_sum[:, :head_width],
        keyval_out,
        attn_sum[:, head_width:].T,
        ffn_sum[:, :ff_part],
        ffn_sum[:, ff_part : 2 * ff_part],
        ffn_sum[:, 2 * ff_part :].T,
    )


def solution(mesh):
    direct = mesh.shape["dp"] == 8 and mesh.shape["tensor"] == 4
    return jax.shard_map(
        per_device_direct if direct else per_device,
        mesh=mesh,
        in_specs=(
            P(("dp", "tensor"), None),
            P("dp"),
            P("dp"),
            P(None, "dp"),
            P(None, "dp"),
            P("dp", "tensor"),
            P("dp", None),
            P("tensor", "dp"),
            P("dp", "tensor"),
            P("dp", "tensor"),
            P("tensor", "dp"),
            P(("dp", "tensor"), None),
        ),
        out_specs=(
            P(("dp", "tensor"), None),
            P(("dp", "tensor"), None),
            P(None, "dp"),
            P(None, "dp"),
            P("dp", "tensor"),
            P("dp", None),
            P("tensor", "dp"),
            P("dp", "tensor"),
            P("dp", "tensor"),
            P("tensor", "dp"),
        ),
        check_vma=False,
    )
```

```python
import functools
import math
import types

import jax
import jax.numpy as jnp
from jax import lax
from jax.experimental import pallas as pl
from jax.experimental.pallas import tpu as pltpu
from jax.sharding import PartitionSpec as P

WINDOW = 512
GAIN_COLUMNS = 128


EPSILON = 1e-06
ROPE_BASE = 10000.0
GELU_SCALE = 0.7978845608028654


def norm_rows(values, gain_row):
    return (
        values * lax.rsqrt(jnp.mean(values * values, axis=-1, keepdims=True) + EPSILON) * gain_row
    )


def norm_back(values, gain_row, grad_out):
    inv_rms = lax.rsqrt(jnp.mean(values * values, axis=-1, keepdims=True) + EPSILON)
    weighted = grad_out * gain_row
    inner_mean = jnp.mean(values * weighted, axis=-1, keepdims=True)
    return (
        inv_rms * weighted - values * inv_rms * inv_rms * inv_rms * inner_mean,
        grad_out * values * inv_rms,
    )


def rotate(values, cosine_table, sine_table):
    half_width = values.shape[-1] // 2
    first_half = values[..., :half_width]
    second_half = values[..., half_width:]
    return jnp.concatenate(
        [
            first_half * cosine_table - second_half * sine_table,
            second_half * cosine_table + first_half * sine_table,
        ],
        axis=-1,
    )


def geglu(gate_pre, up_pre):
    inner_term = GELU_SCALE * (gate_pre + 0.044715 * gate_pre * gate_pre * gate_pre)
    return 0.5 * gate_pre * (1.0 + jnp.tanh(inner_term)) * up_pre


def dot_plain(left_side, right_side):
    return jnp.dot(left_side, right_side, preferred_element_type=jnp.float32)


def dot_last(left_side, right_side):
    return lax.dot_general(
        left_side, right_side, (((1,), (1,)), ((), ())), preferred_element_type=jnp.float32
    )


def dot_first(left_side, right_side):
    return lax.dot_general(
        left_side, right_side, (((0,), (0,)), ((), ())), preferred_element_type=jnp.float32
    )


MESH_ID = pl.DeviceIdType.MESH
PAD_ROWS = 16


class Place:
    def __init__(self):
        self.dp = lax.axis_index("dp")
        self.tensor = lax.axis_index("tensor")
        self.core = lax.rem(self.dp, 2)
        self.chip = self.dp // 2

    def flip_dp(self, bits):
        flipped = self.dp
        for bit in (1, 2, 4):
            if bits & bit:
                flipped = flipped + bit - 2 * bit * lax.rem(self.dp // bit, 2)
        return flipped

    def flip_chip(self, bits):
        return self.flip_dp(2 * bits) // 2

    def flip_tensor(self, bits):
        flipped = self.tensor
        for bit in (1, 2):
            if bits & bit:
                flipped = flipped + bit - 2 * bit * lax.rem(self.tensor // bit, 2)
        return flipped

    def flip_part(self, part):
        return self.flip_tensor(part)

    def near(self, bits):
        return (self.flip_dp(bits), self.tensor)

    def along(self, bits):
        return (self.dp, self.flip_tensor(bits))

    def greet(self):
        partners = [self.near(1), self.near(2), self.near(4)] + [self.along(k) for k in (1, 2, 3)]
        barrier = pltpu.get_barrier_semaphore()
        for partner in partners:
            pl.semaphore_signal(barrier, inc=1, device_id=partner, device_id_type=MESH_ID)
        pl.semaphore_wait(barrier, len(partners))


class Gather:
    SENDS = 32

    def __init__(self, place, shard, slots, send_sem, recv_sem, local_sem):
        self.place, self.shard, self.slots = place, shard, slots
        self.send_sem, self.recv_sem, self.local_sem = send_sem, recv_sem, local_sem
        self.sent = []

    @staticmethod
    def scratch():
        return [
            pltpu.SemaphoreType.DMA((Gather.SENDS,)),
            pltpu.SemaphoreType.DMA((32,)),
            pltpu.SemaphoreType.DMA,
        ]

    def send(self, source, slot, dp, device, lane):
        copy = pltpu.make_async_remote_copy(
            src_ref=source,
            dst_ref=self.slots.at[slot, dp // 2, lax.rem(dp, 2)],
            send_sem=self.send_sem.at[len(self.sent)],
            recv_sem=self.recv_sem.at[slot * 8 + lane],
            device_id=device,
            device_id_type=MESH_ID,
        )
        copy.start()
        self.sent.append(copy)

    def landed(self, slot, bits):
        place = self.place
        dp = place.flip_dp(bits)
        block = self.slots.at[slot, dp // 2, lax.rem(dp, 2)]
        pltpu.make_async_remote_copy(
            src_ref=block,
            dst_ref=block,
            send_sem=self.send_sem.at[0],
            recv_sem=self.recv_sem.at[slot * 8 + bits],
            device_id=place.near(1),
            device_id_type=MESH_ID,
        ).wait_recv()
        return block, dp

    def begin(self):
        place = self.place
        self.local = pltpu.make_async_copy(
            self.shard, self.slots.at[0, place.chip, place.core], self.local_sem
        )
        self.local.start()
        for k in (1, 2, 3):
            self.send(self.shard, k, place.dp, place.along(k), 0)
        for bits in (2, 4, 1):
            self.send(self.shard, 0, place.dp, place.near(bits), bits)

    def from_tensor(self, k):
        block, dp = self.landed(k, 0)
        for bits in (2, 4, 1):
            self.send(block, k, dp, self.place.near(bits), bits)

    def from_first(self, k):
        bits, other = (2, 4) if k % 2 == 0 else (4, 2)
        block, dp = self.landed(k, bits)
        self.send(block, k, dp, self.place.near(other), 6)
        self.send(block, k, dp, self.place.near(1), bits + 1)

    def from_second(self, k):
        block, dp = self.landed(k, 4 if k % 2 == 0 else 2)
        self.send(block, k, dp, self.place.near(1), (4 if k % 2 == 0 else 2) + 1)

    def from_corner(self, k):
        block, dp = self.landed(k, 6)
        self.send(block, k, dp, self.place.near(1), 7)

    def ready(self):
        self.local.wait()
        for k in range(4):
            for bits in (1, 3, 5, 7):
                self.landed(k, bits)

    def finish(self):
        for copy in self.sent:
            copy.wait_send()


def gather_order(gathers):
    count = len(gathers)
    stages = []
    for i in range(count + 2):
        lanes = [[], [], []]
        if i < count:
            lanes[0] = [gathers[i].begin] + [
                functools.partial(gathers[i].from_tensor, k) for k in (1, 2, 3)
            ]
        if 0 <= i - 1 < count:
            lanes[1] = [functools.partial(gathers[i - 1].from_first, k) for k in range(4)]
        if 0 <= i - 2 < count:
            for k in range(4):
                lanes[2].append(functools.partial(gathers[i - 2].from_second, k))
                lanes[2].append(functools.partial(gathers[i - 2].from_corner, k))
        stage = []
        while any(lanes):
            for lane, share in zip(lanes, (1, 1, 2)):
                for _ in range(share):
                    if lane:
                        stage.append(lane.pop(0))
        stages.append(stage)
    return stages


class Scatter:
    def __init__(self, place, grads, sibling, first, second, last, sems):
        self.place, self.grads, self.sibling = place, grads, sibling
        self.first, self.second, self.last = first, second, last
        self.send_sem, self.recv_sem = sems
        self.sent = []

    @staticmethod
    def scratch(rows, columns):
        block = (rows, columns)
        return [
            pltpu.VMEM((4, 4) + block, jnp.bfloat16),
            pltpu.VMEM((2, 4) + block, jnp.bfloat16),
            pltpu.VMEM((4,) + block, jnp.bfloat16),
            pltpu.VMEM((4,) + block, jnp.bfloat16),
            pltpu.SemaphoreType.DMA((20,)),
            pltpu.SemaphoreType.DMA((20,)),
        ]

    def copy(self, source, target, lane, device):
        return pltpu.make_async_remote_copy(
            src_ref=source,
            dst_ref=target,
            send_sem=self.send_sem.at[lane],
            recv_sem=self.recv_sem.at[lane],
            device_id=device,
            device_id_type=MESH_ID,
        )

    def send(self, *args):
        copy = self.copy(*args)
        copy.start()
        self.sent.append(copy)

    def landed(self, target, lane):
        self.copy(target, target, lane, self.place.near(1)).wait_recv()

    def mine(self, k, chip):
        return self.grads.at[k, chip, self.place.core]

    def to_sibling(self, k):
        self.send(
            self.grads.at[k, :, 1 - self.place.core], self.sibling.at[k], k, self.place.near(1)
        )

    def from_sibling(self, k):
        place = self.place
        self.landed(self.sibling.at[k], k)

        def add(chip, carry):
            block = self.mine(k, chip)
            block[...] = (
                block[...].astype(jnp.float32) + self.sibling[k, chip].astype(jnp.float32)
            ).astype(jnp.bfloat16)
            return carry

        lax.fori_loop(0, 4, add, 0)
        near = 1 if k % 2 == 0 else 2
        for which, bits in ((1, 3), (0, near)):
            self.send(
                self.mine(k, place.flip_chip(bits)),
                self.first.at[which, k],
                4 + 2 * k + which,
                place.near(2 * near),
            )

    def from_first(self, k):
        place = self.place
        far = 2 if k % 2 == 0 else 1
        self.landed(self.first.at[1, k], 4 + 2 * k + 1)
        chip = place.flip_chip(far)
        block = self.mine(k, chip)
        block[...] = (
            block[...].astype(jnp.float32) + self.first[1, k].astype(jnp.float32)
        ).astype(jnp.bfloat16)
        self.send(block, self.second.at[k], 12 + k, place.near(2 * far))

    def from_second(self, k, total=None):
        place = self.place
        self.landed(self.first.at[0, k], 4 + 2 * k)
        self.landed(self.second.at[k], 12 + k)
        block = self.mine(k, place.chip)
        value = (
            block[...].astype(jnp.float32)
            + self.first[0, k].astype(jnp.float32)
            + self.second[k].astype(jnp.float32)
        )
        if k == 0:
            total[...] = value
        else:
            block[...] = value.astype(jnp.bfloat16)
            self.send(block, self.last.at[k], 16 + k, place.along(k))

    def from_tensor(self, total):
        value = total[...]
        for k in (1, 2, 3):
            self.landed(self.last.at[k], 16 + k)
            value = value + self.last[k].astype(jnp.float32)
        total[...] = value

    def finish(self):
        for copy in self.sent:
            copy.wait_send()


BLOCK = 128
HALF_WINDOW = 256
VMEM_BYTES = 63 * 2**20
KV, Q, OUT, GATE, UP, DOWN = GROUPS = tuple(range(6))


def nn(left_side, right_side):
    return jnp.dot(left_side, right_side, preferred_element_type=jnp.float32)


def each_block(count, step, body):
    def run(i, carry):
        body(pl.multiple_of(i * step, step))
        return carry

    lax.fori_loop(0, count // step, run, 0)


def inverse_rms(values):
    return lax.rsqrt(jnp.mean(values * values, axis=-1, keepdims=True) + EPSILON)


def transposed(values):
    return values.astype(jnp.float32).T.astype(jnp.bfloat16)


def spread(block_columns, total, index):
    source = lax.broadcasted_iota(jnp.int32, (GAIN_COLUMNS, total), 0)
    target = lax.broadcasted_iota(jnp.int32, (GAIN_COLUMNS, total), 1)
    hit = (target - index * block_columns == source) & (source < block_columns)
    return jnp.where(hit, 1.0, 0.0).astype(jnp.bfloat16)


def layer_scratch(rows, width, head, ff_part, shard, parts):
    bf, f32 = jnp.bfloat16, jnp.float32
    keys = 2 * rows
    window = WINDOW + HALF_WINDOW
    blocks = rows // HALF_WINDOW
    return dict(
        normed=((rows, width), bf),
        normed_t=((width, rows), bf),
        w_keyval=((width, 2 * head), bf),
        gains=((PAD_ROWS, width), f32),
        qk_table=((PAD_ROWS, head), f32),
        gain_sums=((PAD_ROWS, width), f32),
        qk_sums=((PAD_ROWS, head), f32),
        key_raw=((rows, head), f32),
        keyval=((keys, 2 * head), bf),
        keyval_t=((2 * head, keys), bf),
        query_raw=((parts, rows, head), f32),
        queries=((parts, rows, head), bf),
        probs=((parts, blocks, window, HALF_WINDOW), bf),
        score_grad=((window, HALF_WINDOW), bf),
        context=((parts, rows, head), bf),
        attn=((rows, width), f32),
        residual=((rows, width), f32),
        ffn_in=((rows, width), bf),
        ffn_in_t=((width, rows), bf),
        gate_pre=((parts, rows, ff_part), f32),
        up_pre=((rows, ff_part), f32),
        gelu_out=((parts, rows, ff_part), bf),
        gelu_slope=((parts, rows, ff_part), bf),
        hidden=((parts, rows, ff_part), bf),
        ffn=((rows, width), f32),
        ffn_grad=((rows, width), bf),
        ffn_grad_t=((width, rows), bf),
        gate_grad=((rows, ff_part), bf),
        up_grad=((rows, ff_part), bf),
        attn_grad=((rows, width), bf),
        attn_grad_t=((width, rows), bf),
        halo_in=((rows, 2 * head), bf),
        kv_total=((shard + PAD_ROWS, GAIN_COLUMNS), f32),
        kv_shard=((shard + PAD_ROWS, GAIN_COLUMNS), bf),
        cosine=((rows, head // 2), f32),
        sine=((rows, head // 2), f32),
    )


def layer_kernel(names, *refs):
    tokens, cotangent, docs, positions, norm_gains, qk_gains, kv_weight = refs[:7]
    shards = (None,) + refs[7:12]
    block_out, tokens_grad = refs[12:14]
    totals = dict(zip(GROUPS[1:], refs[14:19]))
    shared = refs[19]
    rest = list(refs[20:])
    s = types.SimpleNamespace(**{name: rest.pop(0) for name in names})
    slots = {name: rest.pop(0) for name in GROUPS}
    rows, width = tokens.shape
    head = shards[Q].shape[1]
    ff_part = shards[GATE].shape[1]
    shard = shards[Q].shape[0]
    qk_rows = head // 8
    parts = 4
    blocks = rows // HALF_WINDOW
    window = WINDOW + HALF_WINDOW
    place = Place()

    gathers = {}
    for name, source in zip(GROUPS, (s.kv_shard,) + shards[1:]):
        gathers[name] = Gather(place, source, slots[name], *[rest.pop(0) for _ in range(3)])
    scatters = {}
    for name in GROUPS:
        own = [rest.pop(0) for _ in range(6)]
        scatters[name] = Scatter(place, slots[name], *own[:4], own[4:])
    share_send, share_recv, halo_sems = rest

    def weight(name, k):
        return slots[name][k].reshape(width, -1)

    def put_grad(name, k, value):
        slots[name][k] = value.astype(jnp.bfloat16).reshape(4, 2, shard, -1)

    keyval_grad = s.gate_pre.at[0:2]
    bias, scores = s.gate_pre.at[0:2], s.gate_pre.at[3]

    def tile(j):
        top, left = j % 2 * HALF_WINDOW, j // 2 * HALF_WINDOW
        return slice(top, top + HALF_WINDOW), slice(left, left + HALF_WINDOW)

    query_grads = s.gelu_slope.at[:, :, 0:head]
    context_grad = s.gelu_out.at[:, :, 0:head]
    halo_out, keyval_low = s.hidden.at[0], s.hidden.at[1]

    def keyval_rows(block):
        return block // blocks, slice(
            block % blocks * HALF_WINDOW, (block % blocks + 1) * HALF_WINDOW
        )

    cosine, sine = s.cosine, s.sine
    part_at = pl.multiple_of(place.tensor * GAIN_COLUMNS, GAIN_COLUMNS)
    s.kv_shard[0:shard, :] = kv_weight[:, pl.ds(part_at, GAIN_COLUMNS)]
    s.kv_shard[shard:, :] = jnp.zeros((PAD_ROWS, GAIN_COLUMNS), jnp.bfloat16)
    s.kv_shard[shard : shard + 4, 0:shard] = norm_gains[...]
    s.kv_shard[shard + 4 : shard + 6, 0:qk_rows] = qk_gains[...]
    place.greet()
    gathers[KV].begin()
    gathers[Q].begin()
    queue = gather_order([gathers[name] for name in (KV, Q, GATE, OUT, UP, DOWN)])
    queue[0].pop(0)
    queue[1].pop(0)
    position = [0]

    def through(stage):
        while position[0] <= stage:
            while queue[position[0]]:
                queue[position[0]].pop(0)()
            position[0] += 1

    def pump(count):
        while count and position[0] < len(queue):
            if not queue[position[0]]:
                position[0] += 1
                continue
            queue[position[0]].pop(0)()
            count -= 1

    def as_column(values):
        return jnp.broadcast_to(values.astype(jnp.float32), (GAIN_COLUMNS, values.shape[1])).T

    start = pl.multiple_of(place.tensor * rows, rows)
    before = pl.multiple_of(jnp.maximum(start - rows, 0), rows)
    halo_doc = jnp.where(place.tensor > 0, docs[:, pl.ds(before, rows)], -1)
    own_doc = docs[:, pl.ds(start, rows)]
    doc_pieces = []
    for source in (halo_doc, own_doc):
        for r in range(blocks):
            piece = source[:, r * HALF_WINDOW : (r + 1) * HALF_WINDOW]
            doc_pieces.append(as_column(piece)[:, 0:1])
    for r in range(blocks):
        doc_q = own_doc[:, r * HALF_WINDOW : (r + 1) * HALF_WINDOW].astype(jnp.float32)
        for j in range(window // HALF_WINDOW):
            key_at = lax.broadcasted_iota(jnp.int32, (HALF_WINDOW, HALF_WINDOW), 0)
            query_at = lax.broadcasted_iota(jnp.int32, (HALF_WINDOW, HALF_WINDOW), 1)
            offset = query_at + rows - key_at - j * HALF_WINDOW
            allowed = (offset >= 0) & (offset < WINDOW) & (doc_q == doc_pieces[r + j])
            bias[(r,) + tile(j)] = jnp.where(allowed, 0.0, -1000000000.0)

    exponent = lax.broadcasted_iota(jnp.int32, (1, head // 2), 1).astype(jnp.float32)
    frequency = jnp.exp(exponent * (-2.0 / head * math.log(ROPE_BASE)))
    for i in range(rows // BLOCK):
        own = pl.ds(pl.multiple_of(start + i * BLOCK, BLOCK), BLOCK)
        angle = as_column(positions[:, own]) * frequency
        cosine[i * BLOCK : (i + 1) * BLOCK, :] = jnp.cos(angle)
        sine[i * BLOCK : (i + 1) * BLOCK, :] = jnp.sin(angle)

    s.gain_sums[...] = jnp.zeros_like(s.gain_sums)
    s.qk_sums[...] = jnp.zeros_like(s.qk_sums)

    @pl.when(place.tensor == 0)
    def _():
        s.keyval[0:rows, :] = jnp.zeros((rows, 2 * head), jnp.bfloat16)

    through(2)
    gathers[KV].ready()

    gain_rows = jnp.zeros((PAD_ROWS, width), jnp.float32)
    qk_part = jnp.zeros((PAD_ROWS, head), jnp.float32)
    for d in range(8):
        block = slots[KV][0, d // 2, d % 2, shard:, :]
        gain_rows += nn(block, spread(shard, width, d))
        qk_part += nn(block, spread(qk_rows, head, d))
    s.gains[...] = gain_rows
    s.qk_table[...] = qk_part
    for quarter in range(parts):
        columns = slice(quarter * GAIN_COLUMNS, (quarter + 1) * GAIN_COLUMNS)
        s.w_keyval[:, columns] = slots[KV][
            place.flip_part(quarter), :, :, 0:shard, :
        ].reshape(width, GAIN_COLUMNS)
    query_gain = s.qk_table[4:5, :]
    key_gain = s.qk_table[5:6, :]

    def norm_tokens(start):
        at = pl.ds(start, BLOCK)
        values = tokens[at, :].astype(jnp.float32)
        low = (values * inverse_rms(values) * s.gains[0:1, :]).astype(jnp.bfloat16)
        s.normed[at, :] = low
        s.normed_t[:, at] = transposed(low)

    each_block(rows, BLOCK, norm_tokens)
    pump(4)

    def make_keys(start):
        at = pl.ds(start, BLOCK)
        raw = nn(s.normed[at, :], s.w_keyval[...])
        key = raw[:, :head]
        s.key_raw[at, :] = key
        key = rotate(key * inverse_rms(key) * key_gain, cosine[at, :], sine[at, :])
        both = jnp.concatenate([key, raw[:, head:]], axis=1).astype(jnp.bfloat16)
        own = pl.ds(pl.multiple_of(rows + start, BLOCK), BLOCK)
        s.keyval[own, :] = both
        s.keyval_t[:, own] = transposed(both)

    each_block(rows, BLOCK, make_keys)

    next_part = jnp.minimum(place.tensor + 1, parts - 1)
    halo = pltpu.make_async_remote_copy(
        src_ref=s.keyval.at[pl.ds(rows, rows)],
        dst_ref=s.keyval.at[pl.ds(0, rows)],
        send_sem=halo_sems.at[0],
        recv_sem=halo_sems.at[1],
        device_id=(place.dp, next_part),
        device_id_type=MESH_ID,
    )

    @pl.when(place.tensor < parts - 1)
    def _():
        halo.start()

    through(3)
    gathers[Q].ready()
    for k in range(parts):
        s.query_raw[k] = nn(s.normed[...], weight(Q, k))

        def make_queries(start, k=k):
            at = pl.ds(start, BLOCK)
            raw = s.query_raw[k, at, :]
            low = rotate(raw * inverse_rms(raw) * query_gain, cosine[at, :], sine[at, :])
            s.queries[k, at, :] = (low * head ** (-0.5)).astype(jnp.bfloat16)

        each_block(rows, BLOCK, make_queries)
        pump(4)
    through(4)

    @pl.when(place.tensor > 0)
    def _():
        halo.wait_recv()

    def turn_halo(start):
        at = pl.ds(start, BLOCK)
        s.keyval_t[:, at] = transposed(s.keyval[at, :])

    each_block(rows, BLOCK, turn_halo)

    for k in range(parts):
        for r in range(blocks):
            at = slice(r * HALF_WINDOW, (r + 1) * HALF_WINDOW)
            query = s.queries[k, at, :]
            total = jnp.zeros((1, HALF_WINDOW), jnp.float32)
            for j in range(window // HALF_WINDOW):
                inner = slice(j * HALF_WINDOW, (j + 1) * HALF_WINDOW)
                outer = slice((r + j) * HALF_WINDOW, (r + j + 1) * HALF_WINDOW)
                score = dot_last(s.keyval[outer, :head], query) + bias[(r,) + tile(j)]
                score = jnp.exp(score)
                scores[tile(j)] = score
                total += jnp.sum(score, axis=0, keepdims=True)
            scale = 1.0 / total
            for j in range(window // HALF_WINDOW):
                inner = slice(j * HALF_WINDOW, (j + 1) * HALF_WINDOW)
                s.probs[k, r, inner, :] = (scores[tile(j)] * scale).astype(jnp.bfloat16)
            mixed = nn(
                s.keyval_t[head:, r * HALF_WINDOW : r * HALF_WINDOW + window], s.probs[k, r]
            )
            s.context[k, at, :] = mixed.T.astype(jnp.bfloat16)
            pump(3)

    through(5)
    gathers[OUT].ready()
    for k in range(parts):
        share = dot_last(s.context[k], weight(OUT, k))
        if k == 0:
            s.attn[...] = share
        else:
            s.attn[...] += share
    pump(3)

    def norm_attn(start):
        at = pl.ds(start, BLOCK)
        attn = s.attn[at, :]
        residual = tokens[at, :].astype(jnp.float32) + attn * inverse_rms(attn) * s.gains[1:2, :]
        s.residual[at, :] = residual
        low = (residual * inverse_rms(residual) * s.gains[2:3, :]).astype(jnp.bfloat16)
        s.ffn_in[at, :] = low
        s.ffn_in_t[:, at] = transposed(low)

    each_block(rows, BLOCK, norm_attn)
    gathers[GATE].ready()
    for k in range(parts):
        s.gate_pre[k] = nn(s.ffn_in[...], weight(GATE, k))
        pump(2)
    through(6)
    gathers[UP].ready()
    for k in range(parts):
        s.up_pre[...] = nn(s.ffn_in[...], weight(UP, k))

        def activate(start, k=k):
            at = pl.ds(start, 32)
            gate = s.gate_pre[k, at, :]
            up = s.up_pre[at, :]
            square = gate * gate
            tanh = jnp.tanh(GELU_SCALE * gate * (1.0 + 0.044715 * square))
            upper = 0.5 * (1.0 + tanh)
            gelu = gate * upper
            slope = upper + (
                0.5 * GELU_SCALE * gate * (1.0 - tanh * tanh) * (1.0 + 3 * 0.044715 * square)
            )
            s.gelu_out[k, at, :] = gelu.astype(jnp.bfloat16)
            s.gelu_slope[k, at, :] = (slope * up).astype(jnp.bfloat16)
            s.hidden[k, at, :] = (gelu * up).astype(jnp.bfloat16)

        each_block(rows, 32, activate)
        pump(2)
    through(7)
    gathers[DOWN].ready()
    for k in range(parts):
        share = dot_last(s.hidden[k], weight(DOWN, k))
        if k == 0:
            s.ffn[...] = share
        else:
            s.ffn[...] += share
    for name in GROUPS:
        gathers[name].finish()

    def top_block(start):
        at = pl.ds(start, BLOCK)
        ffn = s.ffn[at, :]
        gain = s.gains[3:4, :]
        top = cotangent[at, :].astype(jnp.float32)
        inverse = inverse_rms(ffn)
        block_out[at, :] = (s.residual[at, :] + ffn * inverse * gain).astype(jnp.bfloat16)
        grad, gain_rows = norm_back(ffn, gain, top)
        s.gain_sums[3:4, :] += jnp.sum(gain_rows, axis=0, keepdims=True)
        low = grad.astype(jnp.bfloat16)
        s.ffn_grad[at, :] = low
        s.ffn_grad_t[:, at] = transposed(low)

    each_block(rows, BLOCK, top_block)

    ffn_groups = (DOWN, GATE, UP)
    order = (3, 2, 1, 0)

    def for_ffn(step, k):
        for name in ffn_groups:
            scatter = scatters[name]
            if step is Scatter.from_second:
                step(scatter, k, totals[name])
            else:
                step(scatter, k)

    for i, k in enumerate(order):
        s.up_pre[...] = nn(s.ffn_grad[...], weight(DOWN, k))

        def activate_back(start, k=k):
            at = pl.ds(start, 32)
            grad = s.up_pre[at, :]
            s.gate_grad[at, :] = (
                grad * s.gelu_slope[k, at, :].astype(jnp.float32)
            ).astype(jnp.bfloat16)
            s.up_grad[at, :] = (
                grad * s.gelu_out[k, at, :].astype(jnp.float32)
            ).astype(jnp.bfloat16)

        each_block(rows, 32, activate_back)
        share = dot_last(s.gate_grad[...], weight(GATE, k))
        share += dot_last(s.up_grad[...], weight(UP, k))
        if i == 0:
            s.ffn[...] = share
        else:
            s.ffn[...] += share
        put_grad(DOWN, k, nn(s.ffn_grad_t[...], s.hidden[k]))
        scatters[DOWN].to_sibling(k)
        put_grad(GATE, k, nn(s.ffn_in_t[...], s.gate_grad[...]))
        scatters[GATE].to_sibling(k)
        put_grad(UP, k, nn(s.ffn_in_t[...], s.up_grad[...]))
        scatters[UP].to_sibling(k)
        if i >= 1:
            for_ffn(Scatter.from_sibling, order[i - 1])

    def middle_block(start):
        at = pl.ds(start, BLOCK)
        residual = s.residual[at, :]
        attn = s.attn[at, :]
        part, gain_rows = norm_back(residual, s.gains[2:3, :], s.ffn[at, :])
        s.gain_sums[2:3, :] += jnp.sum(gain_rows, axis=0, keepdims=True)
        residual_grad = cotangent[at, :].astype(jnp.float32) + part
        s.residual[at, :] = residual_grad
        grad, gain_rows = norm_back(attn, s.gains[1:2, :], residual_grad)
        s.gain_sums[1:2, :] += jnp.sum(gain_rows, axis=0, keepdims=True)
        low = grad.astype(jnp.bfloat16)
        s.attn_grad[at, :] = low
        s.attn_grad_t[:, at] = transposed(low)

    each_block(rows, BLOCK, middle_block)
    keyval_grad[...] = jnp.zeros(keyval_grad.shape, jnp.float32)
    for_ffn(Scatter.from_sibling, 0)

    for k in range(parts):
        context_grad[k] = nn(s.attn_grad[...], weight(OUT, k)).astype(jnp.bfloat16)
        put_grad(OUT, k, nn(s.attn_grad_t[...], s.context[k]))
        scatters[OUT].to_sibling(k)

    def for_all(step, name):
        for k in order:
            if step is Scatter.from_second:
                step(scatters[name], k, totals[name])
            else:
                step(scatters[name], k)

    later = [
        lambda: for_ffn(Scatter.from_first, 3),
        lambda: for_all(Scatter.from_sibling, OUT),
        lambda: for_ffn(Scatter.from_first, 2),
        lambda: for_ffn(Scatter.from_second, 3),
        lambda: for_ffn(Scatter.from_first, 1),
        lambda: for_ffn(Scatter.from_second, 2),
        lambda: for_ffn(Scatter.from_first, 0),
        lambda: for_ffn(Scatter.from_second, 1),
    ]
    last_part = jnp.maximum(place.tensor - 1, 0)
    half = rows // blocks
    halo_back = []
    for r in range(blocks):
        halo_back.append(
            pltpu.make_async_remote_copy(
                src_ref=halo_out.at[pl.ds(r * half, half)],
                dst_ref=s.halo_in.at[pl.ds(r * half, half)],
                send_sem=halo_sems.at[2 + r],
                recv_sem=halo_sems.at[4 + r],
                device_id=(place.dp, last_part),
                device_id_type=MESH_ID,
            )
        )

    @pl.when(place.tensor == parts - 1)
    def _():
        s.halo_in[...] = jnp.zeros_like(s.halo_in)

    for r in range(blocks):
        for k in range(parts):
            at = slice(r * HALF_WINDOW, (r + 1) * HALF_WINDOW)
            query = s.queries[k, at, :]
            grad = context_grad[k, at, :]
            delta = jnp.zeros((1, HALF_WINDOW), jnp.float32)
            for j in range(window // HALF_WINDOW):
                inner = slice(j * HALF_WINDOW, (j + 1) * HALF_WINDOW)
                outer = slice((r + j) * HALF_WINDOW, (r + j + 1) * HALF_WINDOW)
                prob_grad = dot_last(s.keyval[outer, head:], grad)
                scores[tile(j)] = prob_grad
                probs = s.probs[k, r, inner, :].astype(jnp.float32)
                delta += jnp.sum(probs * prob_grad, axis=0, keepdims=True)
            for j in range(window // HALF_WINDOW):
                inner = slice(j * HALF_WINDOW, (j + 1) * HALF_WINDOW)
                outer = slice((r + j) * HALF_WINDOW, (r + j + 1) * HALF_WINDOW)
                probs = s.probs[k, r, inner, :]
                score_grad = probs.astype(jnp.float32) * (scores[tile(j)] - delta)
                score_grad = score_grad.astype(jnp.bfloat16)
                s.score_grad[inner, :] = score_grad
                which, outer = keyval_rows(r + j)
                keyval_grad[which, outer, :head] += nn(score_grad, query)
                keyval_grad[which, outer, head:] += nn(probs, grad)
            turned = nn(
                s.keyval_t[:head, r * HALF_WINDOW : r * HALF_WINDOW + window],
                s.score_grad[...],
            )
            query_grad = turned.T * head ** (-0.5)
            query_grad = rotate(query_grad, cosine[at, :], -sine[at, :])
            raw_grad, gain_rows = norm_back(s.query_raw[k, at, :], query_gain, query_grad)
            s.qk_sums[4:5, :] += jnp.sum(gain_rows, axis=0, keepdims=True)
            query_grads[k, at, :] = raw_grad.astype(jnp.bfloat16)
            if r == blocks - 1:
                share = dot_last(query_grads[k], weight(Q, k))
                if k == 0:
                    s.ffn[...] = share
                else:
                    s.ffn[...] += share
                put_grad(Q, k, nn(s.normed_t[...], query_grads[k]))
                scatters[Q].to_sibling(k)
            later.pop(0)()
        at = slice(r * half, (r + 1) * half)
        halo_out[at, :] = keyval_grad[0, at, :].astype(jnp.bfloat16)

        @pl.when(place.tensor > 0)
        def _(r=r):
            halo_back[r].start()

    for_all(Scatter.from_sibling, Q)
    for_all(Scatter.from_first, OUT)
    for_ffn(Scatter.from_second, 0)

    @pl.when(place.tensor < parts - 1)
    def _():
        for copy in halo_back:
            copy.wait_recv()

    def key_block(start):
        at = pl.ds(start, BLOCK)
        grads = keyval_grad[1, at, :] + s.halo_in[at, :].astype(jnp.float32)
        key_grad = rotate(grads[:, :head], cosine[at, :], -sine[at, :])
        raw_grad, gain_rows = norm_back(s.key_raw[at, :], key_gain, key_grad)
        s.qk_sums[5:6, :] += jnp.sum(gain_rows, axis=0, keepdims=True)
        keyval_low[at, :] = jnp.concatenate([raw_grad, grads[:, head:]], axis=1).astype(
            jnp.bfloat16
        )

    each_block(rows, BLOCK, key_block)
    s.ffn[...] += dot_last(keyval_low[...], s.w_keyval[...])

    def bottom_block(start):
        at = pl.ds(start, BLOCK)
        values = tokens[at, :].astype(jnp.float32)
        part, gain_rows = norm_back(values, s.gains[0:1, :], s.ffn[at, :])
        s.gain_sums[0:1, :] += jnp.sum(gain_rows, axis=0, keepdims=True)
        tokens_grad[at, :] = s.residual[at, :] + part

    each_block(rows, BLOCK, bottom_block)
    for quarter in range(parts):
        columns = slice(quarter * GAIN_COLUMNS, (quarter + 1) * GAIN_COLUMNS)
        value = nn(s.normed_t[...], keyval_low[:, columns])
        slots[KV][place.flip_part(quarter), :, :, 0:shard, :] = value.astype(
            jnp.bfloat16
        ).reshape(4, 2, shard, GAIN_COLUMNS)
    gain_low = s.gain_sums[...].astype(jnp.bfloat16)
    qk_low = s.qk_sums[...].astype(jnp.bfloat16)
    for d in range(8):
        block = dot_last(gain_low, spread(shard, width, d))
        block += dot_last(qk_low, spread(qk_rows, head, d))
        for k in range(parts):
            slots[KV][k, d // 2, d % 2, shard:, :] = block.astype(jnp.bfloat16)
    for k in range(parts):
        scatters[KV].to_sibling(k)
    for_all(Scatter.from_sibling, KV)
    for_all(Scatter.from_first, Q)
    for_all(Scatter.from_second, OUT)
    for_all(Scatter.from_first, KV)
    for_all(Scatter.from_second, Q)
    for k in order:
        scatters[KV].from_second(k, s.kv_total)
    for name in ffn_groups + (OUT, Q):
        scatters[name].from_tensor(totals[name])
    scatters[KV].from_tensor(s.kv_total)
    shared[0] = s.kv_total[...]
    copies = []
    for k in (1, 2, 3):
        copies.append(
            pltpu.make_async_remote_copy(
                src_ref=s.kv_total,
                dst_ref=shared.at[k],
                send_sem=share_send.at[k],
                recv_sem=share_recv.at[k],
                device_id=place.along(k),
                device_id_type=MESH_ID,
            )
        )
    for copy in copies:
        copy.start()
    for copy in copies:
        copy.wait()
    for name in GROUPS:
        scatters[name].finish()

    @pl.when(place.tensor < parts - 1)
    def _():
        halo.wait_send()

    @pl.when(place.tensor > 0)
    def _():
        for copy in halo_back:
            copy.wait_send()


def finish_kernel(count, *refs):
    sources, shared = refs[:count], refs[count]
    targets, keyval, norm_gains, qk_gains = (refs[count + 1 : 2 * count + 1],) + refs[
        2 * count + 1 : 2 * count + 4
    ]
    sems = refs[2 * count + 4]
    copies = [
        pltpu.make_async_copy(source, target, sems.at[i])
        for i, (source, target) in enumerate(zip(sources, targets))
    ]
    for copy in copies:
        copy.start()
    place = Place()
    shard, qk_rows = norm_gains.shape[1], qk_gains.shape[1]
    for part in range(4):
        columns = slice(part * GAIN_COLUMNS, (part + 1) * GAIN_COLUMNS)
        keyval[:, columns] = shared[place.flip_part(part), 0:shard, :]
    norm_gains[...] = shared[0, shard : shard + 4, 0:shard]
    qk_gains[...] = shared[0, shard + 4 : shard + 6, 0:qk_rows]
    for copy in copies:
        copy.wait()


def per_device_direct(
    tokens,
    segments,
    positions,
    norm_gains,
    qk_gains,
    q_weight,
    kv_weight,
    out_weight,
    gate_weight,
    up_weight,
    down_weight,
    cotangent,
):
    parts = lax.axis_size("tensor")
    rows, width = tokens.shape
    shard = q_weight.shape[0]
    head = q_weight.shape[1]
    ff_part = gate_weight.shape[1]
    arguments = [
        tokens,
        cotangent,
        segments[None, :],
        positions[None, :],
        norm_gains,
        qk_gains,
        kv_weight,
        q_weight,
        out_weight.T,
        gate_weight,
        up_weight,
        down_weight.T,
    ]
    kv_shape = (shard + PAD_ROWS, GAIN_COLUMNS)
    shapes = [kv_shape] + [w.shape for w in arguments[7:]]
    buffers = layer_scratch(rows, width, head, ff_part, shard, parts)
    scratch = [pltpu.VMEM(*buffer) for buffer in buffers.values()]
    scratch += [pltpu.VMEM((4, 4, 2) + shape, jnp.bfloat16) for shape in shapes]
    scratch += Gather.scratch() * len(shapes)
    for shape in shapes:
        scratch += Scatter.scratch(*shape)
    scratch += [pltpu.SemaphoreType.DMA((4,))] * 2 + [pltpu.SemaphoreType.DMA((6,))]
    f32 = jnp.float32
    whole = pl.BlockSpec(memory_space=pltpu.VMEM)
    anywhere = pl.BlockSpec(memory_space=pl.ANY)
    kinds = [
        jax.ShapeDtypeStruct((rows, width), jnp.bfloat16),
        jax.ShapeDtypeStruct((rows, width), f32),
    ] + [jax.ShapeDtypeStruct(shape, f32) for shape in shapes[1:]]
    results = pl.pallas_call(
        functools.partial(layer_kernel, list(buffers)),
        out_shape=kinds + [jax.ShapeDtypeStruct((parts,) + kv_shape, f32)],
        in_specs=[whole] * len(arguments),
        out_specs=[whole] * 8,
        scratch_shapes=scratch,
        compiler_params=pltpu.CompilerParams(
            collective_id=0, has_side_effects=True, vmem_limit_bytes=VMEM_BYTES
        ),
        name="layer",
    )(*arguments)
    results = pl.pallas_call(
        functools.partial(finish_kernel, len(kinds)),
        out_shape=kinds
        + [
            jax.ShapeDtypeStruct(kv_weight.shape, f32),
            jax.ShapeDtypeStruct(norm_gains.shape, f32),
            jax.ShapeDtypeStruct(qk_gains.shape, f32),
        ],
        in_specs=[whole] * (len(kinds) + 1),
        out_specs=[anywhere] * len(kinds) + [whole] * 3,
        scratch_shapes=[pltpu.SemaphoreType.DMA((len(kinds),))],
        name="finish",
    )(*results)
    block_out, tokens_grad, q_sum, out_sum, gate_sum, up_sum, down_sum = results[:7]
    keyval, norm_sum, qk_sum = results[7:]
    return (
        block_out,
        tokens_grad,
        norm_sum,
        qk_sum,
        q_sum,
        keyval,
        out_sum.T,
        gate_sum,
        up_sum,
        down_sum.T,
    )


def pack_shards(norm_gains, qk_gains, q_weight, kv_weight, out_weight, gate_weight, up_weight, down_weight):
    rows = q_weight.shape[0]
    kv_columns = kv_weight.shape[1] // lax.axis_size("tensor")
    kv_part = lax.dynamic_slice_in_dim(
        kv_weight, lax.axis_index("tensor") * kv_columns, kv_columns, axis=1
    )
    gain_part = jnp.concatenate(
        [
            norm_gains.T,
            jnp.pad(qk_gains.T, ((0, rows - qk_gains.shape[1]), (0, 0))),
            jnp.zeros((rows, GAIN_COLUMNS - 6), jnp.bfloat16),
        ],
        axis=1,
    )
    return jnp.concatenate(
        [q_weight, out_weight.T, gate_weight, up_weight, down_weight.T, kv_part, gain_part],
        axis=1,
    )


def gather_weights(packed):
    return lax.all_gather(packed, ("tensor", "dp"), axis=0, tiled=True)


def reduce_grads(grads):
    return lax.psum_scatter(
        grads, ("tensor", "dp"), scatter_dimension=0, tiled=True
    ).astype(jnp.float32)


def per_device(
    tokens,
    segments,
    positions,
    norm_gains,
    qk_gains,
    q_weight,
    kv_weight,
    out_weight,
    gate_weight,
    up_weight,
    down_weight,
    cotangent,
):
    parts = lax.axis_size("tensor")
    place = lax.axis_index("tensor")
    rows, width = tokens.shape
    shard_rows = q_weight.shape[0]
    head_width = q_weight.shape[1]
    ff_part = gate_weight.shape[1]
    kv_columns = kv_weight.shape[1]
    kv_part = kv_columns // parts
    qk_rows = qk_gains.shape[1]
    ends = [0]
    for columns in (head_width, head_width, ff_part, ff_part, ff_part, kv_part, GAIN_COLUMNS):
        ends.append(ends[-1] + columns)

    packed = pack_shards(
        norm_gains, qk_gains, q_weight, kv_weight, out_weight, gate_weight, up_weight, down_weight
    )
    gathered = gather_weights(packed).reshape(parts, width, ends[-1])
    halo = lax.ppermute(tokens, "tensor", [(i, i + 1) for i in range(parts - 1)])

    def piece(index):
        return [gathered[t, :, ends[index] : ends[index + 1]] for t in range(parts)]

    w_query, w_out, w_gate, w_up, w_down, w_kv = (piece(i) for i in range(6))
    w_keyval = jnp.concatenate(w_kv, axis=1)
    w_gains = gathered[0, :, ends[6] : ends[7]].astype(jnp.float32)
    gain_table = w_gains[:, :4].T
    qk_table = w_gains.reshape(-1, shard_rows, GAIN_COLUMNS)[:, :qk_rows, 4:6]
    qk_table = qk_table.reshape(head_width, 2).T

    own_input = tokens.astype(jnp.float32)
    both_input = jnp.concatenate([halo, tokens], axis=0).astype(jnp.float32)
    normed_both = norm_rows(both_input, gain_table[0]).astype(jnp.bfloat16)
    normed = normed_both[rows:]
    start = place * rows
    first = jnp.maximum(start - rows, 0)
    own_doc = lax.dynamic_slice_in_dim(segments, start, rows)
    halo_doc = jnp.where(place > 0, lax.dynamic_slice_in_dim(segments, first, rows), -1)
    both_doc = jnp.concatenate([halo_doc, own_doc])
    both_place = jnp.concatenate(
        [
            lax.dynamic_slice_in_dim(positions, first, rows),
            lax.dynamic_slice_in_dim(positions, start, rows),
        ]
    )
    half_width = head_width // 2
    frequency = ROPE_BASE ** (-jnp.arange(half_width, dtype=jnp.float32) * 2.0 / head_width)
    angles = both_place.astype(jnp.float32)[:, None] * frequency[None, :]
    cosine_both = jnp.cos(angles)
    sine_both = jnp.sin(angles)
    cosine_own, sine_own = cosine_both[rows:], sine_both[rows:]

    offsets = jnp.arange(rows)[:, None] + rows - jnp.arange(2 * rows)[None, :]
    allowed = (offsets >= 0) & (offsets < WINDOW) & (own_doc[:, None] == both_doc[None, :])
    score_scale = head_width ** (-0.5)

    keyval_raw = dot_plain(normed_both, w_keyval)
    key_raw = keyval_raw[:, :head_width]
    keys = rotate(norm_rows(key_raw, qk_table[1]), cosine_both, sine_both).astype(jnp.bfloat16)
    value_rows = keyval_raw[:, head_width:].astype(jnp.bfloat16)

    query_raw, queries, lse, context = [], [], [], []
    attn_own = None
    for t in range(parts):
        raw = dot_plain(normed, w_query[t])
        low = rotate(norm_rows(raw, qk_table[0]), cosine_own, sine_own).astype(jnp.bfloat16)
        masked = jnp.where(allowed, dot_last(low, keys) * score_scale, -1000000000.0)
        row_max = jnp.max(masked, axis=1, keepdims=True)
        exponent = jnp.exp(masked - row_max)
        row_total = jnp.sum(exponent, axis=1, keepdims=True)
        probabilities = (exponent / row_total).astype(jnp.bfloat16)
        mixed = dot_plain(probabilities, value_rows).astype(jnp.bfloat16)
        query_raw.append(raw)
        queries.append(low)
        lse.append(row_max + jnp.log(row_total))
        context.append(mixed)
        share = dot_last(mixed, w_out[t])
        attn_own = share if attn_own is None else attn_own + share

    residual = own_input + norm_rows(attn_own, gain_table[1])
    ffn_in = norm_rows(residual, gain_table[2]).astype(jnp.bfloat16)
    gate_pre, up_pre, hidden = [], [], []
    ffn_out = None
    for t in range(parts):
        gate_pre.append(dot_plain(ffn_in, w_gate[t]))
        up_pre.append(dot_plain(ffn_in, w_up[t]))
        hidden.append(geglu(gate_pre[t], up_pre[t]).astype(jnp.bfloat16))
        share = dot_last(hidden[t], w_down[t])
        ffn_out = share if ffn_out is None else ffn_out + share
    block_out = (residual + norm_rows(ffn_out, gain_table[3])).astype(jnp.bfloat16)
    top_grad = cotangent.astype(jnp.float32)
    ffn_grad_value, post_gain_rows = norm_back(ffn_out, gain_table[3], top_grad)
    ffn_grad = ffn_grad_value.astype(jnp.bfloat16)
    ffn_in_grad = None
    grads = [[] for _ in range(parts)]
    down_wgrad, gate_wgrad, up_wgrad = [], [], []
    for t in range(parts):
        hidden_grad = dot_plain(ffn_grad, w_down[t])
        gelu_back = jax.vjp(geglu, gate_pre[t], up_pre[t])[1]
        gate_grad_value, up_grad_value = gelu_back(hidden_grad)
        gate_grad = gate_grad_value.astype(jnp.bfloat16)
        up_grad = up_grad_value.astype(jnp.bfloat16)
        share = dot_last(gate_grad, w_gate[t]) + dot_last(up_grad, w_up[t])
        ffn_in_grad = share if ffn_in_grad is None else ffn_in_grad + share
        gate_wgrad.append(dot_first(ffn_in, gate_grad))
        up_wgrad.append(dot_first(ffn_in, up_grad))
        down_wgrad.append(dot_first(ffn_grad, hidden[t]))
    residual_part, pre_ffn_rows = norm_back(residual, gain_table[2], ffn_in_grad)
    residual_grad = top_grad + residual_part
    attn_grad_value, post_attn_rows = norm_back(attn_own, gain_table[1], residual_grad)
    attn_grad = attn_grad_value.astype(jnp.bfloat16)

    key_grad, value_grad, normed_grad = None, None, None
    query_gain_grad = None
    out_wgrad, query_wgrad = [], []
    for t in range(parts):
        context_grad = dot_plain(attn_grad, w_out[t]).astype(jnp.bfloat16)
        out_wgrad.append(dot_first(attn_grad, context[t]))
        masked = jnp.where(allowed, dot_last(queries[t], keys) * score_scale, -1000000000.0)
        probabilities = jnp.exp(masked - lse[t])
        prob_grad = dot_last(context_grad, value_rows)
        row_delta = jnp.sum(probabilities * prob_grad, axis=1, keepdims=True)
        score_grad = (probabilities * (prob_grad - row_delta) * score_scale).astype(jnp.bfloat16)
        query_grad = dot_plain(score_grad, keys)
        key_share = dot_first(score_grad, queries[t])
        value_share = dot_first(probabilities.astype(jnp.bfloat16), context_grad)
        key_grad = key_share if key_grad is None else key_grad + key_share
        value_grad = value_share if value_grad is None else value_grad + value_share
        unrotated = rotate(query_grad, cosine_own, -sine_own)
        raw_grad, gain_rows = norm_back(query_raw[t], qk_table[0], unrotated)
        gain_share = jnp.sum(gain_rows, axis=0)
        query_gain_grad = gain_share if query_gain_grad is None else query_gain_grad + gain_share
        raw_low = raw_grad.astype(jnp.bfloat16)
        share = dot_last(raw_low, w_query[t])
        normed_grad = share if normed_grad is None else normed_grad + share
        query_wgrad.append(dot_first(normed, raw_low))
    key_raw_grad, key_gain_rows = norm_back(
        key_raw, qk_table[1], rotate(key_grad, cosine_both, -sine_both)
    )
    keyval_low = jnp.concatenate([key_raw_grad, value_grad], axis=1).astype(jnp.bfloat16)
    next_part = lax.ppermute(
        keyval_low[:rows], "tensor", [(i + 1, i) for i in range(parts - 1)]
    )
    keyval_wgrad = dot_first(normed_both, keyval_low)
    keyval_own = (keyval_low[rows:].astype(jnp.float32) + next_part.astype(jnp.float32)).astype(
        jnp.bfloat16
    )
    normed_grad = normed_grad + dot_last(keyval_own, w_keyval)
    input_part, pre_attn_rows = norm_back(own_input, gain_table[0], normed_grad)
    tokens_grad = residual_grad + input_part

    gain_grads = jnp.stack(
        [
            jnp.sum(pre_attn_rows, axis=0),
            jnp.sum(post_attn_rows, axis=0),
            jnp.sum(pre_ffn_rows, axis=0),
            jnp.sum(post_gain_rows, axis=0),
        ],
        axis=1,
    )
    qk_grads = jnp.stack([query_gain_grad, jnp.sum(key_gain_rows, axis=0)], axis=1)
    qk_grads = jnp.pad(
        qk_grads.reshape(-1, qk_rows, 2), ((0, 0), (0, shard_rows - qk_rows), (0, 0))
    ).reshape(width, 2)
    gain_columns = jnp.concatenate(
        [gain_grads, qk_grads, jnp.zeros((width, GAIN_COLUMNS - 6), jnp.float32)], axis=1
    )
    blocks = []
    for t in range(parts):
        blocks.append(
            jnp.concatenate(
                [
                    value.astype(jnp.bfloat16)
                    for value in (
                        query_wgrad[t],
                        out_wgrad[t],
                        gate_wgrad[t],
                        up_wgrad[t],
                        down_wgrad[t],
                        keyval_wgrad[:, t * kv_part : (t + 1) * kv_part],
                        gain_columns if t == 0 else jnp.zeros_like(gain_columns),
                    )
                ],
                axis=1,
            )
        )
    reduced = reduce_grads(jnp.concatenate(blocks, axis=0))
    shared = lax.all_gather(reduced[:, ends[5] :], "tensor", axis=0)
    keyval_out = jnp.concatenate([shared[t, :, :kv_part] for t in range(parts)], axis=1)
    gain_out = shared[0, :, kv_part:]
    cut = [reduced[:, ends[i] : ends[i + 1]] for i in range(5)]
    return (
        block_out,
        tokens_grad,
        gain_out[:, :4].T,
        gain_out[:qk_rows, 4:6].T,
        cut[0],
        keyval_out,
        cut[1].T,
        cut[2],
        cut[3],
        cut[4].T,
    )


def solution(mesh):
    direct = mesh.shape["dp"] == 8 and mesh.shape["tensor"] == 4
    return jax.shard_map(
        per_device_direct if direct else per_device,
        mesh=mesh,
        in_specs=(
            P(("dp", "tensor"), None),
            P("dp"),
            P("dp"),
            P(None, "dp"),
            P(None, "dp"),
            P("dp", "tensor"),
            P("dp", None),
            P("tensor", "dp"),
            P("dp", "tensor"),
            P("dp", "tensor"),
            P("tensor", "dp"),
            P(("dp", "tensor"), None),
        ),
        out_specs=(
            P(("dp", "tensor"), None),
            P(("dp", "tensor"), None),
            P(None, "dp"),
            P(None, "dp"),
            P("dp", "tensor"),
            P("dp", None),
            P("tensor", "dp"),
            P("dp", "tensor"),
            P("dp", "tensor"),
            P("tensor", "dp"),
        ),
        check_vma=False,
    )
```

```python
import functools
import math
import types

import jax
import jax.numpy as jnp
from jax import lax
from jax.experimental import pallas as pl
from jax.experimental.pallas import tpu as pltpu
from jax.sharding import PartitionSpec as P

WINDOW = 512
GAIN_COLUMNS = 128


EPSILON = 1e-06
ROPE_BASE = 10000.0
GELU_SCALE = 0.7978845608028654


def norm_rows(values, gain_row):
    return (
        values * lax.rsqrt(jnp.mean(values * values, axis=-1, keepdims=True) + EPSILON) * gain_row
    )


def norm_back(values, gain_row, grad_out):
    inv_rms = lax.rsqrt(jnp.mean(values * values, axis=-1, keepdims=True) + EPSILON)
    weighted = grad_out * gain_row
    inner_mean = jnp.mean(values * weighted, axis=-1, keepdims=True)
    return (
        inv_rms * weighted - values * inv_rms * inv_rms * inv_rms * inner_mean,
        grad_out * values * inv_rms,
    )


def rotate(values, cosine_table, sine_table):
    half_width = values.shape[-1] // 2
    first_half = values[..., :half_width]
    second_half = values[..., half_width:]
    return jnp.concatenate(
        [
            first_half * cosine_table - second_half * sine_table,
            second_half * cosine_table + first_half * sine_table,
        ],
        axis=-1,
    )


def geglu(gate_pre, up_pre):
    inner_term = GELU_SCALE * (gate_pre + 0.044715 * gate_pre * gate_pre * gate_pre)
    return 0.5 * gate_pre * (1.0 + jnp.tanh(inner_term)) * up_pre


def dot_plain(left_side, right_side):
    return jnp.dot(left_side, right_side, preferred_element_type=jnp.float32)


def dot_last(left_side, right_side):
    return lax.dot_general(
        left_side, right_side, (((1,), (1,)), ((), ())), preferred_element_type=jnp.float32
    )


def dot_first(left_side, right_side):
    return lax.dot_general(
        left_side, right_side, (((0,), (0,)), ((), ())), preferred_element_type=jnp.float32
    )


MESH_ID = pl.DeviceIdType.MESH
PAD_ROWS = 16


class Place:
    def __init__(self):
        self.dp = lax.axis_index("dp")
        self.tensor = lax.axis_index("tensor")
        self.core = lax.rem(self.dp, 2)
        self.chip = self.dp // 2

    def flip_dp(self, bits):
        flipped = self.dp
        for bit in (1, 2, 4):
            if bits & bit:
                flipped = flipped + bit - 2 * bit * lax.rem(self.dp // bit, 2)
        return flipped

    def flip_chip(self, bits):
        return self.flip_dp(2 * bits) // 2

    def flip_tensor(self, bits):
        flipped = self.tensor
        for bit in (1, 2):
            if bits & bit:
                flipped = flipped + bit - 2 * bit * lax.rem(self.tensor // bit, 2)
        return flipped

    def flip_part(self, part):
        return self.flip_tensor(part)

    def near(self, bits):
        return (self.flip_dp(bits), self.tensor)

    def along(self, bits):
        return (self.dp, self.flip_tensor(bits))

    def greet(self):
        partners = [self.near(1), self.near(2), self.near(4)] + [self.along(k) for k in (1, 2, 3)]
        barrier = pltpu.get_barrier_semaphore()
        for partner in partners:
            pl.semaphore_signal(barrier, inc=1, device_id=partner, device_id_type=MESH_ID)
        pl.semaphore_wait(barrier, len(partners))


class Gather:
    SENDS = 32

    def __init__(self, place, shard, slots, send_sem, recv_sem, local_sem):
        self.place, self.shard, self.slots = place, shard, slots
        self.send_sem, self.recv_sem, self.local_sem = send_sem, recv_sem, local_sem
        self.sent = []

    @staticmethod
    def scratch():
        return [
            pltpu.SemaphoreType.DMA((Gather.SENDS,)),
            pltpu.SemaphoreType.DMA((32,)),
            pltpu.SemaphoreType.DMA,
        ]

    def send(self, source, slot, dp, device, lane):
        copy = pltpu.make_async_remote_copy(
            src_ref=source,
            dst_ref=self.slots.at[slot, dp // 2, lax.rem(dp, 2)],
            send_sem=self.send_sem.at[len(self.sent)],
            recv_sem=self.recv_sem.at[slot * 8 + lane],
            device_id=device,
            device_id_type=MESH_ID,
        )
        copy.start()
        self.sent.append(copy)

    def landed(self, slot, bits):
        place = self.place
        dp = place.flip_dp(bits)
        block = self.slots.at[slot, dp // 2, lax.rem(dp, 2)]
        pltpu.make_async_remote_copy(
            src_ref=block,
            dst_ref=block,
            send_sem=self.send_sem.at[0],
            recv_sem=self.recv_sem.at[slot * 8 + bits],
            device_id=place.near(1),
            device_id_type=MESH_ID,
        ).wait_recv()
        return block, dp

    def begin(self):
        place = self.place
        self.local = pltpu.make_async_copy(
            self.shard, self.slots.at[0, place.chip, place.core], self.local_sem
        )
        self.local.start()
        for k in (1, 2, 3):
            self.send(self.shard, k, place.dp, place.along(k), 0)
        for bits in (2, 4, 1):
            self.send(self.shard, 0, place.dp, place.near(bits), bits)

    def from_tensor(self, k):
        block, dp = self.landed(k, 0)
        for bits in (2, 4, 1):
            self.send(block, k, dp, self.place.near(bits), bits)

    def from_first(self, k):
        bits, other = (2, 4) if k % 2 == 0 else (4, 2)
        block, dp = self.landed(k, bits)
        self.send(block, k, dp, self.place.near(other), 6)
        self.send(block, k, dp, self.place.near(1), bits + 1)

    def from_second(self, k):
        block, dp = self.landed(k, 4 if k % 2 == 0 else 2)
        self.send(block, k, dp, self.place.near(1), (4 if k % 2 == 0 else 2) + 1)

    def from_corner(self, k):
        block, dp = self.landed(k, 6)
        self.send(block, k, dp, self.place.near(1), 7)

    def ready(self):
        self.local.wait()
        for k in range(4):
            for bits in (1, 3, 5, 7):
                self.landed(k, bits)

    def finish(self):
        for copy in self.sent:
            copy.wait_send()


def gather_order(gathers):
    count = len(gathers)
    stages = []
    for i in range(count + 2):
        lanes = [[], [], []]
        if i < count:
            lanes[0] = [gathers[i].begin] + [
                functools.partial(gathers[i].from_tensor, k) for k in (1, 2, 3)
            ]
        if 0 <= i - 1 < count:
            lanes[1] = [functools.partial(gathers[i - 1].from_first, k) for k in range(4)]
        if 0 <= i - 2 < count:
            for k in range(4):
                lanes[2].append(functools.partial(gathers[i - 2].from_second, k))
                lanes[2].append(functools.partial(gathers[i - 2].from_corner, k))
        stage = []
        while any(lanes):
            for lane, share in zip(lanes, (1, 1, 2)):
                for _ in range(share):
                    if lane:
                        stage.append(lane.pop(0))
        stages.append(stage)
    return stages


class Scatter:
    def __init__(self, place, grads, sibling, first, second, last, sems, turns):
        self.place, self.grads, self.sibling = place, grads, sibling
        self.first, self.second, self.last = first, second, last
        self.send_sem, self.recv_sem = sems
        self.turns = turns
        self.sent = []

    @staticmethod
    def scratch(rows, columns):
        block = (rows, columns)
        return [
            pltpu.VMEM((4, 4) + block, jnp.bfloat16),
            pltpu.VMEM((2, 4) + block, jnp.bfloat16),
            pltpu.VMEM((4,) + block, jnp.bfloat16),
            pltpu.VMEM((4,) + block, jnp.bfloat16),
            pltpu.SemaphoreType.DMA((20,)),
            pltpu.SemaphoreType.DMA((20,)),
        ]

    def copy(self, source, target, lane, device):
        return pltpu.make_async_remote_copy(
            src_ref=source,
            dst_ref=target,
            send_sem=self.send_sem.at[lane],
            recv_sem=self.recv_sem.at[lane],
            device_id=device,
            device_id_type=MESH_ID,
        )

    def send(self, *args):
        copy = self.copy(*args)
        copy.start()
        self.sent.append(copy)

    def landed(self, target, lane):
        self.copy(target, target, lane, self.place.near(1)).wait_recv()

    def mine(self, k, chip):
        return self.grads.at[k, chip, self.place.core]

    def to_sibling(self, k):
        self.send(
            self.grads.at[k, :, 1 - self.place.core], self.sibling.at[k], k, self.place.near(1)
        )

    def from_sibling(self, k):
        place = self.place
        self.landed(self.sibling.at[k], k)

        def add(chip, carry):
            block = self.mine(k, chip)
            block[...] = (
                block[...].astype(jnp.float32) + self.sibling[k, chip].astype(jnp.float32)
            ).astype(jnp.bfloat16)
            return carry

        lax.fori_loop(0, 4, add, 0)
        near = 1 + self.turns[k]
        for which, bits in ((1, 3), (0, near)):
            self.send(
                self.mine(k, place.flip_chip(bits)),
                self.first.at[which, k],
                4 + 2 * k + which,
                place.near(2 * near),
            )

    def from_first(self, k):
        place = self.place
        far = 2 - self.turns[k]
        self.landed(self.first.at[1, k], 4 + 2 * k + 1)
        chip = place.flip_chip(far)
        block = self.mine(k, chip)
        block[...] = (
            block[...].astype(jnp.float32) + self.first[1, k].astype(jnp.float32)
        ).astype(jnp.bfloat16)
        self.send(block, self.second.at[k], 12 + k, place.near(2 * far))

    def from_second(self, k, total=None):
        place = self.place
        self.landed(self.first.at[0, k], 4 + 2 * k)
        self.landed(self.second.at[k], 12 + k)
        block = self.mine(k, place.chip)
        value = (
            block[...].astype(jnp.float32)
            + self.first[0, k].astype(jnp.float32)
            + self.second[k].astype(jnp.float32)
        )
        if k == 0:
            total[...] = value
        else:
            block[...] = value.astype(jnp.bfloat16)
            self.send(block, self.last.at[k], 16 + k, place.along(k))

    def from_tensor(self, total):
        value = total[...]
        for k in (1, 2, 3):
            self.landed(self.last.at[k], 16 + k)
            value = value + self.last[k].astype(jnp.float32)
        total[...] = value

    def finish(self):
        for copy in self.sent:
            copy.wait_send()


BLOCK = 128
HALF_WINDOW = 256
KV, Q, OUT, GATE, UP, DOWN = GROUPS = tuple(range(6))
TURNS = {GATE: (1, 0, 1, 0), UP: (0, 0, 1, 1)}
VMEM_BYTES = 63 * 2**20


def nn(left_side, right_side):
    return jnp.dot(left_side, right_side, preferred_element_type=jnp.float32)


def each_block(count, step, body):
    def run(i, carry):
        body(pl.multiple_of(i * step, step))
        return carry

    lax.fori_loop(0, count // step, run, 0)


def inverse_rms(values):
    return lax.rsqrt(jnp.mean(values * values, axis=-1, keepdims=True) + EPSILON)


def transposed(values):
    return values.astype(jnp.float32).T.astype(jnp.bfloat16)


def spread(block_columns, total, index):
    source = lax.broadcasted_iota(jnp.int32, (GAIN_COLUMNS, total), 0)
    target = lax.broadcasted_iota(jnp.int32, (GAIN_COLUMNS, total), 1)
    hit = (target - index * block_columns == source) & (source < block_columns)
    return jnp.where(hit, 1.0, 0.0).astype(jnp.bfloat16)


def layer_scratch(rows, width, head, ff_part, shard, parts):
    bf, f32 = jnp.bfloat16, jnp.float32
    keys = 2 * rows
    window = WINDOW + HALF_WINDOW
    blocks = rows // HALF_WINDOW
    return dict(
        normed=((rows, width), bf),
        normed_t=((width, rows), bf),
        w_keyval=((width, 2 * head), bf),
        gains=((PAD_ROWS, width), f32),
        qk_table=((PAD_ROWS, head), f32),
        gain_sums=((PAD_ROWS, width), f32),
        qk_sums=((PAD_ROWS, head), f32),
        key_raw=((rows, head), f32),
        keyval=((keys, 2 * head), bf),
        keyval_t=((2 * head, keys), bf),
        query_raw=((parts, rows, head), f32),
        queries=((parts, rows, head), bf),
        probs=((parts, blocks, window, HALF_WINDOW), bf),
        score_grad=((window, HALF_WINDOW), bf),
        context=((parts, rows, head), bf),
        attn=((rows, width), f32),
        residual=((rows, width), f32),
        ffn_in=((rows, width), bf),
        ffn_in_t=((width, rows), bf),
        gate_pre=((parts, rows, ff_part), f32),
        up_pre=((rows, ff_part), f32),
        gelu_out=((parts, rows, ff_part), bf),
        gelu_slope=((parts, rows, ff_part), bf),
        hidden=((parts, rows, ff_part), bf),
        ffn=((rows, width), f32),
        ffn_grad=((rows, width), bf),
        ffn_grad_t=((width, rows), bf),
        gate_grad=((rows, ff_part), bf),
        up_grad=((rows, ff_part), bf),
        attn_grad=((rows, width), bf),
        attn_grad_t=((width, rows), bf),
        halo_in=((rows, 2 * head), bf),
        kv_total=((shard + PAD_ROWS, GAIN_COLUMNS), f32),
        kv_shard=((shard + PAD_ROWS, GAIN_COLUMNS), bf),
        cosine=((rows, head // 2), f32),
        sine=((rows, head // 2), f32),
    )


def layer_kernel(names, *refs):
    tokens, cotangent, docs, positions, norm_gains, qk_gains, kv_weight = refs[:7]
    shards = (None,) + refs[7:12]
    block_out, tokens_grad = refs[12:14]
    totals = dict(zip(GROUPS[1:], refs[14:19]))
    shared = refs[19]
    rest = list(refs[20:])
    s = types.SimpleNamespace(**{name: rest.pop(0) for name in names})
    slots = {name: rest.pop(0) for name in GROUPS}
    rows, width = tokens.shape
    head = shards[Q].shape[1]
    ff_part = shards[GATE].shape[1]
    shard = shards[Q].shape[0]
    qk_rows = head // 8
    parts = 4
    blocks = rows // HALF_WINDOW
    window = WINDOW + HALF_WINDOW
    place = Place()

    gathers = {}
    for name, source in zip(GROUPS, (s.kv_shard,) + shards[1:]):
        gathers[name] = Gather(place, source, slots[name], *[rest.pop(0) for _ in range(3)])
    scatters = {}
    for name in GROUPS:
        own = [rest.pop(0) for _ in range(6)]
        turns = TURNS.get(name, (0, 1, 0, 1))
        scatters[name] = Scatter(place, slots[name], *own[:4], own[4:], turns)
    share_send, share_recv, halo_sems = rest

    def weight(name, k):
        return slots[name][k].reshape(width, -1)

    def put_grad(name, k, value):
        slots[name][k] = value.astype(jnp.bfloat16).reshape(4, 2, shard, -1)

    keyval_grad = s.gate_pre.at[0:2]
    bias, scores = s.gate_pre.at[0:2], s.gate_pre.at[3]

    def tile(j):
        top, left = j % 2 * HALF_WINDOW, j // 2 * HALF_WINDOW
        return slice(top, top + HALF_WINDOW), slice(left, left + HALF_WINDOW)

    query_grads = s.gelu_slope.at[:, :, 0:head]
    context_grad = s.gelu_out.at[:, :, 0:head]
    halo_out, keyval_low = s.hidden.at[0], s.hidden.at[1]

    def keyval_rows(block):
        return block // blocks, slice(
            block % blocks * HALF_WINDOW, (block % blocks + 1) * HALF_WINDOW
        )

    cosine, sine = s.cosine, s.sine
    part_at = pl.multiple_of(place.tensor * GAIN_COLUMNS, GAIN_COLUMNS)
    s.kv_shard[0:shard, :] = kv_weight[:, pl.ds(part_at, GAIN_COLUMNS)]
    s.kv_shard[shard:, :] = jnp.zeros((PAD_ROWS, GAIN_COLUMNS), jnp.bfloat16)
    s.kv_shard[shard : shard + 4, 0:shard] = norm_gains[...]
    s.kv_shard[shard + 4 : shard + 6, 0:qk_rows] = qk_gains[...]
    place.greet()
    gathers[KV].begin()
    gathers[Q].begin()
    queue = gather_order([gathers[name] for name in (KV, Q, GATE, OUT, UP, DOWN)])
    queue[0].pop(0)
    queue[1].pop(0)
    position = [0]

    def through(stage):
        while position[0] <= stage:
            while queue[position[0]]:
                queue[position[0]].pop(0)()
            position[0] += 1

    def pump(count):
        while count and position[0] < len(queue):
            if not queue[position[0]]:
                position[0] += 1
                continue
            queue[position[0]].pop(0)()
            count -= 1

    def as_column(values):
        return jnp.broadcast_to(values.astype(jnp.float32), (GAIN_COLUMNS, values.shape[1])).T

    start = pl.multiple_of(place.tensor * rows, rows)
    before = pl.multiple_of(jnp.maximum(start - rows, 0), rows)
    halo_doc = jnp.where(place.tensor > 0, docs[:, pl.ds(before, rows)], -1)
    own_doc = docs[:, pl.ds(start, rows)]
    doc_pieces = []
    for source in (halo_doc, own_doc):
        for r in range(blocks):
            piece = source[:, r * HALF_WINDOW : (r + 1) * HALF_WINDOW]
            doc_pieces.append(as_column(piece)[:, 0:1])
    for r in range(blocks):
        doc_q = own_doc[:, r * HALF_WINDOW : (r + 1) * HALF_WINDOW].astype(jnp.float32)
        for j in range(window // HALF_WINDOW):
            key_at = lax.broadcasted_iota(jnp.int32, (HALF_WINDOW, HALF_WINDOW), 0)
            query_at = lax.broadcasted_iota(jnp.int32, (HALF_WINDOW, HALF_WINDOW), 1)
            offset = query_at + rows - key_at - j * HALF_WINDOW
            allowed = (offset >= 0) & (offset < WINDOW) & (doc_q == doc_pieces[r + j])
            bias[(r,) + tile(j)] = jnp.where(allowed, 0.0, -1000000000.0)

    exponent = lax.broadcasted_iota(jnp.int32, (1, head // 2), 1).astype(jnp.float32)
    frequency = jnp.exp(exponent * (-2.0 / head * math.log(ROPE_BASE)))
    for i in range(rows // BLOCK):
        own = pl.ds(pl.multiple_of(start + i * BLOCK, BLOCK), BLOCK)
        angle = as_column(positions[:, own]) * frequency
        cosine[i * BLOCK : (i + 1) * BLOCK, :] = jnp.cos(angle)
        sine[i * BLOCK : (i + 1) * BLOCK, :] = jnp.sin(angle)

    s.gain_sums[...] = jnp.zeros_like(s.gain_sums)
    s.qk_sums[...] = jnp.zeros_like(s.qk_sums)

    @pl.when(place.tensor == 0)
    def _():
        s.keyval[0:rows, :] = jnp.zeros((rows, 2 * head), jnp.bfloat16)

    through(2)
    gathers[KV].ready()

    gain_rows = jnp.zeros((PAD_ROWS, width), jnp.float32)
    qk_part = jnp.zeros((PAD_ROWS, head), jnp.float32)
    for d in range(8):
        block = slots[KV][0, d // 2, d % 2, shard:, :]
        gain_rows += nn(block, spread(shard, width, d))
        qk_part += nn(block, spread(qk_rows, head, d))
    s.gains[...] = gain_rows
    s.qk_table[...] = qk_part
    for quarter in range(parts):
        columns = slice(quarter * GAIN_COLUMNS, (quarter + 1) * GAIN_COLUMNS)
        s.w_keyval[:, columns] = slots[KV][
            place.flip_part(quarter), :, :, 0:shard, :
        ].reshape(width, GAIN_COLUMNS)
    query_gain = s.qk_table[4:5, :]
    key_gain = s.qk_table[5:6, :]

    def norm_tokens(start):
        at = pl.ds(start, BLOCK)
        values = tokens[at, :].astype(jnp.float32)
        low = (values * inverse_rms(values) * s.gains[0:1, :]).astype(jnp.bfloat16)
        s.normed[at, :] = low
        s.normed_t[:, at] = transposed(low)

    each_block(rows, BLOCK, norm_tokens)
    pump(4)

    def make_keys(start):
        at = pl.ds(start, BLOCK)
        raw = nn(s.normed[at, :], s.w_keyval[...])
        key = raw[:, :head]
        s.key_raw[at, :] = key
        key = rotate(key * inverse_rms(key) * key_gain, cosine[at, :], sine[at, :])
        both = jnp.concatenate([key, raw[:, head:]], axis=1).astype(jnp.bfloat16)
        own = pl.ds(pl.multiple_of(rows + start, BLOCK), BLOCK)
        s.keyval[own, :] = both
        s.keyval_t[:, own] = transposed(both)

    each_block(rows, BLOCK, make_keys)

    next_part = jnp.minimum(place.tensor + 1, parts - 1)
    halo = pltpu.make_async_remote_copy(
        src_ref=s.keyval.at[pl.ds(rows, rows)],
        dst_ref=s.keyval.at[pl.ds(0, rows)],
        send_sem=halo_sems.at[0],
        recv_sem=halo_sems.at[1],
        device_id=(place.dp, next_part),
        device_id_type=MESH_ID,
    )

    @pl.when(place.tensor < parts - 1)
    def _():
        halo.start()

    through(3)
    gathers[Q].ready()
    for k in range(parts):
        s.query_raw[k] = nn(s.normed[...], weight(Q, k))

        def make_queries(start, k=k):
            at = pl.ds(start, BLOCK)
            raw = s.query_raw[k, at, :]
            low = rotate(raw * inverse_rms(raw) * query_gain, cosine[at, :], sine[at, :])
            s.queries[k, at, :] = (low * head ** (-0.5)).astype(jnp.bfloat16)

        each_block(rows, BLOCK, make_queries)
        pump(4)
    through(4)

    @pl.when(place.tensor > 0)
    def _():
        halo.wait_recv()

    def turn_halo(start):
        at = pl.ds(start, BLOCK)
        s.keyval_t[:, at] = transposed(s.keyval[at, :])

    each_block(rows, BLOCK, turn_halo)

    for k in range(parts):
        for r in range(blocks):
            at = slice(r * HALF_WINDOW, (r + 1) * HALF_WINDOW)
            query = s.queries[k, at, :]
            total = jnp.zeros((1, HALF_WINDOW), jnp.float32)
            for j in range(window // HALF_WINDOW):
                inner = slice(j * HALF_WINDOW, (j + 1) * HALF_WINDOW)
                outer = slice((r + j) * HALF_WINDOW, (r + j + 1) * HALF_WINDOW)
                score = dot_last(s.keyval[outer, :head], query) + bias[(r,) + tile(j)]
                score = jnp.exp(score)
                scores[tile(j)] = score
                total += jnp.sum(score, axis=0, keepdims=True)
            scale = 1.0 / total
            for j in range(window // HALF_WINDOW):
                inner = slice(j * HALF_WINDOW, (j + 1) * HALF_WINDOW)
                s.probs[k, r, inner, :] = (scores[tile(j)] * scale).astype(jnp.bfloat16)
            mixed = nn(
                s.keyval_t[head:, r * HALF_WINDOW : r * HALF_WINDOW + window], s.probs[k, r]
            )
            s.context[k, at, :] = mixed.T.astype(jnp.bfloat16)
            pump(3)

    through(5)
    gathers[OUT].ready()
    for k in range(parts):
        share = dot_last(s.context[k], weight(OUT, k))
        if k == 0:
            s.attn[...] = share
        else:
            s.attn[...] += share
    pump(3)

    def norm_attn(start):
        at = pl.ds(start, BLOCK)
        attn = s.attn[at, :]
        residual = tokens[at, :].astype(jnp.float32) + attn * inverse_rms(attn) * s.gains[1:2, :]
        s.residual[at, :] = residual
        low = (residual * inverse_rms(residual) * s.gains[2:3, :]).astype(jnp.bfloat16)
        s.ffn_in[at, :] = low
        s.ffn_in_t[:, at] = transposed(low)

    each_block(rows, BLOCK, norm_attn)
    gathers[GATE].ready()
    for k in range(parts):
        s.gate_pre[k] = nn(s.ffn_in[...], weight(GATE, k))
        pump(2)
    through(6)
    gathers[UP].ready()
    for k in range(parts):
        s.up_pre[...] = nn(s.ffn_in[...], weight(UP, k))

        def activate(start, k=k):
            at = pl.ds(start, 32)
            gate = s.gate_pre[k, at, :]
            up = s.up_pre[at, :]
            square = gate * gate
            tanh = jnp.tanh(GELU_SCALE * gate * (1.0 + 0.044715 * square))
            upper = 0.5 * (1.0 + tanh)
            gelu = gate * upper
            slope = upper + (
                0.5 * GELU_SCALE * gate * (1.0 - tanh * tanh) * (1.0 + 3 * 0.044715 * square)
            )
            s.gelu_out[k, at, :] = gelu.astype(jnp.bfloat16)
            s.gelu_slope[k, at, :] = (slope * up).astype(jnp.bfloat16)
            s.hidden[k, at, :] = (gelu * up).astype(jnp.bfloat16)

        each_block(rows, 32, activate)
        pump(2)
    through(7)
    gathers[DOWN].ready()
    for k in range(parts):
        share = dot_last(s.hidden[k], weight(DOWN, k))
        if k == 0:
            s.ffn[...] = share
        else:
            s.ffn[...] += share
    for name in GROUPS:
        gathers[name].finish()

    def top_block(start):
        at = pl.ds(start, BLOCK)
        ffn = s.ffn[at, :]
        gain = s.gains[3:4, :]
        top = cotangent[at, :].astype(jnp.float32)
        inverse = inverse_rms(ffn)
        block_out[at, :] = (s.residual[at, :] + ffn * inverse * gain).astype(jnp.bfloat16)
        grad, gain_rows = norm_back(ffn, gain, top)
        s.gain_sums[3:4, :] += jnp.sum(gain_rows, axis=0, keepdims=True)
        low = grad.astype(jnp.bfloat16)
        s.ffn_grad[at, :] = low
        s.ffn_grad_t[:, at] = transposed(low)

    each_block(rows, BLOCK, top_block)

    ffn_groups = (DOWN, GATE, UP)
    order = (3, 2, 1, 0)

    def for_ffn(step, k):
        for name in ffn_groups:
            scatter = scatters[name]
            if step is Scatter.from_second:
                step(scatter, k, totals[name])
            else:
                step(scatter, k)

    for i, k in enumerate(order):
        s.up_pre[...] = nn(s.ffn_grad[...], weight(DOWN, k))

        def activate_back(start, k=k):
            at = pl.ds(start, 32)
            grad = s.up_pre[at, :]
            s.gate_grad[at, :] = (
                grad * s.gelu_slope[k, at, :].astype(jnp.float32)
            ).astype(jnp.bfloat16)
            s.up_grad[at, :] = (
                grad * s.gelu_out[k, at, :].astype(jnp.float32)
            ).astype(jnp.bfloat16)

        each_block(rows, 32, activate_back)
        share = dot_last(s.gate_grad[...], weight(GATE, k))
        share += dot_last(s.up_grad[...], weight(UP, k))
        if i == 0:
            s.ffn[...] = share
        else:
            s.ffn[...] += share
        put_grad(DOWN, k, nn(s.ffn_grad_t[...], s.hidden[k]))
        scatters[DOWN].to_sibling(k)
        put_grad(GATE, k, nn(s.ffn_in_t[...], s.gate_grad[...]))
        scatters[GATE].to_sibling(k)
        if i >= 1:
            scatters[UP].from_sibling(order[i - 1])
        put_grad(UP, k, nn(s.ffn_in_t[...], s.up_grad[...]))
        scatters[UP].to_sibling(k)
        scatters[DOWN].from_sibling(k)
        scatters[GATE].from_sibling(k)

    def middle_block(start):
        at = pl.ds(start, BLOCK)
        residual = s.residual[at, :]
        attn = s.attn[at, :]
        part, gain_rows = norm_back(residual, s.gains[2:3, :], s.ffn[at, :])
        s.gain_sums[2:3, :] += jnp.sum(gain_rows, axis=0, keepdims=True)
        residual_grad = cotangent[at, :].astype(jnp.float32) + part
        s.residual[at, :] = residual_grad
        grad, gain_rows = norm_back(attn, s.gains[1:2, :], residual_grad)
        s.gain_sums[1:2, :] += jnp.sum(gain_rows, axis=0, keepdims=True)
        low = grad.astype(jnp.bfloat16)
        s.attn_grad[at, :] = low
        s.attn_grad_t[:, at] = transposed(low)

    each_block(rows, BLOCK, middle_block)
    keyval_grad[...] = jnp.zeros(keyval_grad.shape, jnp.float32)
    scatters[UP].from_sibling(0)

    for k in range(parts):
        context_grad[k] = nn(s.attn_grad[...], weight(OUT, k)).astype(jnp.bfloat16)
        put_grad(OUT, k, nn(s.attn_grad_t[...], s.context[k]))
        scatters[OUT].to_sibling(k)

    def for_all(step, name):
        for k in order:
            if step is Scatter.from_second:
                step(scatters[name], k, totals[name])
            else:
                step(scatters[name], k)

    later = {
        1: lambda: for_all(Scatter.from_sibling, OUT),
        3: lambda: for_ffn(Scatter.from_first, 3),
        5: lambda: for_ffn(Scatter.from_first, 2),
        7: lambda: for_ffn(Scatter.from_first, 1),
    }
    last_part = jnp.maximum(place.tensor - 1, 0)
    half = rows // blocks
    halo_back = []
    for r in range(blocks):
        halo_back.append(
            pltpu.make_async_remote_copy(
                src_ref=halo_out.at[pl.ds(r * half, half)],
                dst_ref=s.halo_in.at[pl.ds(r * half, half)],
                send_sem=halo_sems.at[2 + r],
                recv_sem=halo_sems.at[4 + r],
                device_id=(place.dp, last_part),
                device_id_type=MESH_ID,
            )
        )

    @pl.when(place.tensor == parts - 1)
    def _():
        s.halo_in[...] = jnp.zeros_like(s.halo_in)

    for r in range(blocks):
        for k in range(parts):
            at = slice(r * HALF_WINDOW, (r + 1) * HALF_WINDOW)
            query = s.queries[k, at, :]
            grad = context_grad[k, at, :]
            delta = jnp.zeros((1, HALF_WINDOW), jnp.float32)
            for j in range(window // HALF_WINDOW):
                inner = slice(j * HALF_WINDOW, (j + 1) * HALF_WINDOW)
                outer = slice((r + j) * HALF_WINDOW, (r + j + 1) * HALF_WINDOW)
                prob_grad = dot_last(s.keyval[outer, head:], grad)
                scores[tile(j)] = prob_grad
                probs = s.probs[k, r, inner, :].astype(jnp.float32)
                delta += jnp.sum(probs * prob_grad, axis=0, keepdims=True)
            for j in range(window // HALF_WINDOW):
                inner = slice(j * HALF_WINDOW, (j + 1) * HALF_WINDOW)
                outer = slice((r + j) * HALF_WINDOW, (r + j + 1) * HALF_WINDOW)
                probs = s.probs[k, r, inner, :]
                score_grad = probs.astype(jnp.float32) * (scores[tile(j)] - delta)
                score_grad = score_grad.astype(jnp.bfloat16)
                s.score_grad[inner, :] = score_grad
                which, outer = keyval_rows(r + j)
                keyval_grad[which, outer, :head] += nn(score_grad, query)
                keyval_grad[which, outer, head:] += nn(probs, grad)
            turned = nn(
                s.keyval_t[:head, r * HALF_WINDOW : r * HALF_WINDOW + window],
                s.score_grad[...],
            )
            query_grad = turned.T * head ** (-0.5)
            query_grad = rotate(query_grad, cosine[at, :], -sine[at, :])
            raw_grad, gain_rows = norm_back(s.query_raw[k, at, :], query_gain, query_grad)
            s.qk_sums[4:5, :] += jnp.sum(gain_rows, axis=0, keepdims=True)
            query_grads[k, at, :] = raw_grad.astype(jnp.bfloat16)
            later.get(r * parts + k, lambda: None)()
        at = slice(r * half, (r + 1) * half)
        halo_out[at, :] = keyval_grad[0, at, :].astype(jnp.bfloat16)

        @pl.when(place.tensor > 0)
        def _(r=r):
            halo_back[r].start()

    for k in range(parts):
        share = dot_last(query_grads[k], weight(Q, k))
        if k == 0:
            s.ffn[...] = share
        else:
            s.ffn[...] += share
        put_grad(Q, k, nn(s.normed_t[...], query_grads[k]))
        scatters[Q].to_sibling(k)
    for_all(Scatter.from_sibling, Q)
    for_ffn(Scatter.from_first, 0)
    for_all(Scatter.from_first, OUT)
    for_ffn(Scatter.from_second, 3)

    @pl.when(place.tensor < parts - 1)
    def _():
        for copy in halo_back:
            copy.wait_recv()

    def key_block(start):
        at = pl.ds(start, BLOCK)
        grads = keyval_grad[1, at, :] + s.halo_in[at, :].astype(jnp.float32)
        key_grad = rotate(grads[:, :head], cosine[at, :], -sine[at, :])
        raw_grad, gain_rows = norm_back(s.key_raw[at, :], key_gain, key_grad)
        s.qk_sums[5:6, :] += jnp.sum(gain_rows, axis=0, keepdims=True)
        keyval_low[at, :] = jnp.concatenate([raw_grad, grads[:, head:]], axis=1).astype(
            jnp.bfloat16
        )

    each_block(rows, BLOCK, key_block)
    s.ffn[...] += dot_last(keyval_low[...], s.w_keyval[...])

    def bottom_block(start):
        at = pl.ds(start, BLOCK)
        values = tokens[at, :].astype(jnp.float32)
        part, gain_rows = norm_back(values, s.gains[0:1, :], s.ffn[at, :])
        s.gain_sums[0:1, :] += jnp.sum(gain_rows, axis=0, keepdims=True)
        tokens_grad[at, :] = s.residual[at, :] + part

    each_block(rows, BLOCK, bottom_block)
    for quarter in range(parts):
        columns = slice(quarter * GAIN_COLUMNS, (quarter + 1) * GAIN_COLUMNS)
        value = nn(s.normed_t[...], keyval_low[:, columns])
        slots[KV][place.flip_part(quarter), :, :, 0:shard, :] = value.astype(
            jnp.bfloat16
        ).reshape(4, 2, shard, GAIN_COLUMNS)
    gain_low = s.gain_sums[...].astype(jnp.bfloat16)
    qk_low = s.qk_sums[...].astype(jnp.bfloat16)
    for d in range(8):
        block = dot_last(gain_low, spread(shard, width, d))
        block += dot_last(qk_low, spread(qk_rows, head, d))
        for k in range(parts):
            slots[KV][k, d // 2, d % 2, shard:, :] = block.astype(jnp.bfloat16)
    for k in range(parts):
        scatters[KV].to_sibling(k)
    for_all(Scatter.from_sibling, KV)
    for_ffn(Scatter.from_second, 2)
    for_all(Scatter.from_first, Q)
    for_ffn(Scatter.from_second, 1)
    for_all(Scatter.from_second, OUT)
    for_ffn(Scatter.from_second, 0)
    for_all(Scatter.from_first, KV)
    for_all(Scatter.from_second, Q)
    for name in ffn_groups:
        scatters[name].from_tensor(totals[name])
    for k in order:
        scatters[KV].from_second(k, s.kv_total)
    scatters[KV].from_tensor(s.kv_total)
    shared[0] = s.kv_total[...]
    copies = []
    for k in (1, 2, 3):
        copies.append(
            pltpu.make_async_remote_copy(
                src_ref=s.kv_total,
                dst_ref=shared.at[k],
                send_sem=share_send.at[k],
                recv_sem=share_recv.at[k],
                device_id=place.along(k),
                device_id_type=MESH_ID,
            )
        )
    for copy in copies:
        copy.start()
    for name in (OUT, Q):
        scatters[name].from_tensor(totals[name])
    for copy in copies:
        copy.wait()
    for name in GROUPS:
        scatters[name].finish()

    @pl.when(place.tensor < parts - 1)
    def _():
        halo.wait_send()

    @pl.when(place.tensor > 0)
    def _():
        for copy in halo_back:
            copy.wait_send()


def finish_kernel(count, *refs):
    sources, shared = refs[:count], refs[count]
    targets, keyval, norm_gains, qk_gains = (refs[count + 1 : 2 * count + 1],) + refs[
        2 * count + 1 : 2 * count + 4
    ]
    sems = refs[2 * count + 4]
    copies = [
        pltpu.make_async_copy(source, target, sems.at[i])
        for i, (source, target) in enumerate(zip(sources, targets))
    ]
    for copy in copies:
        copy.start()
    place = Place()
    shard, qk_rows = norm_gains.shape[1], qk_gains.shape[1]
    for part in range(4):
        columns = slice(part * GAIN_COLUMNS, (part + 1) * GAIN_COLUMNS)
        keyval[:, columns] = shared[place.flip_part(part), 0:shard, :]
    norm_gains[...] = shared[0, shard : shard + 4, 0:shard]
    qk_gains[...] = shared[0, shard + 4 : shard + 6, 0:qk_rows]
    for copy in copies:
        copy.wait()


def per_device_direct(
    tokens,
    segments,
    positions,
    norm_gains,
    qk_gains,
    q_weight,
    kv_weight,
    out_weight,
    gate_weight,
    up_weight,
    down_weight,
    cotangent,
):
    parts = lax.axis_size("tensor")
    rows, width = tokens.shape
    shard = q_weight.shape[0]
    head = q_weight.shape[1]
    ff_part = gate_weight.shape[1]
    arguments = [
        tokens,
        cotangent,
        segments[None, :],
        positions[None, :],
        norm_gains,
        qk_gains,
        kv_weight,
        q_weight,
        out_weight.T,
        gate_weight,
        up_weight,
        down_weight.T,
    ]
    kv_shape = (shard + PAD_ROWS, GAIN_COLUMNS)
    shapes = [kv_shape] + [w.shape for w in arguments[7:]]
    buffers = layer_scratch(rows, width, head, ff_part, shard, parts)
    scratch = [pltpu.VMEM(*buffer) for buffer in buffers.values()]
    scratch += [pltpu.VMEM((4, 4, 2) + shape, jnp.bfloat16) for shape in shapes]
    scratch += Gather.scratch() * len(shapes)
    for shape in shapes:
        scratch += Scatter.scratch(*shape)
    scratch += [pltpu.SemaphoreType.DMA((4,))] * 2 + [pltpu.SemaphoreType.DMA((6,))]
    f32 = jnp.float32
    whole = pl.BlockSpec(memory_space=pltpu.VMEM)
    anywhere = pl.BlockSpec(memory_space=pl.ANY)
    kinds = [
        jax.ShapeDtypeStruct((rows, width), jnp.bfloat16),
        jax.ShapeDtypeStruct((rows, width), f32),
    ] + [jax.ShapeDtypeStruct(shape, f32) for shape in shapes[1:]]
    results = pl.pallas_call(
        functools.partial(layer_kernel, list(buffers)),
        out_shape=kinds + [jax.ShapeDtypeStruct((parts,) + kv_shape, f32)],
        in_specs=[whole] * len(arguments),
        out_specs=[whole] * 8,
        scratch_shapes=scratch,
        compiler_params=pltpu.CompilerParams(
            collective_id=0, has_side_effects=True, vmem_limit_bytes=VMEM_BYTES
        ),
        name="layer",
    )(*arguments)
    results = pl.pallas_call(
        functools.partial(finish_kernel, len(kinds)),
        out_shape=kinds
        + [
            jax.ShapeDtypeStruct(kv_weight.shape, f32),
            jax.ShapeDtypeStruct(norm_gains.shape, f32),
            jax.ShapeDtypeStruct(qk_gains.shape, f32),
        ],
        in_specs=[whole] * (len(kinds) + 1),
        out_specs=[anywhere] * len(kinds) + [whole] * 3,
        scratch_shapes=[pltpu.SemaphoreType.DMA((len(kinds),))],
        name="finish",
    )(*results)
    block_out, tokens_grad, q_sum, out_sum, gate_sum, up_sum, down_sum = results[:7]
    keyval, norm_sum, qk_sum = results[7:]
    return (
        block_out,
        tokens_grad,
        norm_sum,
        qk_sum,
        q_sum,
        keyval,
        out_sum.T,
        gate_sum,
        up_sum,
        down_sum.T,
    )


def pack_shards(norm_gains, qk_gains, q_weight, kv_weight, out_weight, gate_weight, up_weight, down_weight):
    rows = q_weight.shape[0]
    kv_columns = kv_weight.shape[1] // lax.axis_size("tensor")
    kv_part = lax.dynamic_slice_in_dim(
        kv_weight, lax.axis_index("tensor") * kv_columns, kv_columns, axis=1
    )
    gain_part = jnp.concatenate(
        [
            norm_gains.T,
            jnp.pad(qk_gains.T, ((0, rows - qk_gains.shape[1]), (0, 0))),
            jnp.zeros((rows, GAIN_COLUMNS - 6), jnp.bfloat16),
        ],
        axis=1,
    )
    return jnp.concatenate(
        [q_weight, out_weight.T, gate_weight, up_weight, down_weight.T, kv_part, gain_part],
        axis=1,
    )


def gather_weights(packed):
    return lax.all_gather(packed, ("tensor", "dp"), axis=0, tiled=True)


def reduce_grads(grads):
    return lax.psum_scatter(
        grads, ("tensor", "dp"), scatter_dimension=0, tiled=True
    ).astype(jnp.float32)


def per_device(
    tokens,
    segments,
    positions,
    norm_gains,
    qk_gains,
    q_weight,
    kv_weight,
    out_weight,
    gate_weight,
    up_weight,
    down_weight,
    cotangent,
):
    parts = lax.axis_size("tensor")
    place = lax.axis_index("tensor")
    rows, width = tokens.shape
    shard_rows = q_weight.shape[0]
    head_width = q_weight.shape[1]
    ff_part = gate_weight.shape[1]
    kv_columns = kv_weight.shape[1]
    kv_part = kv_columns // parts
    qk_rows = qk_gains.shape[1]
    ends = [0]
    for columns in (head_width, head_width, ff_part, ff_part, ff_part, kv_part, GAIN_COLUMNS):
        ends.append(ends[-1] + columns)

    packed = pack_shards(
        norm_gains, qk_gains, q_weight, kv_weight, out_weight, gate_weight, up_weight, down_weight
    )
    gathered = gather_weights(packed).reshape(parts, width, ends[-1])
    halo = lax.ppermute(tokens, "tensor", [(i, i + 1) for i in range(parts - 1)])

    def piece(index):
        return [gathered[t, :, ends[index] : ends[index + 1]] for t in range(parts)]

    w_query, w_out, w_gate, w_up, w_down, w_kv = (piece(i) for i in range(6))
    w_keyval = jnp.concatenate(w_kv, axis=1)
    w_gains = gathered[0, :, ends[6] : ends[7]].astype(jnp.float32)
    gain_table = w_gains[:, :4].T
    qk_table = w_gains.reshape(-1, shard_rows, GAIN_COLUMNS)[:, :qk_rows, 4:6]
    qk_table = qk_table.reshape(head_width, 2).T

    own_input = tokens.astype(jnp.float32)
    both_input = jnp.concatenate([halo, tokens], axis=0).astype(jnp.float32)
    normed_both = norm_rows(both_input, gain_table[0]).astype(jnp.bfloat16)
    normed = normed_both[rows:]
    start = place * rows
    first = jnp.maximum(start - rows, 0)
    own_doc = lax.dynamic_slice_in_dim(segments, start, rows)
    halo_doc = jnp.where(place > 0, lax.dynamic_slice_in_dim(segments, first, rows), -1)
    both_doc = jnp.concatenate([halo_doc, own_doc])
    both_place = jnp.concatenate(
        [
            lax.dynamic_slice_in_dim(positions, first, rows),
            lax.dynamic_slice_in_dim(positions, start, rows),
        ]
    )
    half_width = head_width // 2
    frequency = ROPE_BASE ** (-jnp.arange(half_width, dtype=jnp.float32) * 2.0 / head_width)
    angles = both_place.astype(jnp.float32)[:, None] * frequency[None, :]
    cosine_both = jnp.cos(angles)
    sine_both = jnp.sin(angles)
    cosine_own, sine_own = cosine_both[rows:], sine_both[rows:]

    offsets = jnp.arange(rows)[:, None] + rows - jnp.arange(2 * rows)[None, :]
    allowed = (offsets >= 0) & (offsets < WINDOW) & (own_doc[:, None] == both_doc[None, :])
    score_scale = head_width ** (-0.5)

    keyval_raw = dot_plain(normed_both, w_keyval)
    key_raw = keyval_raw[:, :head_width]
    keys = rotate(norm_rows(key_raw, qk_table[1]), cosine_both, sine_both).astype(jnp.bfloat16)
    value_rows = keyval_raw[:, head_width:].astype(jnp.bfloat16)

    query_raw, queries, lse, context = [], [], [], []
    attn_own = None
    for t in range(parts):
        raw = dot_plain(normed, w_query[t])
        low = rotate(norm_rows(raw, qk_table[0]), cosine_own, sine_own).astype(jnp.bfloat16)
        masked = jnp.where(allowed, dot_last(low, keys) * score_scale, -1000000000.0)
        row_max = jnp.max(masked, axis=1, keepdims=True)
        exponent = jnp.exp(masked - row_max)
        row_total = jnp.sum(exponent, axis=1, keepdims=True)
        probabilities = (exponent / row_total).astype(jnp.bfloat16)
        mixed = dot_plain(probabilities, value_rows).astype(jnp.bfloat16)
        query_raw.append(raw)
        queries.append(low)
        lse.append(row_max + jnp.log(row_total))
        context.append(mixed)
        share = dot_last(mixed, w_out[t])
        attn_own = share if attn_own is None else attn_own + share

    residual = own_input + norm_rows(attn_own, gain_table[1])
    ffn_in = norm_rows(residual, gain_table[2]).astype(jnp.bfloat16)
    gate_pre, up_pre, hidden = [], [], []
    ffn_out = None
    for t in range(parts):
        gate_pre.append(dot_plain(ffn_in, w_gate[t]))
        up_pre.append(dot_plain(ffn_in, w_up[t]))
        hidden.append(geglu(gate_pre[t], up_pre[t]).astype(jnp.bfloat16))
        share = dot_last(hidden[t], w_down[t])
        ffn_out = share if ffn_out is None else ffn_out + share
    block_out = (residual + norm_rows(ffn_out, gain_table[3])).astype(jnp.bfloat16)
    top_grad = cotangent.astype(jnp.float32)
    ffn_grad_value, post_gain_rows = norm_back(ffn_out, gain_table[3], top_grad)
    ffn_grad = ffn_grad_value.astype(jnp.bfloat16)
    ffn_in_grad = None
    grads = [[] for _ in range(parts)]
    down_wgrad, gate_wgrad, up_wgrad = [], [], []
    for t in range(parts):
        hidden_grad = dot_plain(ffn_grad, w_down[t])
        gelu_back = jax.vjp(geglu, gate_pre[t], up_pre[t])[1]
        gate_grad_value, up_grad_value = gelu_back(hidden_grad)
        gate_grad = gate_grad_value.astype(jnp.bfloat16)
        up_grad = up_grad_value.astype(jnp.bfloat16)
        share = dot_last(gate_grad, w_gate[t]) + dot_last(up_grad, w_up[t])
        ffn_in_grad = share if ffn_in_grad is None else ffn_in_grad + share
        gate_wgrad.append(dot_first(ffn_in, gate_grad))
        up_wgrad.append(dot_first(ffn_in, up_grad))
        down_wgrad.append(dot_first(ffn_grad, hidden[t]))
    residual_part, pre_ffn_rows = norm_back(residual, gain_table[2], ffn_in_grad)
    residual_grad = top_grad + residual_part
    attn_grad_value, post_attn_rows = norm_back(attn_own, gain_table[1], residual_grad)
    attn_grad = attn_grad_value.astype(jnp.bfloat16)

    key_grad, value_grad, normed_grad = None, None, None
    query_gain_grad = None
    out_wgrad, query_wgrad = [], []
    for t in range(parts):
        context_grad = dot_plain(attn_grad, w_out[t]).astype(jnp.bfloat16)
        out_wgrad.append(dot_first(attn_grad, context[t]))
        masked = jnp.where(allowed, dot_last(queries[t], keys) * score_scale, -1000000000.0)
        probabilities = jnp.exp(masked - lse[t])
        prob_grad = dot_last(context_grad, value_rows)
        row_delta = jnp.sum(probabilities * prob_grad, axis=1, keepdims=True)
        score_grad = (probabilities * (prob_grad - row_delta) * score_scale).astype(jnp.bfloat16)
        query_grad = dot_plain(score_grad, keys)
        key_share = dot_first(score_grad, queries[t])
        value_share = dot_first(probabilities.astype(jnp.bfloat16), context_grad)
        key_grad = key_share if key_grad is None else key_grad + key_share
        value_grad = value_share if value_grad is None else value_grad + value_share
        unrotated = rotate(query_grad, cosine_own, -sine_own)
        raw_grad, gain_rows = norm_back(query_raw[t], qk_table[0], unrotated)
        gain_share = jnp.sum(gain_rows, axis=0)
        query_gain_grad = gain_share if query_gain_grad is None else query_gain_grad + gain_share
        raw_low = raw_grad.astype(jnp.bfloat16)
        share = dot_last(raw_low, w_query[t])
        normed_grad = share if normed_grad is None else normed_grad + share
        query_wgrad.append(dot_first(normed, raw_low))
    key_raw_grad, key_gain_rows = norm_back(
        key_raw, qk_table[1], rotate(key_grad, cosine_both, -sine_both)
    )
    keyval_low = jnp.concatenate([key_raw_grad, value_grad], axis=1).astype(jnp.bfloat16)
    next_part = lax.ppermute(
        keyval_low[:rows], "tensor", [(i + 1, i) for i in range(parts - 1)]
    )
    keyval_wgrad = dot_first(normed_both, keyval_low)
    keyval_own = (keyval_low[rows:].astype(jnp.float32) + next_part.astype(jnp.float32)).astype(
        jnp.bfloat16
    )
    normed_grad = normed_grad + dot_last(keyval_own, w_keyval)
    input_part, pre_attn_rows = norm_back(own_input, gain_table[0], normed_grad)
    tokens_grad = residual_grad + input_part

    gain_grads = jnp.stack(
        [
            jnp.sum(pre_attn_rows, axis=0),
            jnp.sum(post_attn_rows, axis=0),
            jnp.sum(pre_ffn_rows, axis=0),
            jnp.sum(post_gain_rows, axis=0),
        ],
        axis=1,
    )
    qk_grads = jnp.stack([query_gain_grad, jnp.sum(key_gain_rows, axis=0)], axis=1)
    qk_grads = jnp.pad(
        qk_grads.reshape(-1, qk_rows, 2), ((0, 0), (0, shard_rows - qk_rows), (0, 0))
    ).reshape(width, 2)
    gain_columns = jnp.concatenate(
        [gain_grads, qk_grads, jnp.zeros((width, GAIN_COLUMNS - 6), jnp.float32)], axis=1
    )
    blocks = []
    for t in range(parts):
        blocks.append(
            jnp.concatenate(
                [
                    value.astype(jnp.bfloat16)
                    for value in (
                        query_wgrad[t],
                        out_wgrad[t],
                        gate_wgrad[t],
                        up_wgrad[t],
                        down_wgrad[t],
                        keyval_wgrad[:, t * kv_part : (t + 1) * kv_part],
                        gain_columns if t == 0 else jnp.zeros_like(gain_columns),
                    )
                ],
                axis=1,
            )
        )
    reduced = reduce_grads(jnp.concatenate(blocks, axis=0))
    shared = lax.all_gather(reduced[:, ends[5] :], "tensor", axis=0)
    keyval_out = jnp.concatenate([shared[t, :, :kv_part] for t in range(parts)], axis=1)
    gain_out = shared[0, :, kv_part:]
    cut = [reduced[:, ends[i] : ends[i + 1]] for i in range(5)]
    return (
        block_out,
        tokens_grad,
        gain_out[:, :4].T,
        gain_out[:qk_rows, 4:6].T,
        cut[0],
        keyval_out,
        cut[1].T,
        cut[2],
        cut[3],
        cut[4].T,
    )


def solution(mesh):
    direct = mesh.shape["dp"] == 8 and mesh.shape["tensor"] == 4
    return jax.shard_map(
        per_device_direct if direct else per_device,
        mesh=mesh,
        in_specs=(
            P(("dp", "tensor"), None),
            P("dp"),
            P("dp"),
            P(None, "dp"),
            P(None, "dp"),
            P("dp", "tensor"),
            P("dp", None),
            P("tensor", "dp"),
            P("dp", "tensor"),
            P("dp", "tensor"),
            P("tensor", "dp"),
            P(("dp", "tensor"), None),
        ),
        out_specs=(
            P(("dp", "tensor"), None),
            P(("dp", "tensor"), None),
            P(None, "dp"),
            P(None, "dp"),
            P("dp", "tensor"),
            P("dp", None),
            P("tensor", "dp"),
            P("dp", "tensor"),
            P("dp", "tensor"),
            P("tensor", "dp"),
        ),
        check_vma=False,
    )
```

```python
import functools
import math
import types

import jax
import jax.numpy as jnp
from jax import lax
from jax.experimental import pallas as pl
from jax.experimental.pallas import tpu as pltpu
from jax.sharding import PartitionSpec as P

WINDOW = 512
GAIN_COLUMNS = 128


EPSILON = 1e-06
ROPE_BASE = 10000.0
GELU_SCALE = 0.7978845608028654


def norm_rows(values, gain_row):
    return (
        values * lax.rsqrt(jnp.mean(values * values, axis=-1, keepdims=True) + EPSILON) * gain_row
    )


def norm_back(values, gain_row, grad_out):
    inv_rms = lax.rsqrt(jnp.mean(values * values, axis=-1, keepdims=True) + EPSILON)
    weighted = grad_out * gain_row
    inner_mean = jnp.mean(values * weighted, axis=-1, keepdims=True)
    return (
        inv_rms * weighted - values * inv_rms * inv_rms * inv_rms * inner_mean,
        grad_out * values * inv_rms,
    )


def rotate(values, cosine_table, sine_table):
    half_width = values.shape[-1] // 2
    first_half = values[..., :half_width]
    second_half = values[..., half_width:]
    return jnp.concatenate(
        [
            first_half * cosine_table - second_half * sine_table,
            second_half * cosine_table + first_half * sine_table,
        ],
        axis=-1,
    )


def geglu(gate_pre, up_pre):
    inner_term = GELU_SCALE * (gate_pre + 0.044715 * gate_pre * gate_pre * gate_pre)
    return 0.5 * gate_pre * (1.0 + jnp.tanh(inner_term)) * up_pre


def dot_plain(left_side, right_side):
    return jnp.dot(left_side, right_side, preferred_element_type=jnp.float32)


def dot_last(left_side, right_side):
    return lax.dot_general(
        left_side, right_side, (((1,), (1,)), ((), ())), preferred_element_type=jnp.float32
    )


def dot_first(left_side, right_side):
    return lax.dot_general(
        left_side, right_side, (((0,), (0,)), ((), ())), preferred_element_type=jnp.float32
    )


MESH_ID = pl.DeviceIdType.MESH
PAD_ROWS = 16


class Place:
    def __init__(self):
        self.dp = lax.axis_index("dp")
        self.tensor = lax.axis_index("tensor")
        self.core = lax.rem(self.dp, 2)
        self.chip = self.dp // 2

    def flip_dp(self, bits):
        flipped = self.dp
        for bit in (1, 2, 4):
            if bits & bit:
                flipped = flipped + bit - 2 * bit * lax.rem(self.dp // bit, 2)
        return flipped

    def flip_chip(self, bits):
        return self.flip_dp(2 * bits) // 2

    def flip_tensor(self, bits):
        flipped = self.tensor
        for bit in (1, 2):
            if bits & bit:
                flipped = flipped + bit - 2 * bit * lax.rem(self.tensor // bit, 2)
        return flipped

    def flip_part(self, part):
        return self.flip_tensor(part)

    def near(self, bits):
        return (self.flip_dp(bits), self.tensor)

    def along(self, bits):
        return (self.dp, self.flip_tensor(bits))

    def greet(self):
        partners = [self.near(1), self.near(2), self.near(4)] + [self.along(k) for k in (1, 2, 3)]
        barrier = pltpu.get_barrier_semaphore()
        for partner in partners:
            pl.semaphore_signal(barrier, inc=1, device_id=partner, device_id_type=MESH_ID)
        pl.semaphore_wait(barrier, len(partners))


class Gather:
    SENDS = 32

    def __init__(self, place, shard, slots, send_sem, recv_sem, local_sem):
        self.place, self.shard, self.slots = place, shard, slots
        self.send_sem, self.recv_sem, self.local_sem = send_sem, recv_sem, local_sem
        self.sent = []

    @staticmethod
    def scratch():
        return [
            pltpu.SemaphoreType.DMA((Gather.SENDS,)),
            pltpu.SemaphoreType.DMA((32,)),
            pltpu.SemaphoreType.DMA,
        ]

    def send(self, source, slot, dp, device, lane):
        copy = pltpu.make_async_remote_copy(
            src_ref=source,
            dst_ref=self.slots.at[slot, dp // 2, lax.rem(dp, 2)],
            send_sem=self.send_sem.at[len(self.sent)],
            recv_sem=self.recv_sem.at[slot * 8 + lane],
            device_id=device,
            device_id_type=MESH_ID,
        )
        copy.start()
        self.sent.append(copy)

    def landed(self, slot, bits):
        place = self.place
        dp = place.flip_dp(bits)
        block = self.slots.at[slot, dp // 2, lax.rem(dp, 2)]
        pltpu.make_async_remote_copy(
            src_ref=block,
            dst_ref=block,
            send_sem=self.send_sem.at[0],
            recv_sem=self.recv_sem.at[slot * 8 + bits],
            device_id=place.near(1),
            device_id_type=MESH_ID,
        ).wait_recv()
        return block, dp

    def begin(self):
        place = self.place
        self.local = pltpu.make_async_copy(
            self.shard, self.slots.at[0, place.chip, place.core], self.local_sem
        )
        self.local.start()
        for k in (1, 2, 3):
            self.send(self.shard, k, place.dp, place.along(k), 0)
        for bits in (2, 4, 1):
            self.send(self.shard, 0, place.dp, place.near(bits), bits)

    def from_tensor(self, k):
        block, dp = self.landed(k, 0)
        for bits in (2, 4, 1):
            self.send(block, k, dp, self.place.near(bits), bits)

    def from_first(self, k):
        bits, other = (2, 4) if k % 2 == 0 else (4, 2)
        block, dp = self.landed(k, bits)
        self.send(block, k, dp, self.place.near(other), 6)
        self.send(block, k, dp, self.place.near(1), bits + 1)

    def from_second(self, k):
        block, dp = self.landed(k, 4 if k % 2 == 0 else 2)
        self.send(block, k, dp, self.place.near(1), (4 if k % 2 == 0 else 2) + 1)

    def from_corner(self, k):
        block, dp = self.landed(k, 6)
        self.send(block, k, dp, self.place.near(1), 7)

    def ready(self):
        self.local.wait()
        for k in range(4):
            for bits in (1, 3, 5, 7):
                self.landed(k, bits)

    def finish(self):
        for copy in self.sent:
            copy.wait_send()


def gather_order(gathers):
    count = len(gathers)
    stages = []
    for i in range(count + 2):
        lanes = [[], [], []]
        if i < count:
            lanes[0] = [gathers[i].begin] + [
                functools.partial(gathers[i].from_tensor, k) for k in (1, 2, 3)
            ]
        if 0 <= i - 1 < count:
            lanes[1] = [functools.partial(gathers[i - 1].from_first, k) for k in range(4)]
        if 0 <= i - 2 < count:
            for k in range(4):
                lanes[2].append(functools.partial(gathers[i - 2].from_second, k))
                lanes[2].append(functools.partial(gathers[i - 2].from_corner, k))
        stage = []
        while any(lanes):
            for lane, share in zip(lanes, (1, 1, 2)):
                for _ in range(share):
                    if lane:
                        stage.append(lane.pop(0))
        stages.append(stage)
    return stages


class Scatter:
    def __init__(self, place, grads, sibling, first, second, last, sems, turns):
        self.place, self.grads, self.sibling = place, grads, sibling
        self.first, self.second, self.last = first, second, last
        self.send_sem, self.recv_sem = sems
        self.turns = turns
        self.sent = []

    @staticmethod
    def scratch(rows, columns):
        block = (rows, columns)
        return [
            pltpu.VMEM((4, 4) + block, jnp.bfloat16),
            pltpu.VMEM((2, 4) + block, jnp.bfloat16),
            pltpu.VMEM((4,) + block, jnp.bfloat16),
            pltpu.VMEM((4,) + block, jnp.bfloat16),
            pltpu.SemaphoreType.DMA((20,)),
            pltpu.SemaphoreType.DMA((20,)),
        ]

    def copy(self, source, target, lane, device):
        return pltpu.make_async_remote_copy(
            src_ref=source,
            dst_ref=target,
            send_sem=self.send_sem.at[lane],
            recv_sem=self.recv_sem.at[lane],
            device_id=device,
            device_id_type=MESH_ID,
        )

    def send(self, *args):
        copy = self.copy(*args)
        copy.start()
        self.sent.append(copy)

    def landed(self, target, lane):
        self.copy(target, target, lane, self.place.near(1)).wait_recv()

    def mine(self, k, chip):
        return self.grads.at[k, chip, self.place.core]

    def to_sibling(self, k):
        self.send(
            self.grads.at[k, :, 1 - self.place.core], self.sibling.at[k], k, self.place.near(1)
        )

    def from_sibling(self, k):
        place = self.place
        self.landed(self.sibling.at[k], k)

        def add(chip, carry):
            block = self.mine(k, chip)
            block[...] = (
                block[...].astype(jnp.float32) + self.sibling[k, chip].astype(jnp.float32)
            ).astype(jnp.bfloat16)
            return carry

        lax.fori_loop(0, 4, add, 0)
        near = 1 + self.turns[k]
        for which, bits in ((1, 3), (0, near)):
            self.send(
                self.mine(k, place.flip_chip(bits)),
                self.first.at[which, k],
                4 + 2 * k + which,
                place.near(2 * near),
            )

    def from_first(self, k):
        place = self.place
        far = 2 - self.turns[k]
        self.landed(self.first.at[1, k], 4 + 2 * k + 1)
        chip = place.flip_chip(far)
        block = self.mine(k, chip)
        block[...] = (
            block[...].astype(jnp.float32) + self.first[1, k].astype(jnp.float32)
        ).astype(jnp.bfloat16)
        self.send(block, self.second.at[k], 12 + k, place.near(2 * far))

    def from_second(self, k, total=None):
        place = self.place
        self.landed(self.first.at[0, k], 4 + 2 * k)
        self.landed(self.second.at[k], 12 + k)
        block = self.mine(k, place.chip)
        value = (
            block[...].astype(jnp.float32)
            + self.first[0, k].astype(jnp.float32)
            + self.second[k].astype(jnp.float32)
        )
        if k == 0:
            total[...] = value
        else:
            block[...] = value.astype(jnp.bfloat16)
            self.send(block, self.last.at[k], 16 + k, place.along(k))

    def from_tensor(self, total):
        value = total[...]
        for k in (1, 2, 3):
            self.landed(self.last.at[k], 16 + k)
            value = value + self.last[k].astype(jnp.float32)
        total[...] = value

    def finish(self):
        for copy in self.sent:
            copy.wait_send()


BLOCK = 128
HALF_WINDOW = 256
KV, Q, OUT, GATE, UP, DOWN = GROUPS = tuple(range(6))
TURNS = {GATE: (1, 0, 1, 0), UP: (0, 0, 1, 1)}
VMEM_BYTES = 63 * 2**20


def nn(left_side, right_side):
    return jnp.dot(left_side, right_side, preferred_element_type=jnp.float32)


def each_block(count, step, body):
    def run(i, carry):
        body(pl.multiple_of(i * step, step))
        return carry

    lax.fori_loop(0, count // step, run, 0)


def inverse_rms(values):
    return lax.rsqrt(jnp.mean(values * values, axis=-1, keepdims=True) + EPSILON)


def transposed(values):
    return values.astype(jnp.float32).T.astype(jnp.bfloat16)


def spread(block_columns, total, index):
    source = lax.broadcasted_iota(jnp.int32, (GAIN_COLUMNS, total), 0)
    target = lax.broadcasted_iota(jnp.int32, (GAIN_COLUMNS, total), 1)
    hit = (target - index * block_columns == source) & (source < block_columns)
    return jnp.where(hit, 1.0, 0.0).astype(jnp.bfloat16)


def layer_scratch(rows, width, head, ff_part, shard, parts):
    bf, f32 = jnp.bfloat16, jnp.float32
    keys = 2 * rows
    window = WINDOW + HALF_WINDOW
    blocks = rows // HALF_WINDOW
    return dict(
        normed=((rows, width), bf),
        normed_t=((width, rows), bf),
        w_keyval=((width, 2 * head), bf),
        gains=((PAD_ROWS, width), f32),
        qk_table=((PAD_ROWS, head), f32),
        gain_sums=((PAD_ROWS, width), f32),
        qk_sums=((PAD_ROWS, head), f32),
        key_raw=((rows, head), f32),
        keyval=((keys, 2 * head), bf),
        keyval_t=((2 * head, keys), bf),
        query_raw=((parts, rows, head), f32),
        queries=((parts, rows, head), bf),
        probs=((parts, blocks, window, HALF_WINDOW), bf),
        score_grad=((window, HALF_WINDOW), bf),
        context=((parts, rows, head), bf),
        attn=((rows, width), f32),
        residual=((rows, width), f32),
        ffn_in=((rows, width), bf),
        ffn_in_t=((width, rows), bf),
        gate_pre=((parts, rows, ff_part), f32),
        up_pre=((rows, ff_part), f32),
        gelu_out=((parts, rows, ff_part), bf),
        gelu_slope=((parts, rows, ff_part), bf),
        hidden=((parts, rows, ff_part), bf),
        ffn=((rows, width), f32),
        ffn_grad=((rows, width), bf),
        ffn_grad_t=((width, rows), bf),
        gate_grad=((rows, ff_part), bf),
        up_grad=((rows, ff_part), bf),
        attn_grad=((rows, width), bf),
        attn_grad_t=((width, rows), bf),
        halo_in=((rows, 2 * head), bf),
        kv_total=((shard + PAD_ROWS, GAIN_COLUMNS), f32),
        kv_shard=((shard + PAD_ROWS, GAIN_COLUMNS), bf),
        cosine=((rows, head // 2), f32),
        sine=((rows, head // 2), f32),
    )


def layer_kernel(names, *refs):
    tokens, cotangent, docs, positions, norm_gains, qk_gains, kv_weight = refs[:7]
    shards = (None,) + refs[7:12]
    block_out, tokens_grad = refs[12:14]
    totals = dict(zip(GROUPS[1:], refs[14:19]))
    shared = refs[19]
    rest = list(refs[20:])
    s = types.SimpleNamespace(**{name: rest.pop(0) for name in names})
    slots = {name: rest.pop(0) for name in GROUPS}
    rows, width = tokens.shape
    head = shards[Q].shape[1]
    ff_part = shards[GATE].shape[1]
    shard = shards[Q].shape[0]
    qk_rows = head // 8
    parts = 4
    blocks = rows // HALF_WINDOW
    window = WINDOW + HALF_WINDOW
    place = Place()

    gathers = {}
    for name, source in zip(GROUPS, (s.kv_shard,) + shards[1:]):
        gathers[name] = Gather(place, source, slots[name], *[rest.pop(0) for _ in range(3)])
    scatters = {}
    for name in GROUPS:
        own = [rest.pop(0) for _ in range(6)]
        turns = TURNS.get(name, (0, 1, 0, 1))
        scatters[name] = Scatter(place, slots[name], *own[:4], own[4:], turns)
    share_send, share_recv, halo_sems = rest

    def weight(name, k):
        return slots[name][k].reshape(width, -1)

    def put_grad(name, k, value):
        slots[name][k] = value.astype(jnp.bfloat16).reshape(4, 2, shard, -1)

    keyval_grad = s.gate_pre.at[0:2]
    bias, scores = s.gate_pre.at[0:2], s.gate_pre.at[3]

    def tile(j):
        top, left = j % 2 * HALF_WINDOW, j // 2 * HALF_WINDOW
        return slice(top, top + HALF_WINDOW), slice(left, left + HALF_WINDOW)

    query_grads = s.gelu_slope.at[:, :, 0:head]
    context_grad = s.gelu_out.at[:, :, 0:head]
    halo_out, keyval_low = s.hidden.at[0], s.hidden.at[1]

    def keyval_rows(block):
        return block // blocks, slice(
            block % blocks * HALF_WINDOW, (block % blocks + 1) * HALF_WINDOW
        )

    cosine, sine = s.cosine, s.sine
    part_at = pl.multiple_of(place.tensor * GAIN_COLUMNS, GAIN_COLUMNS)
    s.kv_shard[0:shard, :] = kv_weight[:, pl.ds(part_at, GAIN_COLUMNS)]
    s.kv_shard[shard:, :] = jnp.zeros((PAD_ROWS, GAIN_COLUMNS), jnp.bfloat16)
    s.kv_shard[shard : shard + 4, 0:shard] = norm_gains[...]
    s.kv_shard[shard + 4 : shard + 6, 0:qk_rows] = qk_gains[...]
    place.greet()
    gathers[KV].begin()
    gathers[Q].begin()
    queue = gather_order([gathers[name] for name in (KV, Q, GATE, OUT, UP, DOWN)])
    queue[0].pop(0)
    queue[1].pop(0)
    position = [0]

    def through(stage):
        while position[0] <= stage:
            while queue[position[0]]:
                queue[position[0]].pop(0)()
            position[0] += 1

    def pump(count):
        while count and position[0] < len(queue):
            if not queue[position[0]]:
                position[0] += 1
                continue
            queue[position[0]].pop(0)()
            count -= 1

    def as_column(values):
        return jnp.broadcast_to(values.astype(jnp.float32), (GAIN_COLUMNS, values.shape[1])).T

    start = pl.multiple_of(place.tensor * rows, rows)
    before = pl.multiple_of(jnp.maximum(start - rows, 0), rows)
    halo_doc = jnp.where(place.tensor > 0, docs[:, pl.ds(before, rows)], -1)
    own_doc = docs[:, pl.ds(start, rows)]
    doc_pieces = []
    for source in (halo_doc, own_doc):
        for r in range(blocks):
            piece = source[:, r * HALF_WINDOW : (r + 1) * HALF_WINDOW]
            doc_pieces.append(as_column(piece)[:, 0:1])
    for r in range(blocks):
        doc_q = own_doc[:, r * HALF_WINDOW : (r + 1) * HALF_WINDOW].astype(jnp.float32)
        for j in range(window // HALF_WINDOW):
            key_at = lax.broadcasted_iota(jnp.int32, (HALF_WINDOW, HALF_WINDOW), 0)
            query_at = lax.broadcasted_iota(jnp.int32, (HALF_WINDOW, HALF_WINDOW), 1)
            offset = query_at + rows - key_at - j * HALF_WINDOW
            allowed = (offset >= 0) & (offset < WINDOW) & (doc_q == doc_pieces[r + j])
            bias[(r,) + tile(j)] = jnp.where(allowed, 0.0, -1000000000.0)

    exponent = lax.broadcasted_iota(jnp.int32, (1, head // 2), 1).astype(jnp.float32)
    frequency = jnp.exp(exponent * (-2.0 / head * math.log(ROPE_BASE)))
    for i in range(rows // BLOCK):
        own = pl.ds(pl.multiple_of(start + i * BLOCK, BLOCK), BLOCK)
        angle = as_column(positions[:, own]) * frequency
        cosine[i * BLOCK : (i + 1) * BLOCK, :] = jnp.cos(angle)
        sine[i * BLOCK : (i + 1) * BLOCK, :] = jnp.sin(angle)

    s.gain_sums[...] = jnp.zeros_like(s.gain_sums)
    s.qk_sums[...] = jnp.zeros_like(s.qk_sums)

    @pl.when(place.tensor == 0)
    def _():
        s.keyval[0:rows, :] = jnp.zeros((rows, 2 * head), jnp.bfloat16)

    through(2)
    gathers[KV].ready()

    gain_rows = jnp.zeros((PAD_ROWS, width), jnp.float32)
    qk_part = jnp.zeros((PAD_ROWS, head), jnp.float32)
    for d in range(8):
        block = slots[KV][0, d // 2, d % 2, shard:, :]
        gain_rows += nn(block, spread(shard, width, d))
        qk_part += nn(block, spread(qk_rows, head, d))
    s.gains[...] = gain_rows
    s.qk_table[...] = qk_part
    for quarter in range(parts):
        columns = slice(quarter * GAIN_COLUMNS, (quarter + 1) * GAIN_COLUMNS)
        s.w_keyval[:, columns] = slots[KV][
            place.flip_part(quarter), :, :, 0:shard, :
        ].reshape(width, GAIN_COLUMNS)
    query_gain = s.qk_table[4:5, :]
    key_gain = s.qk_table[5:6, :]

    def norm_tokens(start):
        at = pl.ds(start, BLOCK)
        values = tokens[at, :].astype(jnp.float32)
        low = (values * inverse_rms(values) * s.gains[0:1, :]).astype(jnp.bfloat16)
        s.normed[at, :] = low
        s.normed_t[:, at] = transposed(low)

    each_block(rows, BLOCK, norm_tokens)
    pump(4)

    def make_keys(start):
        at = pl.ds(start, BLOCK)
        raw = nn(s.normed[at, :], s.w_keyval[...])
        key = raw[:, :head]
        s.key_raw[at, :] = key
        key = rotate(key * inverse_rms(key) * key_gain, cosine[at, :], sine[at, :])
        both = jnp.concatenate([key, raw[:, head:]], axis=1).astype(jnp.bfloat16)
        own = pl.ds(pl.multiple_of(rows + start, BLOCK), BLOCK)
        s.keyval[own, :] = both
        s.keyval_t[:, own] = transposed(both)

    each_block(rows, BLOCK, make_keys)

    next_part = jnp.minimum(place.tensor + 1, parts - 1)
    halo = pltpu.make_async_remote_copy(
        src_ref=s.keyval.at[pl.ds(rows, rows)],
        dst_ref=s.keyval.at[pl.ds(0, rows)],
        send_sem=halo_sems.at[0],
        recv_sem=halo_sems.at[1],
        device_id=(place.dp, next_part),
        device_id_type=MESH_ID,
    )

    @pl.when(place.tensor < parts - 1)
    def _():
        halo.start()

    through(3)
    gathers[Q].ready()
    for k in range(parts):
        s.query_raw[k] = nn(s.normed[...], weight(Q, k))

        def make_queries(start, k=k):
            at = pl.ds(start, BLOCK)
            raw = s.query_raw[k, at, :]
            low = rotate(raw * inverse_rms(raw) * query_gain, cosine[at, :], sine[at, :])
            s.queries[k, at, :] = (low * head ** (-0.5)).astype(jnp.bfloat16)

        each_block(rows, BLOCK, make_queries)
        pump(2)

    @pl.when(place.tensor > 0)
    def _():
        halo.wait_recv()

    def turn_halo(start):
        at = pl.ds(start, BLOCK)
        s.keyval_t[:, at] = transposed(s.keyval[at, :])

    each_block(rows, BLOCK, turn_halo)

    for k in range(parts):
        for r in range(blocks):
            at = slice(r * HALF_WINDOW, (r + 1) * HALF_WINDOW)
            query = s.queries[k, at, :]
            total = jnp.zeros((1, HALF_WINDOW), jnp.float32)
            for j in range(window // HALF_WINDOW):
                inner = slice(j * HALF_WINDOW, (j + 1) * HALF_WINDOW)
                outer = slice((r + j) * HALF_WINDOW, (r + j + 1) * HALF_WINDOW)
                score = dot_last(s.keyval[outer, :head], query) + bias[(r,) + tile(j)]
                score = jnp.exp(score)
                scores[tile(j)] = score
                total += jnp.sum(score, axis=0, keepdims=True)
            scale = 1.0 / total
            for j in range(window // HALF_WINDOW):
                inner = slice(j * HALF_WINDOW, (j + 1) * HALF_WINDOW)
                s.probs[k, r, inner, :] = (scores[tile(j)] * scale).astype(jnp.bfloat16)
            mixed = nn(
                s.keyval_t[head:, r * HALF_WINDOW : r * HALF_WINDOW + window], s.probs[k, r]
            )
            s.context[k, at, :] = mixed.T.astype(jnp.bfloat16)
            pump(3)

    through(5)
    gathers[OUT].ready()
    for k in range(parts):
        share = dot_last(s.context[k], weight(OUT, k))
        if k == 0:
            s.attn[...] = share
        else:
            s.attn[...] += share
    pump(3)

    def norm_attn(start):
        at = pl.ds(start, BLOCK)
        attn = s.attn[at, :]
        residual = tokens[at, :].astype(jnp.float32) + attn * inverse_rms(attn) * s.gains[1:2, :]
        s.residual[at, :] = residual
        low = (residual * inverse_rms(residual) * s.gains[2:3, :]).astype(jnp.bfloat16)
        s.ffn_in[at, :] = low
        s.ffn_in_t[:, at] = transposed(low)

    each_block(rows, BLOCK, norm_attn)
    gathers[GATE].ready()
    for k in range(parts):
        s.gate_pre[k] = nn(s.ffn_in[...], weight(GATE, k))
        pump(2)
    through(6)
    gathers[UP].ready()
    for k in range(parts):
        s.up_pre[...] = nn(s.ffn_in[...], weight(UP, k))

        def activate(start, k=k):
            at = pl.ds(start, 32)
            gate = s.gate_pre[k, at, :]
            up = s.up_pre[at, :]
            square = gate * gate
            tanh = jnp.tanh(GELU_SCALE * gate * (1.0 + 0.044715 * square))
            upper = 0.5 * (1.0 + tanh)
            gelu = gate * upper
            slope = upper + (
                0.5 * GELU_SCALE * gate * (1.0 - tanh * tanh) * (1.0 + 3 * 0.044715 * square)
            )
            s.gelu_out[k, at, :] = gelu.astype(jnp.bfloat16)
            s.gelu_slope[k, at, :] = (slope * up).astype(jnp.bfloat16)
            s.hidden[k, at, :] = (gelu * up).astype(jnp.bfloat16)

        each_block(rows, 32, activate)
        pump(2)
    through(7)
    gathers[DOWN].ready()
    for k in range(parts):
        share = dot_last(s.hidden[k], weight(DOWN, k))
        if k == 0:
            s.ffn[...] = share
        else:
            s.ffn[...] += share
    for name in GROUPS:
        gathers[name].finish()

    def top_block(start):
        at = pl.ds(start, BLOCK)
        ffn = s.ffn[at, :]
        gain = s.gains[3:4, :]
        top = cotangent[at, :].astype(jnp.float32)
        inverse = inverse_rms(ffn)
        block_out[at, :] = (s.residual[at, :] + ffn * inverse * gain).astype(jnp.bfloat16)
        grad, gain_rows = norm_back(ffn, gain, top)
        s.gain_sums[3:4, :] += jnp.sum(gain_rows, axis=0, keepdims=True)
        low = grad.astype(jnp.bfloat16)
        s.ffn_grad[at, :] = low
        s.ffn_grad_t[:, at] = transposed(low)

    each_block(rows, BLOCK, top_block)

    ffn_groups = (DOWN, GATE, UP)
    order = (3, 2, 1, 0)

    def for_ffn(step, k):
        for name in ffn_groups:
            scatter = scatters[name]
            if step is Scatter.from_second:
                step(scatter, k, totals[name])
            else:
                step(scatter, k)

    for i, k in enumerate(order):
        s.up_pre[...] = nn(s.ffn_grad[...], weight(DOWN, k))

        def activate_back(start, k=k):
            at = pl.ds(start, 32)
            grad = s.up_pre[at, :]
            s.gate_grad[at, :] = (
                grad * s.gelu_slope[k, at, :].astype(jnp.float32)
            ).astype(jnp.bfloat16)
            s.up_grad[at, :] = (
                grad * s.gelu_out[k, at, :].astype(jnp.float32)
            ).astype(jnp.bfloat16)

        each_block(rows, 32, activate_back)
        share = dot_last(s.gate_grad[...], weight(GATE, k))
        share += dot_last(s.up_grad[...], weight(UP, k))
        if i == 0:
            s.ffn[...] = share
        else:
            s.ffn[...] += share
        put_grad(DOWN, k, nn(s.ffn_grad_t[...], s.hidden[k]))
        scatters[DOWN].to_sibling(k)
        put_grad(GATE, k, nn(s.ffn_in_t[...], s.gate_grad[...]))
        scatters[GATE].to_sibling(k)
        if i >= 1:
            scatters[UP].from_sibling(order[i - 1])
        put_grad(UP, k, nn(s.ffn_in_t[...], s.up_grad[...]))
        scatters[UP].to_sibling(k)
        scatters[DOWN].from_sibling(k)
        scatters[GATE].from_sibling(k)

    def middle_block(start):
        at = pl.ds(start, BLOCK)
        residual = s.residual[at, :]
        attn = s.attn[at, :]
        part, gain_rows = norm_back(residual, s.gains[2:3, :], s.ffn[at, :])
        s.gain_sums[2:3, :] += jnp.sum(gain_rows, axis=0, keepdims=True)
        residual_grad = cotangent[at, :].astype(jnp.float32) + part
        s.residual[at, :] = residual_grad
        grad, gain_rows = norm_back(attn, s.gains[1:2, :], residual_grad)
        s.gain_sums[1:2, :] += jnp.sum(gain_rows, axis=0, keepdims=True)
        low = grad.astype(jnp.bfloat16)
        s.attn_grad[at, :] = low
        s.attn_grad_t[:, at] = transposed(low)

    each_block(rows, BLOCK, middle_block)
    keyval_grad[...] = jnp.zeros(keyval_grad.shape, jnp.float32)
    scatters[UP].from_sibling(0)

    for k in range(parts):
        context_grad[k] = nn(s.attn_grad[...], weight(OUT, k)).astype(jnp.bfloat16)
        put_grad(OUT, k, nn(s.attn_grad_t[...], s.context[k]))
        scatters[OUT].to_sibling(k)

    def for_all(step, name):
        for k in order:
            if step is Scatter.from_second:
                step(scatters[name], k, totals[name])
            else:
                step(scatters[name], k)

    later = {
        1: lambda: for_all(Scatter.from_sibling, OUT),
        3: lambda: for_ffn(Scatter.from_first, 3),
        5: lambda: for_ffn(Scatter.from_first, 2),
        7: lambda: for_ffn(Scatter.from_first, 1),
    }
    last_part = jnp.maximum(place.tensor - 1, 0)
    half = rows // blocks
    halo_back = []
    for r in range(blocks):
        halo_back.append(
            pltpu.make_async_remote_copy(
                src_ref=halo_out.at[pl.ds(r * half, half)],
                dst_ref=s.halo_in.at[pl.ds(r * half, half)],
                send_sem=halo_sems.at[2 + r],
                recv_sem=halo_sems.at[4 + r],
                device_id=(place.dp, last_part),
                device_id_type=MESH_ID,
            )
        )

    @pl.when(place.tensor == parts - 1)
    def _():
        s.halo_in[...] = jnp.zeros_like(s.halo_in)

    for r in range(blocks):
        for k in range(parts):
            at = slice(r * HALF_WINDOW, (r + 1) * HALF_WINDOW)
            query = s.queries[k, at, :]
            grad = context_grad[k, at, :]
            delta = jnp.zeros((1, HALF_WINDOW), jnp.float32)
            for j in range(window // HALF_WINDOW):
                inner = slice(j * HALF_WINDOW, (j + 1) * HALF_WINDOW)
                outer = slice((r + j) * HALF_WINDOW, (r + j + 1) * HALF_WINDOW)
                prob_grad = dot_last(s.keyval[outer, head:], grad)
                scores[tile(j)] = prob_grad
                probs = s.probs[k, r, inner, :].astype(jnp.float32)
                delta += jnp.sum(probs * prob_grad, axis=0, keepdims=True)
            for j in range(window // HALF_WINDOW):
                inner = slice(j * HALF_WINDOW, (j + 1) * HALF_WINDOW)
                outer = slice((r + j) * HALF_WINDOW, (r + j + 1) * HALF_WINDOW)
                probs = s.probs[k, r, inner, :]
                score_grad = probs.astype(jnp.float32) * (scores[tile(j)] - delta)
                score_grad = score_grad.astype(jnp.bfloat16)
                s.score_grad[inner, :] = score_grad
                which, outer = keyval_rows(r + j)
                keyval_grad[which, outer, :head] += nn(score_grad, query)
                keyval_grad[which, outer, head:] += nn(probs, grad)
            turned = nn(
                s.keyval_t[:head, r * HALF_WINDOW : r * HALF_WINDOW + window],
                s.score_grad[...],
            )
            query_grad = turned.T * head ** (-0.5)
            query_grad = rotate(query_grad, cosine[at, :], -sine[at, :])
            raw_grad, gain_rows = norm_back(s.query_raw[k, at, :], query_gain, query_grad)
            s.qk_sums[4:5, :] += jnp.sum(gain_rows, axis=0, keepdims=True)
            query_grads[k, at, :] = raw_grad.astype(jnp.bfloat16)
            later.get(r * parts + k, lambda: None)()
        at = slice(r * half, (r + 1) * half)
        halo_out[at, :] = keyval_grad[0, at, :].astype(jnp.bfloat16)

        @pl.when(place.tensor > 0)
        def _(r=r):
            halo_back[r].start()

    for k in range(parts):
        share = dot_last(query_grads[k], weight(Q, k))
        if k == 0:
            s.ffn[...] = share
        else:
            s.ffn[...] += share
        put_grad(Q, k, nn(s.normed_t[...], query_grads[k]))
        scatters[Q].to_sibling(k)
    for_all(Scatter.from_sibling, Q)
    for_ffn(Scatter.from_first, 0)
    for_all(Scatter.from_first, OUT)
    for_ffn(Scatter.from_second, 3)

    @pl.when(place.tensor < parts - 1)
    def _():
        for copy in halo_back:
            copy.wait_recv()

    def key_block(start):
        at = pl.ds(start, BLOCK)
        grads = keyval_grad[1, at, :] + s.halo_in[at, :].astype(jnp.float32)
        key_grad = rotate(grads[:, :head], cosine[at, :], -sine[at, :])
        raw_grad, gain_rows = norm_back(s.key_raw[at, :], key_gain, key_grad)
        s.qk_sums[5:6, :] += jnp.sum(gain_rows, axis=0, keepdims=True)
        keyval_low[at, :] = jnp.concatenate([raw_grad, grads[:, head:]], axis=1).astype(
            jnp.bfloat16
        )

    each_block(rows, BLOCK, key_block)
    s.ffn[...] += dot_last(keyval_low[...], s.w_keyval[...])

    def bottom_block(start):
        at = pl.ds(start, BLOCK)
        values = tokens[at, :].astype(jnp.float32)
        part, gain_rows = norm_back(values, s.gains[0:1, :], s.ffn[at, :])
        s.gain_sums[0:1, :] += jnp.sum(gain_rows, axis=0, keepdims=True)
        tokens_grad[at, :] = s.residual[at, :] + part

    each_block(rows, BLOCK, bottom_block)
    for quarter in range(parts):
        columns = slice(quarter * GAIN_COLUMNS, (quarter + 1) * GAIN_COLUMNS)
        value = nn(s.normed_t[...], keyval_low[:, columns])
        slots[KV][place.flip_part(quarter), :, :, 0:shard, :] = value.astype(
            jnp.bfloat16
        ).reshape(4, 2, shard, GAIN_COLUMNS)
    gain_low = s.gain_sums[...].astype(jnp.bfloat16)
    qk_low = s.qk_sums[...].astype(jnp.bfloat16)
    for d in range(8):
        block = dot_last(gain_low, spread(shard, width, d))
        block += dot_last(qk_low, spread(qk_rows, head, d))
        for k in range(parts):
            slots[KV][k, d // 2, d % 2, shard:, :] = block.astype(jnp.bfloat16)
    for k in range(parts):
        scatters[KV].to_sibling(k)
    for_all(Scatter.from_sibling, KV)
    for_ffn(Scatter.from_second, 2)
    for_all(Scatter.from_first, Q)
    for_ffn(Scatter.from_second, 1)
    for_all(Scatter.from_second, OUT)
    for_ffn(Scatter.from_second, 0)
    for_all(Scatter.from_first, KV)
    for_all(Scatter.from_second, Q)
    for name in ffn_groups:
        scatters[name].from_tensor(totals[name])
    for k in order:
        scatters[KV].from_second(k, s.kv_total)
    scatters[KV].from_tensor(s.kv_total)
    shared[0] = s.kv_total[...]
    copies = []
    for k in (1, 2, 3):
        copies.append(
            pltpu.make_async_remote_copy(
                src_ref=s.kv_total,
                dst_ref=shared.at[k],
                send_sem=share_send.at[k],
                recv_sem=share_recv.at[k],
                device_id=place.along(k),
                device_id_type=MESH_ID,
            )
        )
    for copy in copies:
        copy.start()
    for name in (OUT, Q):
        scatters[name].from_tensor(totals[name])
    for copy in copies:
        copy.wait()
    for name in GROUPS:
        scatters[name].finish()

    @pl.when(place.tensor < parts - 1)
    def _():
        halo.wait_send()

    @pl.when(place.tensor > 0)
    def _():
        for copy in halo_back:
            copy.wait_send()


def finish_kernel(count, *refs):
    sources, shared = refs[:count], refs[count]
    targets, keyval, norm_gains, qk_gains = (refs[count + 1 : 2 * count + 1],) + refs[
        2 * count + 1 : 2 * count + 4
    ]
    sems = refs[2 * count + 4]
    copies = [
        pltpu.make_async_copy(source, target, sems.at[i])
        for i, (source, target) in enumerate(zip(sources, targets))
    ]
    for copy in copies:
        copy.start()
    place = Place()
    shard, qk_rows = norm_gains.shape[1], qk_gains.shape[1]
    for part in range(4):
        columns = slice(part * GAIN_COLUMNS, (part + 1) * GAIN_COLUMNS)
        keyval[:, columns] = shared[place.flip_part(part), 0:shard, :]
    norm_gains[...] = shared[0, shard : shard + 4, 0:shard]
    qk_gains[...] = shared[0, shard + 4 : shard + 6, 0:qk_rows]
    for copy in copies:
        copy.wait()


def per_device_direct(
    tokens,
    segments,
    positions,
    norm_gains,
    qk_gains,
    q_weight,
    kv_weight,
    out_weight,
    gate_weight,
    up_weight,
    down_weight,
    cotangent,
):
    parts = lax.axis_size("tensor")
    rows, width = tokens.shape
    shard = q_weight.shape[0]
    head = q_weight.shape[1]
    ff_part = gate_weight.shape[1]
    arguments = [
        tokens,
        cotangent,
        segments[None, :],
        positions[None, :],
        norm_gains,
        qk_gains,
        kv_weight,
        q_weight,
        out_weight.T,
        gate_weight,
        up_weight,
        down_weight.T,
    ]
    kv_shape = (shard + PAD_ROWS, GAIN_COLUMNS)
    shapes = [kv_shape] + [w.shape for w in arguments[7:]]
    buffers = layer_scratch(rows, width, head, ff_part, shard, parts)
    scratch = [pltpu.VMEM(*buffer) for buffer in buffers.values()]
    scratch += [pltpu.VMEM((4, 4, 2) + shape, jnp.bfloat16) for shape in shapes]
    scratch += Gather.scratch() * len(shapes)
    for shape in shapes:
        scratch += Scatter.scratch(*shape)
    scratch += [pltpu.SemaphoreType.DMA((4,))] * 2 + [pltpu.SemaphoreType.DMA((6,))]
    f32 = jnp.float32
    whole = pl.BlockSpec(memory_space=pltpu.VMEM)
    anywhere = pl.BlockSpec(memory_space=pl.ANY)
    kinds = [
        jax.ShapeDtypeStruct((rows, width), jnp.bfloat16),
        jax.ShapeDtypeStruct((rows, width), f32),
    ] + [jax.ShapeDtypeStruct(shape, f32) for shape in shapes[1:]]
    results = pl.pallas_call(
        functools.partial(layer_kernel, list(buffers)),
        out_shape=kinds + [jax.ShapeDtypeStruct((parts,) + kv_shape, f32)],
        in_specs=[whole] * len(arguments),
        out_specs=[whole] * 8,
        scratch_shapes=scratch,
        compiler_params=pltpu.CompilerParams(
            collective_id=0, has_side_effects=True, vmem_limit_bytes=VMEM_BYTES
        ),
        name="layer",
    )(*arguments)
    results = pl.pallas_call(
        functools.partial(finish_kernel, len(kinds)),
        out_shape=kinds
        + [
            jax.ShapeDtypeStruct(kv_weight.shape, f32),
            jax.ShapeDtypeStruct(norm_gains.shape, f32),
            jax.ShapeDtypeStruct(qk_gains.shape, f32),
        ],
        in_specs=[whole] * (len(kinds) + 1),
        out_specs=[anywhere] * len(kinds) + [whole] * 3,
        scratch_shapes=[pltpu.SemaphoreType.DMA((len(kinds),))],
        name="finish",
    )(*results)
    block_out, tokens_grad, q_sum, out_sum, gate_sum, up_sum, down_sum = results[:7]
    keyval, norm_sum, qk_sum = results[7:]
    return (
        block_out,
        tokens_grad,
        norm_sum,
        qk_sum,
        q_sum,
        keyval,
        out_sum.T,
        gate_sum,
        up_sum,
        down_sum.T,
    )


def pack_shards(norm_gains, qk_gains, q_weight, kv_weight, out_weight, gate_weight, up_weight, down_weight):
    rows = q_weight.shape[0]
    kv_columns = kv_weight.shape[1] // lax.axis_size("tensor")
    kv_part = lax.dynamic_slice_in_dim(
        kv_weight, lax.axis_index("tensor") * kv_columns, kv_columns, axis=1
    )
    gain_part = jnp.concatenate(
        [
            norm_gains.T,
            jnp.pad(qk_gains.T, ((0, rows - qk_gains.shape[1]), (0, 0))),
            jnp.zeros((rows, GAIN_COLUMNS - 6), jnp.bfloat16),
        ],
        axis=1,
    )
    return jnp.concatenate(
        [q_weight, out_weight.T, gate_weight, up_weight, down_weight.T, kv_part, gain_part],
        axis=1,
    )


def gather_weights(packed):
    return lax.all_gather(packed, ("tensor", "dp"), axis=0, tiled=True)


def reduce_grads(grads):
    return lax.psum_scatter(
        grads, ("tensor", "dp"), scatter_dimension=0, tiled=True
    ).astype(jnp.float32)


def per_device(
    tokens,
    segments,
    positions,
    norm_gains,
    qk_gains,
    q_weight,
    kv_weight,
    out_weight,
    gate_weight,
    up_weight,
    down_weight,
    cotangent,
):
    parts = lax.axis_size("tensor")
    place = lax.axis_index("tensor")
    rows, width = tokens.shape
    shard_rows = q_weight.shape[0]
    head_width = q_weight.shape[1]
    ff_part = gate_weight.shape[1]
    kv_columns = kv_weight.shape[1]
    kv_part = kv_columns // parts
    qk_rows = qk_gains.shape[1]
    ends = [0]
    for columns in (head_width, head_width, ff_part, ff_part, ff_part, kv_part, GAIN_COLUMNS):
        ends.append(ends[-1] + columns)

    packed = pack_shards(
        norm_gains, qk_gains, q_weight, kv_weight, out_weight, gate_weight, up_weight, down_weight
    )
    gathered = gather_weights(packed).reshape(parts, width, ends[-1])
    halo = lax.ppermute(tokens, "tensor", [(i, i + 1) for i in range(parts - 1)])

    def piece(index):
        return [gathered[t, :, ends[index] : ends[index + 1]] for t in range(parts)]

    w_query, w_out, w_gate, w_up, w_down, w_kv = (piece(i) for i in range(6))
    w_keyval = jnp.concatenate(w_kv, axis=1)
    w_gains = gathered[0, :, ends[6] : ends[7]].astype(jnp.float32)
    gain_table = w_gains[:, :4].T
    qk_table = w_gains.reshape(-1, shard_rows, GAIN_COLUMNS)[:, :qk_rows, 4:6]
    qk_table = qk_table.reshape(head_width, 2).T

    own_input = tokens.astype(jnp.float32)
    both_input = jnp.concatenate([halo, tokens], axis=0).astype(jnp.float32)
    normed_both = norm_rows(both_input, gain_table[0]).astype(jnp.bfloat16)
    normed = normed_both[rows:]
    start = place * rows
    first = jnp.maximum(start - rows, 0)
    own_doc = lax.dynamic_slice_in_dim(segments, start, rows)
    halo_doc = jnp.where(place > 0, lax.dynamic_slice_in_dim(segments, first, rows), -1)
    both_doc = jnp.concatenate([halo_doc, own_doc])
    both_place = jnp.concatenate(
        [
            lax.dynamic_slice_in_dim(positions, first, rows),
            lax.dynamic_slice_in_dim(positions, start, rows),
        ]
    )
    half_width = head_width // 2
    frequency = ROPE_BASE ** (-jnp.arange(half_width, dtype=jnp.float32) * 2.0 / head_width)
    angles = both_place.astype(jnp.float32)[:, None] * frequency[None, :]
    cosine_both = jnp.cos(angles)
    sine_both = jnp.sin(angles)
    cosine_own, sine_own = cosine_both[rows:], sine_both[rows:]

    offsets = jnp.arange(rows)[:, None] + rows - jnp.arange(2 * rows)[None, :]
    allowed = (offsets >= 0) & (offsets < WINDOW) & (own_doc[:, None] == both_doc[None, :])
    score_scale = head_width ** (-0.5)

    keyval_raw = dot_plain(normed_both, w_keyval)
    key_raw = keyval_raw[:, :head_width]
    keys = rotate(norm_rows(key_raw, qk_table[1]), cosine_both, sine_both).astype(jnp.bfloat16)
    value_rows = keyval_raw[:, head_width:].astype(jnp.bfloat16)

    query_raw, queries, lse, context = [], [], [], []
    attn_own = None
    for t in range(parts):
        raw = dot_plain(normed, w_query[t])
        low = rotate(norm_rows(raw, qk_table[0]), cosine_own, sine_own).astype(jnp.bfloat16)
        masked = jnp.where(allowed, dot_last(low, keys) * score_scale, -1000000000.0)
        row_max = jnp.max(masked, axis=1, keepdims=True)
        exponent = jnp.exp(masked - row_max)
        row_total = jnp.sum(exponent, axis=1, keepdims=True)
        probabilities = (exponent / row_total).astype(jnp.bfloat16)
        mixed = dot_plain(probabilities, value_rows).astype(jnp.bfloat16)
        query_raw.append(raw)
        queries.append(low)
        lse.append(row_max + jnp.log(row_total))
        context.append(mixed)
        share = dot_last(mixed, w_out[t])
        attn_own = share if attn_own is None else attn_own + share

    residual = own_input + norm_rows(attn_own, gain_table[1])
    ffn_in = norm_rows(residual, gain_table[2]).astype(jnp.bfloat16)
    gate_pre, up_pre, hidden = [], [], []
    ffn_out = None
    for t in range(parts):
        gate_pre.append(dot_plain(ffn_in, w_gate[t]))
        up_pre.append(dot_plain(ffn_in, w_up[t]))
        hidden.append(geglu(gate_pre[t], up_pre[t]).astype(jnp.bfloat16))
        share = dot_last(hidden[t], w_down[t])
        ffn_out = share if ffn_out is None else ffn_out + share
    block_out = (residual + norm_rows(ffn_out, gain_table[3])).astype(jnp.bfloat16)
    top_grad = cotangent.astype(jnp.float32)
    ffn_grad_value, post_gain_rows = norm_back(ffn_out, gain_table[3], top_grad)
    ffn_grad = ffn_grad_value.astype(jnp.bfloat16)
    ffn_in_grad = None
    grads = [[] for _ in range(parts)]
    down_wgrad, gate_wgrad, up_wgrad = [], [], []
    for t in range(parts):
        hidden_grad = dot_plain(ffn_grad, w_down[t])
        gelu_back = jax.vjp(geglu, gate_pre[t], up_pre[t])[1]
        gate_grad_value, up_grad_value = gelu_back(hidden_grad)
        gate_grad = gate_grad_value.astype(jnp.bfloat16)
        up_grad = up_grad_value.astype(jnp.bfloat16)
        share = dot_last(gate_grad, w_gate[t]) + dot_last(up_grad, w_up[t])
        ffn_in_grad = share if ffn_in_grad is None else ffn_in_grad + share
        gate_wgrad.append(dot_first(ffn_in, gate_grad))
        up_wgrad.append(dot_first(ffn_in, up_grad))
        down_wgrad.append(dot_first(ffn_grad, hidden[t]))
    residual_part, pre_ffn_rows = norm_back(residual, gain_table[2], ffn_in_grad)
    residual_grad = top_grad + residual_part
    attn_grad_value, post_attn_rows = norm_back(attn_own, gain_table[1], residual_grad)
    attn_grad = attn_grad_value.astype(jnp.bfloat16)

    key_grad, value_grad, normed_grad = None, None, None
    query_gain_grad = None
    out_wgrad, query_wgrad = [], []
    for t in range(parts):
        context_grad = dot_plain(attn_grad, w_out[t]).astype(jnp.bfloat16)
        out_wgrad.append(dot_first(attn_grad, context[t]))
        masked = jnp.where(allowed, dot_last(queries[t], keys) * score_scale, -1000000000.0)
        probabilities = jnp.exp(masked - lse[t])
        prob_grad = dot_last(context_grad, value_rows)
        row_delta = jnp.sum(probabilities * prob_grad, axis=1, keepdims=True)
        score_grad = (probabilities * (prob_grad - row_delta) * score_scale).astype(jnp.bfloat16)
        query_grad = dot_plain(score_grad, keys)
        key_share = dot_first(score_grad, queries[t])
        value_share = dot_first(probabilities.astype(jnp.bfloat16), context_grad)
        key_grad = key_share if key_grad is None else key_grad + key_share
        value_grad = value_share if value_grad is None else value_grad + value_share
        unrotated = rotate(query_grad, cosine_own, -sine_own)
        raw_grad, gain_rows = norm_back(query_raw[t], qk_table[0], unrotated)
        gain_share = jnp.sum(gain_rows, axis=0)
        query_gain_grad = gain_share if query_gain_grad is None else query_gain_grad + gain_share
        raw_low = raw_grad.astype(jnp.bfloat16)
        share = dot_last(raw_low, w_query[t])
        normed_grad = share if normed_grad is None else normed_grad + share
        query_wgrad.append(dot_first(normed, raw_low))
    key_raw_grad, key_gain_rows = norm_back(
        key_raw, qk_table[1], rotate(key_grad, cosine_both, -sine_both)
    )
    keyval_low = jnp.concatenate([key_raw_grad, value_grad], axis=1).astype(jnp.bfloat16)
    next_part = lax.ppermute(
        keyval_low[:rows], "tensor", [(i + 1, i) for i in range(parts - 1)]
    )
    keyval_wgrad = dot_first(normed_both, keyval_low)
    keyval_own = (keyval_low[rows:].astype(jnp.float32) + next_part.astype(jnp.float32)).astype(
        jnp.bfloat16
    )
    normed_grad = normed_grad + dot_last(keyval_own, w_keyval)
    input_part, pre_attn_rows = norm_back(own_input, gain_table[0], normed_grad)
    tokens_grad = residual_grad + input_part

    gain_grads = jnp.stack(
        [
            jnp.sum(pre_attn_rows, axis=0),
            jnp.sum(post_attn_rows, axis=0),
            jnp.sum(pre_ffn_rows, axis=0),
            jnp.sum(post_gain_rows, axis=0),
        ],
        axis=1,
    )
    qk_grads = jnp.stack([query_gain_grad, jnp.sum(key_gain_rows, axis=0)], axis=1)
    qk_grads = jnp.pad(
        qk_grads.reshape(-1, qk_rows, 2), ((0, 0), (0, shard_rows - qk_rows), (0, 0))
    ).reshape(width, 2)
    gain_columns = jnp.concatenate(
        [gain_grads, qk_grads, jnp.zeros((width, GAIN_COLUMNS - 6), jnp.float32)], axis=1
    )
    blocks = []
    for t in range(parts):
        blocks.append(
            jnp.concatenate(
                [
                    value.astype(jnp.bfloat16)
                    for value in (
                        query_wgrad[t],
                        out_wgrad[t],
                        gate_wgrad[t],
                        up_wgrad[t],
                        down_wgrad[t],
                        keyval_wgrad[:, t * kv_part : (t + 1) * kv_part],
                        gain_columns if t == 0 else jnp.zeros_like(gain_columns),
                    )
                ],
                axis=1,
            )
        )
    reduced = reduce_grads(jnp.concatenate(blocks, axis=0))
    shared = lax.all_gather(reduced[:, ends[5] :], "tensor", axis=0)
    keyval_out = jnp.concatenate([shared[t, :, :kv_part] for t in range(parts)], axis=1)
    gain_out = shared[0, :, kv_part:]
    cut = [reduced[:, ends[i] : ends[i + 1]] for i in range(5)]
    return (
        block_out,
        tokens_grad,
        gain_out[:, :4].T,
        gain_out[:qk_rows, 4:6].T,
        cut[0],
        keyval_out,
        cut[1].T,
        cut[2],
        cut[3],
        cut[4].T,
    )


def solution(mesh):
    direct = mesh.shape["dp"] == 8 and mesh.shape["tensor"] == 4
    return jax.shard_map(
        per_device_direct if direct else per_device,
        mesh=mesh,
        in_specs=(
            P(("dp", "tensor"), None),
            P("dp"),
            P("dp"),
            P(None, "dp"),
            P(None, "dp"),
            P("dp", "tensor"),
            P("dp", None),
            P("tensor", "dp"),
            P("dp", "tensor"),
            P("dp", "tensor"),
            P("tensor", "dp"),
            P(("dp", "tensor"), None),
        ),
        out_specs=(
            P(("dp", "tensor"), None),
            P(("dp", "tensor"), None),
            P(None, "dp"),
            P(None, "dp"),
            P("dp", "tensor"),
            P("dp", None),
            P("tensor", "dp"),
            P("dp", "tensor"),
            P("dp", "tensor"),
            P("tensor", "dp"),
        ),
        check_vma=False,
    )
```
